32 devices in a mesh: tilt: 2 (over y), dom: 16 (over z, x, core).
Axes of the slice: x: 2, y: 2, z: 4, core: 2. Of those that a mesh axis runs over, the one named last changes fastest.
Arguments:
- sections: bfloat16 [32, 256, 256], P('dom'), may hold values from -6 to 6
- images: bfloat16 [32, 4, 256, 256], P('dom', 'tilt'), may hold values from -6 to 6
- slice_rows: bfloat16 [4, 256, 256], P('tilt'), may hold values from -0.375 to 0.375
- slice_cols: bfloat16 [4, 256, 256], P('tilt'), may hold values from -0.375 to 0.375
- ctf_filter: bfloat16 [4, 256, 256], P('tilt'), may hold values from -0.375 to 0.375
- nbr_owner: int32 [32, 2, 8], P('dom'), may hold values from 0 to 15, all different within a row; in each aligned block of 4 rows (0 to 3, 4 to 7, ..., all dimensions but the last counted through in order) at most 4 rows name the same one
- nbr_local: int32 [32, 16], P('dom'), may hold values from 0 to 1
- nbr_side: int32 [32, 16], P('dom'), may hold values from 0 to 1
- nbr_weight: float32 [32, 16], P('dom'), may hold values from 0.25 to 2
Outputs:
- section_grad: float32 [32, 256, 256], P('dom', 'tilt')
- scores: float32 [32], P('dom')
The draws below stay inside these ranges and needn't reach their ends.
Inputs may be any that keep to these rules, and one draw needn't show every extreme that they name: `nbr_owner`: among the 32 neighbour entries of one spatial block's particles, at most 4 name the same owner block; some blocks reach 4.
All inputs are finite; a program needn't handle non-finite values.
Results may differ from the reference program's by a relative error of at most 0.013.
Values may be sent and summed in bfloat16 or wider, within the bound.
No kernel may reach another device: no remote copies, remote signals or barrier semaphores. Data moves between devices by JAX's collectives and lax.ppermute only.
A program may use at most 64 MiB of HBM per device.

```python
import math
import jax
import jax.numpy as jnp
import numpy as np
from jax import lax

PIX = 256
OVL = 16
NB = 16
PART_DEV = 2
CAP = 4
PARTICLES = 32
TILTS = 4
N_DOM = 16


def set_ends(values, rng, least, high):
    longest = values.shape.index(max(values.shape))
    spots = []
    for shift in (0, 1):
        where = [jax.random.randint(jax.random.fold_in(rng, axis), (), 0, length) for axis, length in enumerate(values.shape)]
        where[longest] = (where[longest] + shift) % values.shape[longest]
        spots.append(tuple(where))
    return values.at[spots[0]].set(least).at[spots[1]].set(high)


def shard_levels(stream_key, shape, cuts, smallest, largest):
    def one(axis_at, shards_of):
        heights = jax.random.uniform(jax.random.fold_in(jax.random.fold_in(stream_key, 6), axis_at), (shards_of,), jnp.float32, smallest / len(cuts), largest / len(cuts))
        return jnp.repeat(jnp.exp(heights), shape[axis_at] // shards_of).reshape((-1,) + (1,) * (len(shape) - axis_at - 1))

    gain = one(*cuts[0])
    for cut in cuts[1:]:
        gain = gain * one(*cut)
    return gain


def assign_block(own_key, own, number, rows, number_of, top, reach, lean):
    sequence = jax.random.permutation(own_key, number_of)
    packed, usual = shares(number_of, rows * top, reach, lean, True), shares(number_of, rows * top, reach, lean, False)
    places = jnp.arange(number_of)

    def named(lengths, rotation):
        used = int((lengths > 0).sum())
        fixed = max(1, used // 4)
        passed = fixed + (places - fixed + rotation * (used - fixed)) % max(1, number_of - fixed)
        return jnp.zeros((number_of,), jnp.int32).at[sequence[jnp.where(places < fixed, places, passed)]].set(jnp.asarray(lengths, jnp.int32))

    lengths = jnp.where(number % 4 == 0, named(packed, number // 4), named(usual, number - number // 4 - 1))
    mixed = jax.random.permutation(jax.random.fold_in(own, 3), number_of)
    giver, taker = mixed[0:number_of // 2 * 2:2], mixed[1:number_of // 2 * 2:2]
    slack = jnp.minimum(lengths[giver] - 1, reach - lengths[taker]) // 2
    slack = jnp.where((giver == sequence[0]) | (taker == sequence[0]) | (lengths[taker] == 0), 0, jnp.maximum(slack, 0))
    passed = jax.random.randint(jax.random.fold_in(own, 4), (number_of // 2,), 0, 1 << 20) % (slack + 1)
    lengths = lengths.at[giver].add(-passed).at[taker].add(passed)
    labels = jnp.searchsorted(jnp.cumsum(lengths), jnp.arange(rows * top), side="right").astype(jnp.int32)
    listing = labels.reshape(top, rows).T
    listing = listing[jax.random.permutation(jax.random.fold_in(own, 1), rows)]
    rotation = jax.random.randint(jax.random.fold_in(own, 2), (rows, 1), 0, top)
    return jnp.take_along_axis(listing, (jnp.arange(top)[None, :] + rotation) % top, axis=1)


def shares(number_of, total, limit, skew, full):
    loads = [(1 << 20) // math.isqrt(standing ** skew) + 1 for standing in range(1, number_of + 1)]
    largest = limit if full else min(limit, max(-(-total // number_of), total * loads[0] // sum(loads)))
    least = 1 if total - largest >= number_of - 1 else 0
    counts, surplus = [largest] + [least] * (number_of - 1), total - largest - least * (number_of - 1)
    while surplus > 0:
        free = [i for i in range(1, number_of) if counts[i] < largest] or [i for i in range(1, number_of) if counts[i] < limit]
        whole, remaining = sum([loads[i] for i in free]), surplus
        for i in free:
            more = min(limit - counts[i], max(1, remaining * loads[i] // whole), surplus)
            counts[i] = counts[i] + more
            surplus = surplus - more
    return np.array(counts)


def centred(stream_key, shape, width, reach, pieces=(), held_as=jnp.bfloat16):
    entries = jax.random.normal(stream_key, shape, jnp.float32) * width
    if len(pieces) > 0:
        entries = shard_levels(stream_key, shape, pieces, -0.22, 0.18) * entries
    return jnp.clip(entries, min=-reach, max=reach).astype(held_as)


def setup_inputs(seed: int = 0) -> dict:
    key_of = jax.random.split(jax.random.key(seed), 10)
    sections = centred(key_of[0], (PARTICLES, PIX, PIX), 1.0, 6.0, ((0, 16),))
    images = centred(key_of[1], (PARTICLES, TILTS, PIX, PIX), 1.0, 6.0, ((0, 16), (1, 2)))
    slice_rows = centred(key_of[2], (TILTS, PIX, PIX), PIX ** -0.5, 0.375, ((0, 2),))
    slice_cols = centred(key_of[3], (TILTS, PIX, PIX), PIX ** -0.5, 0.375, ((0, 2),))
    ctf_filter = centred(key_of[4], (TILTS, PIX, PIX), PIX ** -0.5, 0.375, ((0, 2),))
    nbr_owner_keys = jax.random.split(jax.random.fold_in(key_of[5], 1), PARTICLES * 2 // (2 * PART_DEV))
    nbr_owner_turns = jax.random.permutation(jax.random.fold_in(key_of[5], 3), PARTICLES * 2 // (2 * PART_DEV))
    nbr_owner = jax.vmap(lambda own, number: assign_block(jax.random.fold_in(key_of[5], 2), own, number, 2 * PART_DEV, N_DOM, NB // 2, CAP, 2))(nbr_owner_keys, nbr_owner_turns).reshape((PARTICLES, 2, NB // 2))
    nbr_local = set_ends(jax.random.randint(key_of[6], (PARTICLES, NB), 0, PART_DEV), jax.random.fold_in(key_of[6], 1), 0, PART_DEV - 1).astype(jnp.int32)
    nbr_side = set_ends(jax.random.randint(key_of[7], (PARTICLES, NB), 0, 2), jax.random.fold_in(key_of[7], 1), 0, 1).astype(jnp.int32)
    nbr_weight = jnp.clip(jnp.exp(math.log(2.0) - 2.0794415 * jax.random.uniform(key_of[8], (PARTICLES, NB), jnp.float32) ** shard_levels(key_of[8], (PARTICLES, NB), ((0, 16),), -0.2, 0.2)), 0.25, 2.0)
    return dict(sections=sections, images=images, slice_rows=slice_rows, slice_cols=slice_cols, ctf_filter=ctf_filter, nbr_owner=nbr_owner, nbr_local=nbr_local, nbr_side=nbr_side, nbr_weight=nbr_weight)


def project_tiles(section, rows_weight, cols_weight):
    halfway = jnp.einsum('ij,tlj->til', section.astype(jnp.float32), cols_weight.astype(jnp.float32)).astype(jnp.bfloat16)
    return jnp.einsum('tai,til->tal', rows_weight.astype(jnp.float32), halfway.astype(jnp.float32)).astype(jnp.bfloat16)


def weighted_error(section, image_tiles, near_bands, side_list, weights, rows_weight, cols_weight, ctf_filter):
    projected = project_tiles(section, rows_weight, cols_weight)
    weight_lower = jnp.where(side_list == 0, weights, 0.0)
    weight_upper = jnp.where(side_list == 1, weights, 0.0)
    band_data = near_bands.astype(jnp.float32)
    lower_part = jnp.einsum('j,jtrc->trc', weight_lower, band_data)
    upper_part = jnp.einsum('j,jtrc->trc', weight_upper, band_data)
    residual = image_tiles.astype(jnp.float32) - projected.astype(jnp.float32)
    residual = residual.at[:, :OVL].add(-upper_part)
    residual = residual.at[:, PIX - OVL:].add(-lower_part)
    residual_portion = residual.astype(jnp.bfloat16)
    broad_filter = ctf_filter.astype(jnp.float32)
    smoothed_images = jnp.einsum('gku,guo->gko', broad_filter, residual_portion.astype(jnp.float32)).astype(jnp.bfloat16)
    filtered_images = jnp.einsum('rws,rus->rwu', smoothed_images.astype(jnp.float32), broad_filter)
    score_sum = jnp.sum(filtered_images * filtered_images)
    filtered_portion = filtered_images.astype(jnp.bfloat16)
    reverse_pass = jnp.einsum('zxs,zxo->zso', broad_filter, filtered_portion.astype(jnp.float32)).astype(jnp.bfloat16)
    weighted = jnp.einsum('tbc,tcd->tbd', reverse_pass.astype(jnp.float32), broad_filter).astype(jnp.bfloat16)
    return weighted, score_sum


def reference(sections, images, slice_rows, slice_cols, ctf_filter, nbr_owner, nbr_local, nbr_side, nbr_weight):
    near_ids = (nbr_owner.reshape(PARTICLES, NB) * PART_DEV + nbr_local).astype(jnp.int32)

    def edge_of(section):
        projected = project_tiles(section, slice_rows, slice_cols)
        return jnp.stack((projected[:, :OVL], projected[:, PIX - OVL:]), axis=0)

    border_rows = lax.map(edge_of, sections)

    def forward_step(totals, inputs):
        section, image_tiles, near_list, side_list, weights = inputs
        near_bands = border_rows[near_list, side_list]
        weighted, score_sum = weighted_error(section, image_tiles, near_bands, side_list, weights, slice_rows, slice_cols, ctf_filter)
        chosen = jnp.where((side_list == 0)[:, None, None, None], weighted[None, :, PIX - OVL:], weighted[None, :, :OVL])
        sent_back = (weights[:, None, None, None] * chosen.astype(jnp.float32)).astype(jnp.bfloat16)
        sent_back = lax.optimization_barrier(sent_back).astype(jnp.float32)
        totals = totals.at[near_list * 2 + side_list].add(sent_back)
        return totals, score_sum

    empty_sum = jnp.zeros((PARTICLES * 2, TILTS, OVL, PIX), jnp.float32)
    totals, score_sums = lax.scan(forward_step, empty_sum, (sections, images, near_ids, nbr_side, nbr_weight))
    scores = 0.5 * score_sums / (TILTS * PIX * PIX)
    totals = totals.reshape(PARTICLES, 2, TILTS, OVL, PIX)

    def backward_of(inputs):
        section, image_tiles, near_list, side_list, weights, returned = inputs
        near_bands = border_rows[near_list, side_list]
        weighted, score_sum = weighted_error(section, image_tiles, near_bands, side_list, weights, slice_rows, slice_cols, ctf_filter)
        proj_grad = weighted.astype(jnp.float32)
        proj_grad = proj_grad.at[:, :OVL].add(returned[0])
        proj_grad = proj_grad.at[:, PIX - OVL:].add(returned[1])
        proj_half = proj_grad.astype(jnp.bfloat16)
        upward = jnp.einsum('tai,tal->til', slice_rows.astype(jnp.float32), proj_half.astype(jnp.float32)).astype(jnp.bfloat16)
        return -jnp.einsum('til,tlj->ij', upward.astype(jnp.float32), slice_cols.astype(jnp.float32))

    section_grad = lax.map(backward_of, (sections, images, near_ids, nbr_side, nbr_weight, totals))
    return section_grad, scores
```

```python
import jax
import jax.numpy as jnp
from jax import lax
from jax.sharding import PartitionSpec as P

OVL = 16


def split_dot(weights, bands):
    hi = weights.astype(jnp.bfloat16)
    rest = weights - hi.astype(jnp.float32)
    mid = rest.astype(jnp.bfloat16)
    low = (rest - mid.astype(jnp.float32)).astype(jnp.bfloat16)
    total = jnp.dot(hi, bands, preferred_element_type=jnp.float32)
    total = total + jnp.dot(mid, bands, preferred_element_type=jnp.float32)
    return total + jnp.dot(low, bands, preferred_element_type=jnp.float32)


def on_device(
    sections, images, slice_rows, slice_cols, ctf_filter, nbr_owner, nbr_local, nbr_side, nbr_weight
):
    own_count = sections.shape[0]
    pixels = sections.shape[1]
    tilt_count = images.shape[1]
    neighbours = nbr_local.shape[1]
    peer_count = lax.axis_size("dom")
    total = own_count * peer_count
    me = lax.axis_index("dom")
    band_size = tilt_count * OVL * pixels

    target = nbr_owner.reshape(own_count, neighbours) * own_count + nbr_local
    every = jnp.arange(total)

    hits = target[:, :, None] == every[None, None, :]
    fwd = [
        jnp.sum(jnp.where(hits & (nbr_side == s)[:, :, None], nbr_weight[:, :, None], 0.0), axis=1)
        for s in (0, 1)
    ]

    target_all = lax.all_gather(target, "dom", axis=0, tiled=True)
    side_all = lax.all_gather(nbr_side, "dom", axis=0, tiled=True)
    weight_all = lax.all_gather(nbr_weight, "dom", axis=0, tiled=True)

    halfway = jnp.einsum(
        "kij,tlj->ktil", sections, slice_cols, preferred_element_type=jnp.float32
    ).astype(jnp.bfloat16)
    projected = jnp.einsum(
        "tai,ktil->ktal", slice_rows, halfway, preferred_element_type=jnp.float32
    ).astype(jnp.bfloat16)
    edges = jnp.stack((projected[:, :, :OVL], projected[:, :, pixels - OVL :]), axis=1)
    edges_all = lax.all_gather(edges, "dom", axis=0, tiled=True)

    lower_part = split_dot(fwd[0], edges_all[:, 0].reshape(total, band_size))
    upper_part = split_dot(fwd[1], edges_all[:, 1].reshape(total, band_size))
    lower_part = lower_part.reshape(own_count, tilt_count, OVL, pixels)
    upper_part = upper_part.reshape(own_count, tilt_count, OVL, pixels)

    residual = images.astype(jnp.float32) - projected.astype(jnp.float32)
    residual = residual.at[:, :, :OVL].add(-upper_part)
    residual = residual.at[:, :, pixels - OVL :].add(-lower_part)
    residual_portion = residual.astype(jnp.bfloat16)
    smoothed_images = jnp.einsum(
        "tab,ktbc->ktac", ctf_filter, residual_portion, preferred_element_type=jnp.float32
    ).astype(jnp.bfloat16)
    filtered_images = jnp.einsum(
        "ktac,tdc->ktad", smoothed_images, ctf_filter, preferred_element_type=jnp.float32
    )
    score_part = jnp.sum(filtered_images * filtered_images, axis=(1, 2, 3))
    tilt_groups = lax.axis_size("tilt")
    scores = 0.5 * lax.psum(score_part, "tilt") / (tilt_count * tilt_groups * pixels * pixels)
    filtered_portion = filtered_images.astype(jnp.bfloat16)
    reverse_pass = jnp.einsum(
        "tab,ktac->ktbc", ctf_filter, filtered_portion, preferred_element_type=jnp.float32
    ).astype(jnp.bfloat16)
    weighted = jnp.einsum(
        "ktbc,tcd->ktbd", reverse_pass, ctf_filter, preferred_element_type=jnp.float32
    ).astype(jnp.bfloat16)

    grad_bands = jnp.stack((weighted[:, :, :OVL], weighted[:, :, pixels - OVL :]), axis=1)
    grad_all = lax.all_gather(grad_bands, "dom", axis=0, tiled=True)

    mine = me * own_count + jnp.arange(own_count)
    named = target_all[None, :, :] == mine[:, None, None]
    back = [
        jnp.sum(jnp.where(named & (side_all == s)[None], weight_all[None], 0.0), axis=2)
        for s in (0, 1)
    ]
    add_top = split_dot(back[0], grad_all[:, 1].reshape(total, band_size))
    add_bottom = split_dot(back[1], grad_all[:, 0].reshape(total, band_size))
    add_top = add_top.reshape(own_count, tilt_count, OVL, pixels)
    add_bottom = add_bottom.reshape(own_count, tilt_count, OVL, pixels)

    proj_grad = weighted.astype(jnp.float32)
    proj_grad = proj_grad.at[:, :, :OVL].add(add_top)
    proj_grad = proj_grad.at[:, :, pixels - OVL :].add(add_bottom)
    proj_half = proj_grad.astype(jnp.bfloat16)
    upward = jnp.einsum(
        "tai,ktal->ktil", slice_rows, proj_half, preferred_element_type=jnp.float32
    ).astype(jnp.bfloat16)
    partial_grad = -jnp.einsum(
        "ktil,tlj->kij", upward, slice_cols, preferred_element_type=jnp.float32
    )
    section_grad = lax.psum_scatter(partial_grad, "tilt", scatter_dimension=1, tiled=True)
    return (section_grad, scores)


def solution(mesh):
    in_specs = (
        P("dom", None, None),
        P("dom", "tilt", None, None),
        P("tilt", None, None),
        P("tilt", None, None),
        P("tilt", None, None),
        P("dom", None, None),
        P("dom", None),
        P("dom", None),
        P("dom", None),
    )
    out_specs = (P("dom", "tilt", None), P("dom"))
    return jax.shard_map(
        on_device, mesh=mesh, in_specs=in_specs, out_specs=out_specs, check_vma=False
    )
```

```python
import jax
import jax.numpy as jnp
from jax import lax
from jax.sharding import PartitionSpec as P

OVL = 16


def split_dot(weights, bands):
    hi = weights.astype(jnp.bfloat16)
    rest = weights - hi.astype(jnp.float32)
    mid = rest.astype(jnp.bfloat16)
    low = (rest - mid.astype(jnp.float32)).astype(jnp.bfloat16)
    total = jnp.dot(hi, bands, preferred_element_type=jnp.float32)
    total = total + jnp.dot(mid, bands, preferred_element_type=jnp.float32)
    return total + jnp.dot(low, bands, preferred_element_type=jnp.float32)


def on_device(
    sections, images, slice_rows, slice_cols, ctf_filter, nbr_owner, nbr_local, nbr_side, nbr_weight
):
    own_count = sections.shape[0]
    pixels = sections.shape[1]
    tilt_count = images.shape[1]
    neighbours = nbr_local.shape[1]
    peer_count = lax.axis_size("dom")
    total = own_count * peer_count
    me = lax.axis_index("dom")
    band_size = tilt_count * OVL * pixels

    target = nbr_owner.reshape(own_count, neighbours) * own_count + nbr_local
    every = jnp.arange(total)

    hits = target[:, :, None] == every[None, None, :]
    fwd = [
        jnp.sum(jnp.where(hits & (nbr_side == s)[:, :, None], nbr_weight[:, :, None], 0.0), axis=1)
        for s in (0, 1)
    ]

    halfway = jnp.einsum(
        "kij,tlj->ktil", sections, slice_cols, preferred_element_type=jnp.float32
    ).astype(jnp.bfloat16)
    projected = jnp.einsum(
        "tai,ktil->ktal", slice_rows, halfway, preferred_element_type=jnp.float32
    ).astype(jnp.bfloat16)
    edges = jnp.stack((projected[:, :, :OVL], projected[:, :, pixels - OVL :]), axis=1)
    edges_all = lax.all_to_all(
        jnp.broadcast_to(edges[None], (peer_count,) + edges.shape).reshape(
            (total,) + edges.shape[1:]
        ),
        "dom",
        split_axis=0,
        concat_axis=0,
        tiled=True,
    )

    lower_part = split_dot(fwd[0], edges_all[:, 0].reshape(total, band_size))
    upper_part = split_dot(fwd[1], edges_all[:, 1].reshape(total, band_size))
    lower_part = lower_part.reshape(own_count, tilt_count, OVL, pixels)
    upper_part = upper_part.reshape(own_count, tilt_count, OVL, pixels)

    residual = images.astype(jnp.float32) - projected.astype(jnp.float32)
    residual = residual.at[:, :, :OVL].add(-upper_part)
    residual = residual.at[:, :, pixels - OVL :].add(-lower_part)
    residual_portion = residual.astype(jnp.bfloat16)
    smoothed_images = jnp.einsum(
        "tab,ktbc->ktac", ctf_filter, residual_portion, preferred_element_type=jnp.float32
    ).astype(jnp.bfloat16)
    filtered_images = jnp.einsum(
        "ktac,tdc->ktad", smoothed_images, ctf_filter, preferred_element_type=jnp.float32
    )
    score_part = jnp.sum(filtered_images * filtered_images, axis=(1, 2, 3))
    tilt_groups = lax.axis_size("tilt")
    filtered_portion = filtered_images.astype(jnp.bfloat16)
    reverse_pass = jnp.einsum(
        "tab,ktac->ktbc", ctf_filter, filtered_portion, preferred_element_type=jnp.float32
    ).astype(jnp.bfloat16)
    weighted = jnp.einsum(
        "ktbc,tcd->ktbd", reverse_pass, ctf_filter, preferred_element_type=jnp.float32
    ).astype(jnp.bfloat16)

    bottom_rows = weighted[:, :, pixels - OVL :].reshape(own_count, band_size)
    top_rows = weighted[:, :, :OVL].reshape(own_count, band_size)
    to_top = split_dot(fwd[0].T, bottom_rows)
    to_bottom = split_dot(fwd[1].T, top_rows)
    outgoing = jnp.stack((to_top, to_bottom), axis=1).astype(jnp.bfloat16)
    returned = lax.all_to_all(outgoing, "dom", split_axis=0, concat_axis=0, tiled=True)
    returned = jnp.sum(
        returned.reshape(peer_count, own_count, 2, band_size).astype(jnp.float32), axis=0
    )
    add_top = returned[:, 0].reshape(own_count, tilt_count, OVL, pixels)
    add_bottom = returned[:, 1].reshape(own_count, tilt_count, OVL, pixels)

    proj_grad = weighted.astype(jnp.float32)
    proj_grad = proj_grad.at[:, :, :OVL].add(add_top)
    proj_grad = proj_grad.at[:, :, pixels - OVL :].add(add_bottom)
    proj_half = proj_grad.astype(jnp.bfloat16)
    upward = jnp.einsum(
        "tai,ktal->ktil", slice_rows, proj_half, preferred_element_type=jnp.float32
    ).astype(jnp.bfloat16)
    partial_grad = -jnp.einsum(
        "ktil,tlj->kij", upward, slice_cols, preferred_element_type=jnp.float32
    )
    scale = 0.5 / (tilt_count * tilt_groups * pixels * pixels)
    if tilt_groups != 2:
        scores = scale * lax.psum(score_part, "tilt")
        section_grad = lax.psum_scatter(partial_grad, "tilt", scatter_dimension=1, tiled=True)
        return (section_grad, scores)
    half = pixels // 2
    side = lax.axis_index("tilt")
    kept = lax.dynamic_slice_in_dim(partial_grad, side * half, half, axis=1)
    given = lax.dynamic_slice_in_dim(partial_grad, (1 - side) * half, half, axis=1)
    parcel = jnp.concatenate((given.reshape(-1), score_part))
    parcel = lax.ppermute(parcel, "tilt", [(0, 1), (1, 0)])
    section_grad = kept + parcel[: given.size].reshape(given.shape)
    scores = scale * (score_part + parcel[given.size :])
    return (section_grad, scores)


def solution(mesh):
    in_specs = (
        P("dom", None, None),
        P("dom", "tilt", None, None),
        P("tilt", None, None),
        P("tilt", None, None),
        P("tilt", None, None),
        P("dom", None, None),
        P("dom", None),
        P("dom", None),
        P("dom", None),
    )
    out_specs = (P("dom", "tilt", None), P("dom"))
    return jax.shard_map(
        on_device, mesh=mesh, in_specs=in_specs, out_specs=out_specs, check_vma=False
    )
```

```python
import jax
import jax.numpy as jnp
from jax import lax
from jax.sharding import PartitionSpec as P

OVL = 16


def split_dot(weights, bands):
    hi = weights.astype(jnp.bfloat16)
    rest = weights - hi.astype(jnp.float32)
    mid = rest.astype(jnp.bfloat16)
    low = (rest - mid.astype(jnp.float32)).astype(jnp.bfloat16)
    total = jnp.dot(hi, bands, preferred_element_type=jnp.float32)
    total = total + jnp.dot(mid, bands, preferred_element_type=jnp.float32)
    return total + jnp.dot(low, bands, preferred_element_type=jnp.float32)


def on_device(
    sections, images, slice_rows, slice_cols, ctf_filter, nbr_owner, nbr_local, nbr_side, nbr_weight
):
    own_count = sections.shape[0]
    pixels = sections.shape[1]
    tilt_count = images.shape[1]
    neighbours = nbr_local.shape[1]
    peer_count = lax.axis_size("dom")
    total = own_count * peer_count
    me = lax.axis_index("dom")
    band_size = tilt_count * OVL * pixels

    steps = peer_count.bit_length() - 1
    relative = nbr_owner.reshape(own_count, neighbours) ^ me
    flipped = sum(((relative >> (steps - 1 - b)) & 1) << b for b in range(steps))
    every = jnp.arange(total)

    def weights_for(blocks, side):
        hits = (blocks * own_count + nbr_local)[:, :, None] == every[None, None, :]
        hits = hits & (nbr_side == side)[:, :, None]
        return jnp.sum(jnp.where(hits, nbr_weight[:, :, None], 0.0), axis=1)

    fwd = [weights_for(flipped, s) for s in (0, 1)]
    back = [weights_for(relative, s) for s in (0, 1)]

    halfway = jnp.einsum(
        "kij,tlj->ktil", sections, slice_cols, preferred_element_type=jnp.float32
    ).astype(jnp.bfloat16)
    projected = jnp.einsum(
        "tai,ktil->ktal", slice_rows, halfway, preferred_element_type=jnp.float32
    ).astype(jnp.bfloat16)
    edges = jnp.stack((projected[:, :, :OVL], projected[:, :, pixels - OVL :]), axis=1)
    edges_all = edges
    for b in range(steps):
        stride = peer_count >> (b + 1)
        pairs = [(i, i ^ stride) for i in range(peer_count)]
        edges_all = jnp.concatenate((edges_all, lax.ppermute(edges_all, "dom", pairs)), axis=0)

    lower_part = split_dot(fwd[0], edges_all[:, 0].reshape(total, band_size))
    upper_part = split_dot(fwd[1], edges_all[:, 1].reshape(total, band_size))
    lower_part = lower_part.reshape(own_count, tilt_count, OVL, pixels)
    upper_part = upper_part.reshape(own_count, tilt_count, OVL, pixels)

    residual = images.astype(jnp.float32) - projected.astype(jnp.float32)
    residual = residual.at[:, :, :OVL].add(-upper_part)
    residual = residual.at[:, :, pixels - OVL :].add(-lower_part)
    residual_portion = residual.astype(jnp.bfloat16)
    smoothed_images = jnp.einsum(
        "tab,ktbc->ktac", ctf_filter, residual_portion, preferred_element_type=jnp.float32
    ).astype(jnp.bfloat16)
    filtered_images = jnp.einsum(
        "ktac,tdc->ktad", smoothed_images, ctf_filter, preferred_element_type=jnp.float32
    )
    score_part = jnp.sum(filtered_images * filtered_images, axis=(1, 2, 3))
    tilt_groups = lax.axis_size("tilt")
    filtered_portion = filtered_images.astype(jnp.bfloat16)
    reverse_pass = jnp.einsum(
        "tab,ktac->ktbc", ctf_filter, filtered_portion, preferred_element_type=jnp.float32
    ).astype(jnp.bfloat16)
    weighted = jnp.einsum(
        "ktbc,tcd->ktbd", reverse_pass, ctf_filter, preferred_element_type=jnp.float32
    ).astype(jnp.bfloat16)

    bottom_rows = weighted[:, :, pixels - OVL :].reshape(own_count, band_size)
    top_rows = weighted[:, :, :OVL].reshape(own_count, band_size)
    to_top = split_dot(back[0].T, bottom_rows)
    to_bottom = split_dot(back[1].T, top_rows)
    returned = jnp.stack((to_top, to_bottom), axis=1).reshape(
        (2,) * steps + (own_count, 2, band_size)
    )
    for b in range(steps):
        stride = 1 << b
        pairs = [(i, i ^ stride) for i in range(peer_count)]
        axis = steps - 1 - b
        kept = lax.index_in_dim(returned, 0, axis, keepdims=False)
        given = lax.index_in_dim(returned, 1, axis, keepdims=False).astype(jnp.bfloat16)
        returned = kept + lax.ppermute(given, "dom", pairs).astype(jnp.float32)
    add_top = returned[:, 0].reshape(own_count, tilt_count, OVL, pixels)
    add_bottom = returned[:, 1].reshape(own_count, tilt_count, OVL, pixels)

    proj_grad = weighted.astype(jnp.float32)
    proj_grad = proj_grad.at[:, :, :OVL].add(add_top)
    proj_grad = proj_grad.at[:, :, pixels - OVL :].add(add_bottom)
    proj_half = proj_grad.astype(jnp.bfloat16)
    upward = jnp.einsum(
        "tai,ktal->ktil", slice_rows, proj_half, preferred_element_type=jnp.float32
    ).astype(jnp.bfloat16)
    partial_grad = -jnp.einsum(
        "ktil,tlj->kij", upward, slice_cols, preferred_element_type=jnp.float32
    )
    scale = 0.5 / (tilt_count * tilt_groups * pixels * pixels)
    if tilt_groups != 2:
        scores = scale * lax.psum(score_part, "tilt")
        section_grad = lax.psum_scatter(partial_grad, "tilt", scatter_dimension=1, tiled=True)
        return (section_grad, scores)
    half = pixels // 2
    side = lax.axis_index("tilt")
    kept = lax.dynamic_slice_in_dim(partial_grad, side * half, half, axis=1)
    given = lax.dynamic_slice_in_dim(partial_grad, (1 - side) * half, half, axis=1)
    score_hi = score_part.astype(jnp.bfloat16)
    score_rest = score_part - score_hi.astype(jnp.float32)
    score_mid = score_rest.astype(jnp.bfloat16)
    score_low = (score_rest - score_mid.astype(jnp.float32)).astype(jnp.bfloat16)
    parcel = jnp.concatenate(
        (given.reshape(-1).astype(jnp.bfloat16), score_hi, score_mid, score_low)
    )
    parcel = lax.ppermute(parcel, "tilt", [(0, 1), (1, 0)]).astype(jnp.float32)
    section_grad = kept + parcel[: given.size].reshape(given.shape)
    parts = parcel[given.size :].reshape(3, own_count)
    scores = scale * (score_part + (parts[0] + (parts[1] + parts[2])))
    return (section_grad, scores)


def solution(mesh):
    in_specs = (
        P("dom", None, None),
        P("dom", "tilt", None, None),
        P("tilt", None, None),
        P("tilt", None, None),
        P("tilt", None, None),
        P("dom", None, None),
        P("dom", None),
        P("dom", None),
        P("dom", None),
    )
    out_specs = (P("dom", "tilt", None), P("dom"))
    return jax.shard_map(
        on_device, mesh=mesh, in_specs=in_specs, out_specs=out_specs, check_vma=False
    )
```

```python
import jax
import jax.numpy as jnp
from jax import lax
from jax.experimental import pallas as pl
from jax.experimental.pallas import tpu as pltpu
from jax.sharding import PartitionSpec as P

OVL = 16


def split_dot(weights, bands):
    hi = weights.astype(jnp.bfloat16)
    rest = weights - hi.astype(jnp.float32)
    mid = rest.astype(jnp.bfloat16)
    low = (rest - mid.astype(jnp.float32)).astype(jnp.bfloat16)
    total = jnp.dot(hi, bands, preferred_element_type=jnp.float32)
    total = total + jnp.dot(mid, bands, preferred_element_type=jnp.float32)
    return total + jnp.dot(low, bands, preferred_element_type=jnp.float32)


def middle_kernel(
    fwd_ref, back_ref, image_ref, proj_ref, edge_ref, ctf_ref,
    weighted_ref, score_ref, return_ref, residual_ref,
):
    k = pl.program_id(1)
    own_count = pl.num_programs(1)
    total = edge_ref.shape[0]
    pixels = image_ref.shape[-1]

    def band_sum(q, carry):
        lower, upper = carry
        lower = lower + fwd_ref[k * total + q] * edge_ref[q, 0, 0].astype(jnp.float32)
        upper = upper + fwd_ref[(own_count + k) * total + q] * edge_ref[q, 1, 0].astype(jnp.float32)
        return lower, upper

    zero = jnp.zeros((OVL, pixels), jnp.float32)
    lower, upper = lax.fori_loop(0, total, band_sum, (zero, zero))
    residual_ref[...] = image_ref[0, 0].astype(jnp.float32) - proj_ref[0, 0].astype(jnp.float32)
    residual_ref[:OVL] = residual_ref[:OVL] - upper
    residual_ref[pixels - OVL :] = residual_ref[pixels - OVL :] - lower
    residual = residual_ref[...].astype(jnp.bfloat16)
    ctf = ctf_ref[0]
    smoothed = jnp.dot(ctf, residual, preferred_element_type=jnp.float32).astype(jnp.bfloat16)
    filtered = lax.dot_general(
        smoothed, ctf, (((1,), (1,)), ((), ())), preferred_element_type=jnp.float32
    )
    score_ref[...] = jnp.full(score_ref.shape, jnp.sum(filtered * filtered), jnp.float32)
    reverse = lax.dot_general(
        ctf, filtered.astype(jnp.bfloat16), (((0,), (0,)), ((), ())),
        preferred_element_type=jnp.float32,
    ).astype(jnp.bfloat16)
    weighted = jnp.dot(reverse, ctf, preferred_element_type=jnp.float32).astype(jnp.bfloat16)
    weighted_ref[0, 0] = weighted

    @pl.when(k == 0)
    def _():
        return_ref[...] = jnp.zeros_like(return_ref)

    bottom_rows = weighted[pixels - OVL :].astype(jnp.float32)
    top_rows = weighted[:OVL].astype(jnp.float32)

    def give_back(q, carry):
        return_ref[q, 0, 0] = return_ref[q, 0, 0] + back_ref[k * total + q] * bottom_rows
        return_ref[q, 1, 0] = return_ref[q, 1, 0] + back_ref[(own_count + k) * total + q] * top_rows
        return carry

    lax.fori_loop(0, total, give_back, 0)


def middle(fwd, back, images, projected, edges_all, ctf_filter):
    own_count, tilt_count, pixels, _ = images.shape
    total = edges_all.shape[0]
    tile = pl.BlockSpec((1, 1, pixels, pixels), lambda t, k: (k, t, 0, 0))
    bands = pl.BlockSpec((total, 2, 1, OVL, pixels), lambda t, k: (0, 0, t, 0, 0))
    smem = pl.BlockSpec(memory_space=pltpu.SMEM)
    flops = own_count * tilt_count * (8 * pixels**3 + 8 * total * OVL * pixels)
    moved = 2 * images.size * 3 + 2 * edges_all.size + 4 * edges_all.size + 2 * ctf_filter.size
    return pl.pallas_call(
        middle_kernel,
        grid=(tilt_count, own_count),
        in_specs=[
            smem,
            smem,
            tile,
            tile,
            bands,
            pl.BlockSpec((1, pixels, pixels), lambda t, k: (t, 0, 0)),
        ],
        out_specs=[
            tile,
            pl.BlockSpec((1, 1, 8, 128), lambda t, k: (t, k, 0, 0)),
            bands,
        ],
        out_shape=[
            jax.ShapeDtypeStruct(images.shape, jnp.bfloat16),
            jax.ShapeDtypeStruct((tilt_count, own_count, 8, 128), jnp.float32),
            jax.ShapeDtypeStruct(edges_all.shape, jnp.float32),
        ],
        scratch_shapes=[pltpu.VMEM((pixels, pixels), jnp.float32)],
        compiler_params=pltpu.CompilerParams(
            dimension_semantics=("arbitrary", "arbitrary")
        ),
        cost_estimate=pl.CostEstimate(flops=flops, transcendentals=0, bytes_accessed=moved),
    )(fwd.reshape(-1), back.reshape(-1), images, projected, edges_all, ctf_filter)


def on_device(
    sections, images, slice_rows, slice_cols, ctf_filter, nbr_owner, nbr_local, nbr_side, nbr_weight
):
    own_count = sections.shape[0]
    pixels = sections.shape[1]
    tilt_count = images.shape[1]
    neighbours = nbr_local.shape[1]
    peer_count = lax.axis_size("dom")
    total = own_count * peer_count
    me = lax.axis_index("dom")
    band_size = tilt_count * OVL * pixels

    steps = peer_count.bit_length() - 1
    relative = nbr_owner.reshape(own_count, neighbours) ^ me
    flipped = sum(((relative >> (steps - 1 - b)) & 1) << b for b in range(steps))
    every = jnp.arange(total)

    def weights_for(blocks, side):
        hits = (blocks * own_count + nbr_local)[:, :, None] == every[None, None, :]
        hits = hits & (nbr_side == side)[:, :, None]
        return jnp.sum(jnp.where(hits, nbr_weight[:, :, None], 0.0), axis=1)

    fwd = [weights_for(flipped, s) for s in (0, 1)]
    back = [weights_for(relative, s) for s in (0, 1)]

    halfway = jnp.einsum(
        "kij,tlj->ktil", sections, slice_cols, preferred_element_type=jnp.float32
    ).astype(jnp.bfloat16)
    projected = jnp.einsum(
        "tai,ktil->ktal", slice_rows, halfway, preferred_element_type=jnp.float32
    ).astype(jnp.bfloat16)
    edges = jnp.stack((projected[:, :, :OVL], projected[:, :, pixels - OVL :]), axis=1)
    edges_all = edges
    for b in range(steps):
        stride = peer_count >> (b + 1)
        pairs = [(i, i ^ stride) for i in range(peer_count)]
        edges_all = jnp.concatenate((edges_all, lax.ppermute(edges_all, "dom", pairs)), axis=0)

    weighted, score_tiles, returned = middle(
        jnp.stack(fwd), jnp.stack(back), images, projected, edges_all, ctf_filter
    )
    score_part = jnp.sum(score_tiles[:, :, 0, 0], axis=0)
    tilt_groups = lax.axis_size("tilt")

    returned = returned.reshape((2,) * steps + (own_count, 2, band_size))
    for b in range(steps):
        stride = 1 << b
        pairs = [(i, i ^ stride) for i in range(peer_count)]
        axis = steps - 1 - b
        kept = lax.index_in_dim(returned, 0, axis, keepdims=False)
        given = lax.index_in_dim(returned, 1, axis, keepdims=False).astype(jnp.bfloat16)
        returned = kept + lax.ppermute(given, "dom", pairs).astype(jnp.float32)
    add_top = returned[:, 0].reshape(own_count, tilt_count, OVL, pixels)
    add_bottom = returned[:, 1].reshape(own_count, tilt_count, OVL, pixels)

    proj_grad = weighted.astype(jnp.float32)
    proj_grad = proj_grad.at[:, :, :OVL].add(add_top)
    proj_grad = proj_grad.at[:, :, pixels - OVL :].add(add_bottom)
    proj_half = proj_grad.astype(jnp.bfloat16)
    upward = jnp.einsum(
        "tai,ktal->ktil", slice_rows, proj_half, preferred_element_type=jnp.float32
    ).astype(jnp.bfloat16)
    partial_grad = -jnp.einsum(
        "ktil,tlj->kij", upward, slice_cols, preferred_element_type=jnp.float32
    )
    scale = 0.5 / (tilt_count * tilt_groups * pixels * pixels)
    if tilt_groups != 2:
        scores = scale * lax.psum(score_part, "tilt")
        section_grad = lax.psum_scatter(partial_grad, "tilt", scatter_dimension=1, tiled=True)
        return (section_grad, scores)
    half = pixels // 2
    side = lax.axis_index("tilt")
    kept = lax.dynamic_slice_in_dim(partial_grad, side * half, half, axis=1)
    given = lax.dynamic_slice_in_dim(partial_grad, (1 - side) * half, half, axis=1)
    score_hi = score_part.astype(jnp.bfloat16)
    score_rest = score_part - score_hi.astype(jnp.float32)
    score_mid = score_rest.astype(jnp.bfloat16)
    score_low = (score_rest - score_mid.astype(jnp.float32)).astype(jnp.bfloat16)
    parcel = jnp.concatenate(
        (given.reshape(-1).astype(jnp.bfloat16), score_hi, score_mid, score_low)
    )
    parcel = lax.ppermute(parcel, "tilt", [(0, 1), (1, 0)]).astype(jnp.float32)
    section_grad = kept + parcel[: given.size].reshape(given.shape)
    parts = parcel[given.size :].reshape(3, own_count)
    scores = scale * (score_part + (parts[0] + (parts[1] + parts[2])))
    return (section_grad, scores)


def solution(mesh):
    in_specs = (
        P("dom", None, None),
        P("dom", "tilt", None, None),
        P("tilt", None, None),
        P("tilt", None, None),
        P("tilt", None, None),
        P("dom", None, None),
        P("dom", None),
        P("dom", None),
        P("dom", None),
    )
    out_specs = (P("dom", "tilt", None), P("dom"))
    return jax.shard_map(
        on_device, mesh=mesh, in_specs=in_specs, out_specs=out_specs, check_vma=False
    )
```

```python
import jax
import jax.numpy as jnp
from jax import lax
from jax.experimental import pallas as pl
from jax.experimental.pallas import tpu as pltpu
from jax.sharding import PartitionSpec as P

OVL = 16


def split_dot(weights, bands):
    hi = weights.astype(jnp.bfloat16)
    rest = weights - hi.astype(jnp.float32)
    mid = rest.astype(jnp.bfloat16)
    low = (rest - mid.astype(jnp.float32)).astype(jnp.bfloat16)
    total = jnp.dot(hi, bands, preferred_element_type=jnp.float32)
    total = total + jnp.dot(mid, bands, preferred_element_type=jnp.float32)
    return total + jnp.dot(low, bands, preferred_element_type=jnp.float32)


def middle_kernel(
    fwd_ref, back_ref, image_ref, proj_ref, edge_ref, ctf_ref,
    weighted_ref, score_ref, return_ref, residual_ref,
):
    k = pl.program_id(1)
    total = edge_ref.shape[0]
    pixels = image_ref.shape[-1]

    def band_sum(q, carry):
        lower, upper = carry
        lower = lower + fwd_ref[0, k, q] * edge_ref[q, 0, 0].astype(jnp.float32)
        upper = upper + fwd_ref[1, k, q] * edge_ref[q, 1, 0].astype(jnp.float32)
        return lower, upper

    zero = jnp.zeros((OVL, pixels), jnp.float32)
    lower, upper = lax.fori_loop(0, total, band_sum, (zero, zero))
    residual_ref[...] = image_ref[0, 0].astype(jnp.float32) - proj_ref[0, 0].astype(jnp.float32)
    residual_ref[:OVL] = residual_ref[:OVL] - upper
    residual_ref[pixels - OVL :] = residual_ref[pixels - OVL :] - lower
    residual = residual_ref[...].astype(jnp.bfloat16)
    ctf = ctf_ref[0]
    smoothed = jnp.dot(ctf, residual, preferred_element_type=jnp.float32).astype(jnp.bfloat16)
    filtered = lax.dot_general(
        smoothed, ctf, (((1,), (1,)), ((), ())), preferred_element_type=jnp.float32
    )
    score_ref[...] = jnp.full(score_ref.shape, jnp.sum(filtered * filtered), jnp.float32)
    reverse = lax.dot_general(
        ctf, filtered.astype(jnp.bfloat16), (((0,), (0,)), ((), ())),
        preferred_element_type=jnp.float32,
    ).astype(jnp.bfloat16)
    weighted = jnp.dot(reverse, ctf, preferred_element_type=jnp.float32).astype(jnp.bfloat16)
    weighted_ref[0, 0] = weighted

    @pl.when(k == 0)
    def _():
        return_ref[...] = jnp.zeros_like(return_ref)

    bottom_rows = weighted[pixels - OVL :].astype(jnp.float32)
    top_rows = weighted[:OVL].astype(jnp.float32)

    def give_back(q, carry):
        return_ref[q, 0, 0] = return_ref[q, 0, 0] + back_ref[0, k, q] * bottom_rows
        return_ref[q, 1, 0] = return_ref[q, 1, 0] + back_ref[1, k, q] * top_rows
        return carry

    lax.fori_loop(0, total, give_back, 0)


def middle(fwd, back, images, projected, edges_all, ctf_filter):
    own_count, tilt_count, pixels, _ = images.shape
    total = edges_all.shape[0]
    tile = pl.BlockSpec((1, 1, pixels, pixels), lambda t, k: (k, t, 0, 0))
    bands = pl.BlockSpec((total, 2, 1, OVL, pixels), lambda t, k: (0, 0, t, 0, 0))
    smem = pl.BlockSpec(memory_space=pltpu.SMEM)
    flops = own_count * tilt_count * (8 * pixels**3 + 8 * total * OVL * pixels)
    moved = 2 * images.size * 3 + 2 * edges_all.size + 4 * edges_all.size + 2 * ctf_filter.size
    return pl.pallas_call(
        middle_kernel,
        grid=(tilt_count, own_count),
        in_specs=[
            smem,
            smem,
            tile,
            tile,
            bands,
            pl.BlockSpec((1, pixels, pixels), lambda t, k: (t, 0, 0)),
        ],
        out_specs=[
            tile,
            pl.BlockSpec((1, 1, 8, 128), lambda t, k: (t, k, 0, 0)),
            bands,
        ],
        out_shape=[
            jax.ShapeDtypeStruct(images.shape, jnp.bfloat16),
            jax.ShapeDtypeStruct((tilt_count, own_count, 8, 128), jnp.float32),
            jax.ShapeDtypeStruct(edges_all.shape, jnp.float32),
        ],
        scratch_shapes=[pltpu.VMEM((pixels, pixels), jnp.float32)],
        compiler_params=pltpu.CompilerParams(
            dimension_semantics=("arbitrary", "arbitrary")
        ),
        cost_estimate=pl.CostEstimate(flops=flops, transcendentals=0, bytes_accessed=moved),
    )(fwd, back, images, projected, edges_all, ctf_filter)


def on_device(
    sections, images, slice_rows, slice_cols, ctf_filter, nbr_owner, nbr_local, nbr_side, nbr_weight
):
    own_count = sections.shape[0]
    pixels = sections.shape[1]
    tilt_count = images.shape[1]
    neighbours = nbr_local.shape[1]
    peer_count = lax.axis_size("dom")
    total = own_count * peer_count
    me = lax.axis_index("dom")
    band_size = tilt_count * OVL * pixels

    steps = peer_count.bit_length() - 1
    relative = nbr_owner.reshape(own_count, neighbours) ^ me
    flipped = sum(((relative >> (steps - 1 - b)) & 1) << b for b in range(steps))
    every = jnp.arange(total)

    def weights_for(blocks, side):
        hits = (blocks * own_count + nbr_local)[:, :, None] == every[None, None, :]
        hits = hits & (nbr_side == side)[:, :, None]
        return jnp.sum(jnp.where(hits, nbr_weight[:, :, None], 0.0), axis=1)

    fwd = [weights_for(flipped, s) for s in (0, 1)]
    back = [weights_for(relative, s) for s in (0, 1)]

    halfway = jnp.einsum(
        "kij,tlj->ktil", sections, slice_cols, preferred_element_type=jnp.float32
    ).astype(jnp.bfloat16)
    projected = jnp.einsum(
        "tai,ktil->ktal", slice_rows, halfway, preferred_element_type=jnp.float32
    ).astype(jnp.bfloat16)
    edges = jnp.stack((projected[:, :, :OVL], projected[:, :, pixels - OVL :]), axis=1)
    edges_all = edges
    for b in range(steps):
        stride = peer_count >> (b + 1)
        pairs = [(i, i ^ stride) for i in range(peer_count)]
        edges_all = jnp.concatenate((edges_all, lax.ppermute(edges_all, "dom", pairs)), axis=0)

    weighted, score_tiles, returned = middle(
        jnp.stack(fwd), jnp.stack(back), images, projected, edges_all, ctf_filter
    )
    score_part = jnp.sum(score_tiles[:, :, 0, 0], axis=0)
    tilt_groups = lax.axis_size("tilt")

    returned = returned.reshape((2,) * steps + (own_count,) + returned.shape[1:])
    for b in range(steps):
        stride = 1 << b
        pairs = [(i, i ^ stride) for i in range(peer_count)]
        axis = steps - 1 - b
        kept = lax.index_in_dim(returned, 0, axis, keepdims=False)
        given = lax.index_in_dim(returned, 1, axis, keepdims=False).astype(jnp.bfloat16)
        returned = kept + lax.ppermute(given, "dom", pairs).astype(jnp.float32)
    add_top = returned[:, 0]
    add_bottom = returned[:, 1]

    proj_grad = weighted.astype(jnp.float32)
    proj_grad = proj_grad.at[:, :, :OVL].add(add_top)
    proj_grad = proj_grad.at[:, :, pixels - OVL :].add(add_bottom)
    proj_half = proj_grad.astype(jnp.bfloat16)
    upward = jnp.einsum(
        "tai,ktal->ktil", slice_rows, proj_half, preferred_element_type=jnp.float32
    ).astype(jnp.bfloat16)
    partial_grad = -jnp.einsum(
        "ktil,tlj->kij", upward, slice_cols, preferred_element_type=jnp.float32
    )
    scale = 0.5 / (tilt_count * tilt_groups * pixels * pixels)
    if tilt_groups != 2:
        scores = scale * lax.psum(score_part, "tilt")
        section_grad = lax.psum_scatter(partial_grad, "tilt", scatter_dimension=1, tiled=True)
        return (section_grad, scores)
    half = pixels // 2
    side = lax.axis_index("tilt")
    kept = lax.dynamic_slice_in_dim(partial_grad, side * half, half, axis=1)
    given = lax.dynamic_slice_in_dim(partial_grad, (1 - side) * half, half, axis=1)
    score_hi = score_part.astype(jnp.bfloat16)
    score_rest = score_part - score_hi.astype(jnp.float32)
    score_mid = score_rest.astype(jnp.bfloat16)
    score_low = (score_rest - score_mid.astype(jnp.float32)).astype(jnp.bfloat16)
    parcel = jnp.concatenate(
        (given.reshape(-1).astype(jnp.bfloat16), score_hi, score_mid, score_low)
    )
    parcel = lax.ppermute(parcel, "tilt", [(0, 1), (1, 0)]).astype(jnp.float32)
    section_grad = kept + parcel[: given.size].reshape(given.shape)
    parts = parcel[given.size :].reshape(3, own_count)
    scores = scale * (score_part + (parts[0] + (parts[1] + parts[2])))
    return (section_grad, scores)


def solution(mesh):
    in_specs = (
        P("dom", None, None),
        P("dom", "tilt", None, None),
        P("tilt", None, None),
        P("tilt", None, None),
        P("tilt", None, None),
        P("dom", None, None),
        P("dom", None),
        P("dom", None),
        P("dom", None),
    )
    out_specs = (P("dom", "tilt", None), P("dom"))
    return jax.shard_map(
        on_device, mesh=mesh, in_specs=in_specs, out_specs=out_specs, check_vma=False
    )
```

```python
import jax
import jax.numpy as jnp
from jax import lax
from jax.experimental import pallas as pl
from jax.experimental.pallas import tpu as pltpu
from jax.sharding import PartitionSpec as P

OVL = 16


def split_dot(weights, bands):
    hi = weights.astype(jnp.bfloat16)
    rest = weights - hi.astype(jnp.float32)
    mid = rest.astype(jnp.bfloat16)
    low = (rest - mid.astype(jnp.float32)).astype(jnp.bfloat16)
    total = jnp.dot(hi, bands, preferred_element_type=jnp.float32)
    total = total + jnp.dot(mid, bands, preferred_element_type=jnp.float32)
    return total + jnp.dot(low, bands, preferred_element_type=jnp.float32)


def middle_kernel(
    fwd_ref, back_ref, image_ref, proj_ref, edge_ref, ctf_ref,
    weighted_ref, score_ref, return_ref, residual_ref,
):
    k = pl.program_id(1)
    total = edge_ref.shape[0]
    pixels = image_ref.shape[-1]

    def band_sum(q, carry):
        lower, upper = carry
        lower = lower + fwd_ref[0, k, q] * edge_ref[q, 0, 0].astype(jnp.float32)
        upper = upper + fwd_ref[1, k, q] * edge_ref[q, 1, 0].astype(jnp.float32)
        return lower, upper

    zero = jnp.zeros((OVL, pixels), jnp.float32)
    lower, upper = lax.fori_loop(0, total, band_sum, (zero, zero), unroll=8)
    residual_ref[...] = image_ref[0, 0].astype(jnp.float32) - proj_ref[0, 0].astype(jnp.float32)
    residual_ref[:OVL] = residual_ref[:OVL] - upper
    residual_ref[pixels - OVL :] = residual_ref[pixels - OVL :] - lower
    residual = residual_ref[...].astype(jnp.bfloat16)
    ctf = ctf_ref[0]
    smoothed = jnp.dot(ctf, residual, preferred_element_type=jnp.float32).astype(jnp.bfloat16)
    filtered = lax.dot_general(
        smoothed, ctf, (((1,), (1,)), ((), ())), preferred_element_type=jnp.float32
    )
    score_ref[...] = jnp.full(score_ref.shape, jnp.sum(filtered * filtered), jnp.float32)
    reverse = lax.dot_general(
        ctf, filtered.astype(jnp.bfloat16), (((0,), (0,)), ((), ())),
        preferred_element_type=jnp.float32,
    ).astype(jnp.bfloat16)
    weighted = jnp.dot(reverse, ctf, preferred_element_type=jnp.float32).astype(jnp.bfloat16)
    weighted_ref[0, 0] = weighted

    @pl.when(k == 0)
    def _():
        return_ref[...] = jnp.zeros_like(return_ref)

    bottom_rows = weighted[pixels - OVL :].astype(jnp.float32)
    top_rows = weighted[:OVL].astype(jnp.float32)

    def give_back(q, carry):
        return_ref[q, 0, 0] = return_ref[q, 0, 0] + back_ref[0, k, q] * bottom_rows
        return_ref[q, 1, 0] = return_ref[q, 1, 0] + back_ref[1, k, q] * top_rows
        return carry

    lax.fori_loop(0, total, give_back, 0, unroll=8)


def middle(fwd, back, images, projected, edges_all, ctf_filter):
    own_count, tilt_count, pixels, _ = images.shape
    total = edges_all.shape[0]
    tile = pl.BlockSpec((1, 1, pixels, pixels), lambda t, k: (k, t, 0, 0))
    bands = pl.BlockSpec((total, 2, 1, OVL, pixels), lambda t, k: (0, 0, t, 0, 0))
    smem = pl.BlockSpec(memory_space=pltpu.SMEM)
    flops = own_count * tilt_count * (8 * pixels**3 + 8 * total * OVL * pixels)
    moved = 2 * images.size * 3 + 2 * edges_all.size + 4 * edges_all.size + 2 * ctf_filter.size
    return pl.pallas_call(
        middle_kernel,
        grid=(tilt_count, own_count),
        in_specs=[
            smem,
            smem,
            tile,
            tile,
            bands,
            pl.BlockSpec((1, pixels, pixels), lambda t, k: (t, 0, 0)),
        ],
        out_specs=[
            tile,
            pl.BlockSpec((1, 1, 8, 128), lambda t, k: (t, k, 0, 0)),
            bands,
        ],
        out_shape=[
            jax.ShapeDtypeStruct(images.shape, jnp.bfloat16),
            jax.ShapeDtypeStruct((tilt_count, own_count, 8, 128), jnp.float32),
            jax.ShapeDtypeStruct(edges_all.shape, jnp.float32),
        ],
        scratch_shapes=[pltpu.VMEM((pixels, pixels), jnp.float32)],
        compiler_params=pltpu.CompilerParams(
            dimension_semantics=("arbitrary", "arbitrary")
        ),
        cost_estimate=pl.CostEstimate(flops=flops, transcendentals=0, bytes_accessed=moved),
    )(fwd, back, images, projected, edges_all, ctf_filter)


def on_device(
    sections, images, slice_rows, slice_cols, ctf_filter, nbr_owner, nbr_local, nbr_side, nbr_weight
):
    own_count = sections.shape[0]
    pixels = sections.shape[1]
    tilt_count = images.shape[1]
    neighbours = nbr_local.shape[1]
    peer_count = lax.axis_size("dom")
    total = own_count * peer_count
    me = lax.axis_index("dom")
    band_size = tilt_count * OVL * pixels

    steps = peer_count.bit_length() - 1
    relative = nbr_owner.reshape(own_count, neighbours) ^ me
    flipped = sum(((relative >> (steps - 1 - b)) & 1) << b for b in range(steps))
    every = jnp.arange(total)

    def weights_for(blocks, side):
        hits = (blocks * own_count + nbr_local)[:, :, None] == every[None, None, :]
        hits = hits & (nbr_side == side)[:, :, None]
        return jnp.sum(jnp.where(hits, nbr_weight[:, :, None], 0.0), axis=1)

    fwd = [weights_for(flipped, s) for s in (0, 1)]

    halfway = jnp.einsum(
        "kij,tlj->ktil", sections, slice_cols, preferred_element_type=jnp.float32
    ).astype(jnp.bfloat16)
    projected = jnp.einsum(
        "tai,ktil->ktal", slice_rows, halfway, preferred_element_type=jnp.float32
    ).astype(jnp.bfloat16)
    edges = jnp.stack((projected[:, :, :OVL], projected[:, :, pixels - OVL :]), axis=1)
    edges_all = edges
    for b in range(steps):
        stride = peer_count >> (b + 1)
        pairs = [(i, i ^ stride) for i in range(peer_count)]
        edges_all = jnp.concatenate((edges_all, lax.ppermute(edges_all, "dom", pairs)), axis=0)

    weighted, score_tiles, returned = middle(
        jnp.stack(fwd), jnp.stack(fwd), images, projected, edges_all, ctf_filter
    )
    score_part = jnp.sum(score_tiles[:, :, 0, 0], axis=0)
    tilt_groups = lax.axis_size("tilt")

    for b in range(steps):
        stride = 1 << b
        pairs = [(i, i ^ stride) for i in range(peer_count)]
        half = returned.shape[0] // 2
        given = returned[half:].astype(jnp.bfloat16)
        returned = returned[:half] + lax.ppermute(given, "dom", pairs).astype(jnp.float32)
    add_top = returned[:, 0]
    add_bottom = returned[:, 1]

    proj_grad = weighted.astype(jnp.float32)
    proj_grad = proj_grad.at[:, :, :OVL].add(add_top)
    proj_grad = proj_grad.at[:, :, pixels - OVL :].add(add_bottom)
    proj_half = proj_grad.astype(jnp.bfloat16)
    upward = jnp.einsum(
        "tai,ktal->ktil", slice_rows, proj_half, preferred_element_type=jnp.float32
    ).astype(jnp.bfloat16)
    partial_grad = -jnp.einsum(
        "ktil,tlj->kij", upward, slice_cols, preferred_element_type=jnp.float32
    )
    scale = 0.5 / (tilt_count * tilt_groups * pixels * pixels)
    if tilt_groups != 2:
        scores = scale * lax.psum(score_part, "tilt")
        section_grad = lax.psum_scatter(partial_grad, "tilt", scatter_dimension=1, tiled=True)
        return (section_grad, scores)
    half = pixels // 2
    side = lax.axis_index("tilt")
    kept = lax.dynamic_slice_in_dim(partial_grad, side * half, half, axis=1)
    given = lax.dynamic_slice_in_dim(partial_grad, (1 - side) * half, half, axis=1)
    score_hi = score_part.astype(jnp.bfloat16)
    score_rest = score_part - score_hi.astype(jnp.float32)
    score_mid = score_rest.astype(jnp.bfloat16)
    score_low = (score_rest - score_mid.astype(jnp.float32)).astype(jnp.bfloat16)
    parcel = jnp.concatenate(
        (given.reshape(-1).astype(jnp.bfloat16), score_hi, score_mid, score_low)
    )
    parcel = lax.ppermute(parcel, "tilt", [(0, 1), (1, 0)]).astype(jnp.float32)
    section_grad = kept + parcel[: given.size].reshape(given.shape)
    parts = parcel[given.size :].reshape(3, own_count)
    scores = scale * (score_part + (parts[0] + (parts[1] + parts[2])))
    return (section_grad, scores)


def solution(mesh):
    in_specs = (
        P("dom", None, None),
        P("dom", "tilt", None, None),
        P("tilt", None, None),
        P("tilt", None, None),
        P("tilt", None, None),
        P("dom", None, None),
        P("dom", None),
        P("dom", None),
        P("dom", None),
    )
    out_specs = (P("dom", "tilt", None), P("dom"))
    return jax.shard_map(
        on_device, mesh=mesh, in_specs=in_specs, out_specs=out_specs, check_vma=False
    )
```

```python
import jax
import jax.numpy as jnp
from jax import lax
from jax.experimental import pallas as pl
from jax.experimental.pallas import tpu as pltpu
from jax.sharding import PartitionSpec as P

OVL = 16


def middle_kernel(
    place_ref, side_ref, weight_ref, image_ref, proj_ref, edge_ref, ctf_ref,
    weighted_ref, score_ref, kept_ref, sent_ref, residual_ref,
):
    k = pl.program_id(1)
    neighbours = place_ref.shape[1]
    half = kept_ref.shape[0]
    pixels = image_ref.shape[-1]

    def band_sum(j, carry):
        lower, upper = carry
        q = place_ref[k, j]
        s = side_ref[k, j]
        w = weight_ref[k, j]
        band = edge_ref[q, s, 0].astype(jnp.float32)
        lower = lower + jnp.where(s == 0, w, 0.0) * band
        upper = upper + jnp.where(s == 1, w, 0.0) * band
        return lower, upper

    zero = jnp.zeros((OVL, pixels), jnp.float32)
    lower, upper = lax.fori_loop(0, neighbours, band_sum, (zero, zero), unroll=True)
    residual_ref[...] = image_ref[0, 0].astype(jnp.float32) - proj_ref[0, 0].astype(jnp.float32)
    residual_ref[:OVL] = residual_ref[:OVL] - upper
    residual_ref[pixels - OVL :] = residual_ref[pixels - OVL :] - lower
    residual = residual_ref[...].astype(jnp.bfloat16)
    ctf = ctf_ref[0]
    smoothed = jnp.dot(ctf, residual, preferred_element_type=jnp.float32).astype(jnp.bfloat16)
    filtered = lax.dot_general(
        smoothed, ctf, (((1,), (1,)), ((), ())), preferred_element_type=jnp.float32
    )
    score_ref[...] = jnp.full(score_ref.shape, jnp.sum(filtered * filtered), jnp.float32)
    reverse = lax.dot_general(
        ctf, filtered.astype(jnp.bfloat16), (((0,), (0,)), ((), ())),
        preferred_element_type=jnp.float32,
    ).astype(jnp.bfloat16)
    weighted = jnp.dot(reverse, ctf, preferred_element_type=jnp.float32).astype(jnp.bfloat16)
    weighted_ref[0, 0] = weighted

    @pl.when(k == 0)
    def _():
        kept_ref[...] = jnp.zeros_like(kept_ref)
        sent_ref[...] = jnp.zeros_like(sent_ref)

    bottom_rows = weighted[pixels - OVL :].astype(jnp.float32)
    top_rows = weighted[:OVL].astype(jnp.float32)

    def give_back(j, carry):
        q = place_ref[k, j]
        s = side_ref[k, j]
        rows = jnp.where(s == 0, bottom_rows, top_rows)
        part = (weight_ref[k, j] * rows).astype(jnp.bfloat16).astype(jnp.float32)

        @pl.when(q < half)
        def _():
            kept_ref[q, s, 0] = kept_ref[q, s, 0] + part

        @pl.when(q >= half)
        def _():
            sent_ref[q - half, s, 0] = sent_ref[q - half, s, 0] + part

        return carry

    lax.fori_loop(0, neighbours, give_back, 0, unroll=True)


def middle(place, side, weight, images, projected, edges_all, ctf_filter):
    own_count, tilt_count, pixels, _ = images.shape
    total = edges_all.shape[0]
    half = total // 2
    tile = pl.BlockSpec((1, 1, pixels, pixels), lambda t, k: (k, t, 0, 0))
    bands = pl.BlockSpec((total, 2, 1, OVL, pixels), lambda t, k: (0, 0, t, 0, 0))
    halves = pl.BlockSpec((half, 2, 1, OVL, pixels), lambda t, k: (0, 0, t, 0, 0))
    smem = pl.BlockSpec(memory_space=pltpu.SMEM)
    flops = own_count * tilt_count * 8 * pixels**3
    moved = 2 * images.size * 3 + 2 * edges_all.size + 4 * edges_all.size + 2 * ctf_filter.size
    return pl.pallas_call(
        middle_kernel,
        grid=(tilt_count, own_count),
        in_specs=[
            smem,
            smem,
            smem,
            tile,
            tile,
            bands,
            pl.BlockSpec((1, pixels, pixels), lambda t, k: (t, 0, 0)),
        ],
        out_specs=[
            tile,
            pl.BlockSpec((1, 1, 8, 128), lambda t, k: (t, k, 0, 0)),
            halves,
            halves,
        ],
        out_shape=[
            jax.ShapeDtypeStruct(images.shape, jnp.bfloat16),
            jax.ShapeDtypeStruct((tilt_count, own_count, 8, 128), jnp.float32),
            jax.ShapeDtypeStruct((half,) + edges_all.shape[1:], jnp.float32),
            jax.ShapeDtypeStruct((half,) + edges_all.shape[1:], jnp.float32),
        ],
        scratch_shapes=[pltpu.VMEM((pixels, pixels), jnp.float32)],
        compiler_params=pltpu.CompilerParams(
            dimension_semantics=("arbitrary", "arbitrary")
        ),
        cost_estimate=pl.CostEstimate(flops=flops, transcendentals=0, bytes_accessed=moved),
    )(place, side, weight, images, projected, edges_all, ctf_filter)


def on_device(
    sections, images, slice_rows, slice_cols, ctf_filter, nbr_owner, nbr_local, nbr_side, nbr_weight
):
    own_count = sections.shape[0]
    pixels = sections.shape[1]
    tilt_count = images.shape[1]
    neighbours = nbr_local.shape[1]
    peer_count = lax.axis_size("dom")
    total = own_count * peer_count
    me = lax.axis_index("dom")
    band_size = tilt_count * OVL * pixels

    steps = peer_count.bit_length() - 1
    relative = nbr_owner.reshape(own_count, neighbours) ^ me
    flipped = sum(((relative >> (steps - 1 - b)) & 1) << b for b in range(steps))
    place = flipped * own_count + nbr_local

    halfway = jnp.einsum(
        "kij,tlj->ktil", sections, slice_cols, preferred_element_type=jnp.float32
    ).astype(jnp.bfloat16)
    projected = jnp.einsum(
        "tai,ktil->ktal", slice_rows, halfway, preferred_element_type=jnp.float32
    ).astype(jnp.bfloat16)
    edges = jnp.stack((projected[:, :, :OVL], projected[:, :, pixels - OVL :]), axis=1)
    edges_all = edges
    for b in range(steps):
        stride = peer_count >> (b + 1)
        pairs = [(i, i ^ stride) for i in range(peer_count)]
        edges_all = jnp.concatenate((edges_all, lax.ppermute(edges_all, "dom", pairs)), axis=0)

    weighted, score_tiles, kept_half, sent_half = middle(
        place, nbr_side, nbr_weight, images, projected, edges_all, ctf_filter
    )
    score_part = jnp.sum(score_tiles[:, :, 0, 0], axis=0)
    tilt_groups = lax.axis_size("tilt")

    pairs = [(i, i ^ 1) for i in range(peer_count)]
    returned = kept_half + lax.ppermute(sent_half.astype(jnp.bfloat16), "dom", pairs).astype(
        jnp.float32
    )
    for b in range(1, steps):
        stride = 1 << b
        pairs = [(i, i ^ stride) for i in range(peer_count)]
        half = returned.shape[0] // 2
        given = returned[half:].astype(jnp.bfloat16)
        returned = returned[:half] + lax.ppermute(given, "dom", pairs).astype(jnp.float32)
    add_top = returned[:, 0]
    add_bottom = returned[:, 1]

    proj_grad = weighted.astype(jnp.float32)
    proj_grad = proj_grad.at[:, :, :OVL].add(add_top)
    proj_grad = proj_grad.at[:, :, pixels - OVL :].add(add_bottom)
    proj_half = proj_grad.astype(jnp.bfloat16)
    upward = jnp.einsum(
        "tai,ktal->ktil", slice_rows, proj_half, preferred_element_type=jnp.float32
    ).astype(jnp.bfloat16)
    partial_grad = -jnp.einsum(
        "ktil,tlj->kij", upward, slice_cols, preferred_element_type=jnp.float32
    )
    scale = 0.5 / (tilt_count * tilt_groups * pixels * pixels)
    if tilt_groups != 2:
        scores = scale * lax.psum(score_part, "tilt")
        section_grad = lax.psum_scatter(partial_grad, "tilt", scatter_dimension=1, tiled=True)
        return (section_grad, scores)
    half = pixels // 2
    side = lax.axis_index("tilt")
    kept = lax.dynamic_slice_in_dim(partial_grad, side * half, half, axis=1)
    given = lax.dynamic_slice_in_dim(partial_grad, (1 - side) * half, half, axis=1)
    score_hi = score_part.astype(jnp.bfloat16)
    score_rest = score_part - score_hi.astype(jnp.float32)
    score_mid = score_rest.astype(jnp.bfloat16)
    score_low = (score_rest - score_mid.astype(jnp.float32)).astype(jnp.bfloat16)
    parcel = jnp.concatenate(
        (given.reshape(-1).astype(jnp.bfloat16), score_hi, score_mid, score_low)
    )
    parcel = lax.ppermute(parcel, "tilt", [(0, 1), (1, 0)]).astype(jnp.float32)
    section_grad = kept + parcel[: given.size].reshape(given.shape)
    parts = parcel[given.size :].reshape(3, own_count)
    scores = scale * (score_part + (parts[0] + (parts[1] + parts[2])))
    return (section_grad, scores)


def solution(mesh):
    in_specs = (
        P("dom", None, None),
        P("dom", "tilt", None, None),
        P("tilt", None, None),
        P("tilt", None, None),
        P("tilt", None, None),
        P("dom", None, None),
        P("dom", None),
        P("dom", None),
        P("dom", None),
    )
    out_specs = (P("dom", "tilt", None), P("dom"))
    return jax.shard_map(
        on_device, mesh=mesh, in_specs=in_specs, out_specs=out_specs, check_vma=False
    )
```

```python
import jax
import jax.numpy as jnp
from jax import lax
from jax.experimental import pallas as pl
from jax.experimental.pallas import tpu as pltpu
from jax.sharding import PartitionSpec as P

OVL = 16


def middle_kernel(
    place_ref, side_ref, weight_ref, image_ref, proj_ref, edge_ref, ctf_ref,
    weighted_ref, score_ref, kept_ref, sent_ref, residual_ref, return_ref,
):
    own_count, neighbours = place_ref.shape
    half = kept_ref.shape[0]
    pixels = image_ref.shape[-1]
    ctf = ctf_ref[0]
    zero = jnp.zeros((OVL, pixels), jnp.float32)
    edge_rows = []
    for k in range(own_count):

        def band_sum(j, carry, k=k):
            lower, upper = carry
            q = place_ref[k, j]
            s = side_ref[k, j]
            w = weight_ref[k, j]
            band = edge_ref[q, s, 0].astype(jnp.float32)
            lower = lower + jnp.where(s == 0, w, 0.0) * band
            upper = upper + jnp.where(s == 1, w, 0.0) * band
            return lower, upper

        lower, upper = lax.fori_loop(0, neighbours, band_sum, (zero, zero), unroll=True)
        residual_ref[k] = image_ref[k, 0].astype(jnp.float32) - proj_ref[k, 0].astype(jnp.float32)
        residual_ref[k, :OVL] = residual_ref[k, :OVL] - upper
        residual_ref[k, pixels - OVL :] = residual_ref[k, pixels - OVL :] - lower
        residual = residual_ref[k].astype(jnp.bfloat16)
        smoothed = jnp.dot(ctf, residual, preferred_element_type=jnp.float32).astype(jnp.bfloat16)
        filtered = lax.dot_general(
            smoothed, ctf, (((1,), (1,)), ((), ())), preferred_element_type=jnp.float32
        )
        score_ref[0, k] = jnp.full(score_ref.shape[2:], jnp.sum(filtered * filtered), jnp.float32)
        reverse = lax.dot_general(
            ctf, filtered.astype(jnp.bfloat16), (((0,), (0,)), ((), ())),
            preferred_element_type=jnp.float32,
        ).astype(jnp.bfloat16)
        weighted = jnp.dot(reverse, ctf, preferred_element_type=jnp.float32).astype(jnp.bfloat16)
        weighted_ref[k, 0] = weighted
        edge_rows.append(
            (weighted[pixels - OVL :].astype(jnp.float32), weighted[:OVL].astype(jnp.float32))
        )

    return_ref[...] = jnp.zeros_like(return_ref)
    for k in range(own_count):
        bottom_rows, top_rows = edge_rows[k]

        def give_back(j, carry, k=k, bottom_rows=bottom_rows, top_rows=top_rows):
            q = place_ref[k, j]
            s = side_ref[k, j]
            rows = jnp.where(s == 0, bottom_rows, top_rows)
            part = (weight_ref[k, j] * rows).astype(jnp.bfloat16).astype(jnp.float32)
            return_ref[q, s] = return_ref[q, s] + part
            return carry

        lax.fori_loop(0, neighbours, give_back, 0, unroll=True)
    kept_ref[:, :, 0] = return_ref[:half]
    sent_ref[:, :, 0] = return_ref[half:].astype(jnp.bfloat16)


def middle(place, side, weight, images, projected, edges_all, ctf_filter):
    own_count, tilt_count, pixels, _ = images.shape
    total = edges_all.shape[0]
    half = total // 2
    tiles = pl.BlockSpec((own_count, 1, pixels, pixels), lambda t: (0, t, 0, 0))
    bands = pl.BlockSpec((total, 2, 1, OVL, pixels), lambda t: (0, 0, t, 0, 0))
    halves = pl.BlockSpec((half, 2, 1, OVL, pixels), lambda t: (0, 0, t, 0, 0))
    smem = pl.BlockSpec(memory_space=pltpu.SMEM)
    flops = own_count * tilt_count * 8 * pixels**3
    moved = 2 * images.size * 3 + 2 * edges_all.size + 3 * edges_all.size + 2 * ctf_filter.size
    return pl.pallas_call(
        middle_kernel,
        grid=(tilt_count,),
        in_specs=[
            smem,
            smem,
            smem,
            tiles,
            tiles,
            bands,
            pl.BlockSpec((1, pixels, pixels), lambda t: (t, 0, 0)),
        ],
        out_specs=[
            tiles,
            pl.BlockSpec((1, own_count, 8, 128), lambda t: (t, 0, 0, 0)),
            halves,
            halves,
        ],
        out_shape=[
            jax.ShapeDtypeStruct(images.shape, jnp.bfloat16),
            jax.ShapeDtypeStruct((tilt_count, own_count, 8, 128), jnp.float32),
            jax.ShapeDtypeStruct((half,) + edges_all.shape[1:], jnp.float32),
            jax.ShapeDtypeStruct((half,) + edges_all.shape[1:], jnp.bfloat16),
        ],
        scratch_shapes=[
            pltpu.VMEM((own_count, pixels, pixels), jnp.float32),
            pltpu.VMEM((total, 2, OVL, pixels), jnp.float32),
        ],
        compiler_params=pltpu.CompilerParams(dimension_semantics=("arbitrary",)),
        cost_estimate=pl.CostEstimate(flops=flops, transcendentals=0, bytes_accessed=moved),
    )(place, side, weight, images, projected, edges_all, ctf_filter)


def on_device(
    sections, images, slice_rows, slice_cols, ctf_filter, nbr_owner, nbr_local, nbr_side, nbr_weight
):
    own_count = sections.shape[0]
    pixels = sections.shape[1]
    tilt_count = images.shape[1]
    neighbours = nbr_local.shape[1]
    peer_count = lax.axis_size("dom")
    total = own_count * peer_count
    me = lax.axis_index("dom")
    band_size = tilt_count * OVL * pixels

    steps = peer_count.bit_length() - 1
    relative = nbr_owner.reshape(own_count, neighbours) ^ me
    flipped = sum(((relative >> (steps - 1 - b)) & 1) << b for b in range(steps))
    place = flipped * own_count + nbr_local

    halfway = jnp.einsum(
        "kij,tlj->ktil", sections, slice_cols, preferred_element_type=jnp.float32
    ).astype(jnp.bfloat16)
    projected = jnp.einsum(
        "tai,ktil->ktal", slice_rows, halfway, preferred_element_type=jnp.float32
    ).astype(jnp.bfloat16)
    edges = jnp.stack((projected[:, :, :OVL], projected[:, :, pixels - OVL :]), axis=1)
    edges_all = edges
    for b in range(steps):
        stride = peer_count >> (b + 1)
        pairs = [(i, i ^ stride) for i in range(peer_count)]
        edges_all = jnp.concatenate((edges_all, lax.ppermute(edges_all, "dom", pairs)), axis=0)

    weighted, score_tiles, kept_half, sent_half = middle(
        place, nbr_side, nbr_weight, images, projected, edges_all, ctf_filter
    )
    score_part = jnp.sum(score_tiles[:, :, 0, 0], axis=0)
    tilt_groups = lax.axis_size("tilt")

    pairs = [(i, i ^ 1) for i in range(peer_count)]
    returned = kept_half + lax.ppermute(sent_half, "dom", pairs).astype(jnp.float32)
    for b in range(1, steps):
        stride = 1 << b
        pairs = [(i, i ^ stride) for i in range(peer_count)]
        half = returned.shape[0] // 2
        given = returned[half:].astype(jnp.bfloat16)
        returned = returned[:half] + lax.ppermute(given, "dom", pairs).astype(jnp.float32)
    add_top = returned[:, 0]
    add_bottom = returned[:, 1]

    proj_grad = weighted.astype(jnp.float32)
    proj_grad = proj_grad.at[:, :, :OVL].add(add_top)
    proj_grad = proj_grad.at[:, :, pixels - OVL :].add(add_bottom)
    proj_half = proj_grad.astype(jnp.bfloat16)
    upward = jnp.einsum(
        "tai,ktal->ktil", slice_rows, proj_half, preferred_element_type=jnp.float32
    ).astype(jnp.bfloat16)
    partial_grad = -jnp.einsum(
        "ktil,tlj->kij", upward, slice_cols, preferred_element_type=jnp.float32
    )
    scale = 0.5 / (tilt_count * tilt_groups * pixels * pixels)
    if tilt_groups != 2:
        scores = scale * lax.psum(score_part, "tilt")
        section_grad = lax.psum_scatter(partial_grad, "tilt", scatter_dimension=1, tiled=True)
        return (section_grad, scores)
    half = pixels // 2
    side = lax.axis_index("tilt")
    kept = lax.dynamic_slice_in_dim(partial_grad, side * half, half, axis=1)
    given = lax.dynamic_slice_in_dim(partial_grad, (1 - side) * half, half, axis=1)
    score_hi = score_part.astype(jnp.bfloat16)
    score_rest = score_part - score_hi.astype(jnp.float32)
    score_mid = score_rest.astype(jnp.bfloat16)
    score_low = (score_rest - score_mid.astype(jnp.float32)).astype(jnp.bfloat16)
    parcel = jnp.concatenate(
        (given.reshape(-1).astype(jnp.bfloat16), score_hi, score_mid, score_low)
    )
    parcel = lax.ppermute(parcel, "tilt", [(0, 1), (1, 0)]).astype(jnp.float32)
    section_grad = kept + parcel[: given.size].reshape(given.shape)
    parts = parcel[given.size :].reshape(3, own_count)
    scores = scale * (score_part + (parts[0] + (parts[1] + parts[2])))
    return (section_grad, scores)


def solution(mesh):
    in_specs = (
        P("dom", None, None),
        P("dom", "tilt", None, None),
        P("tilt", None, None),
        P("tilt", None, None),
        P("tilt", None, None),
        P("dom", None, None),
        P("dom", None),
        P("dom", None),
        P("dom", None),
    )
    out_specs = (P("dom", "tilt", None), P("dom"))
    return jax.shard_map(
        on_device, mesh=mesh, in_specs=in_specs, out_specs=out_specs, check_vma=False
    )
```

```python
import jax
import jax.numpy as jnp
from jax import lax
from jax.experimental import pallas as pl
from jax.experimental.pallas import tpu as pltpu
from jax.sharding import PartitionSpec as P

OVL = 16


def middle_kernel(
    place_ref, side_ref, weight_ref, image_ref, proj_ref, edge_ref, ctf_ref,
    weighted_ref, score_ref, kept_ref, sent_ref, residual_ref, return_ref,
):
    own_count, neighbours = place_ref.shape
    half = kept_ref.shape[0]
    pixels = image_ref.shape[-1]
    ctf = ctf_ref[0]
    zero = jnp.zeros((OVL, pixels), jnp.float32)
    edge_rows = []
    for k in range(own_count):

        def band_sum(j, carry, k=k):
            lower, upper = carry
            q = place_ref[k, j]
            s = side_ref[k, j]
            w = weight_ref[k, j]
            band = edge_ref[q, s, 0].astype(jnp.float32)
            lower = lower + jnp.where(s == 0, w, 0.0) * band
            upper = upper + jnp.where(s == 1, w, 0.0) * band
            return lower, upper

        lower, upper = lax.fori_loop(0, neighbours, band_sum, (zero, zero), unroll=True)
        residual_ref[k] = image_ref[k, 0].astype(jnp.float32) - proj_ref[k, 0].astype(jnp.float32)
        residual_ref[k, :OVL] = residual_ref[k, :OVL] - upper
        residual_ref[k, pixels - OVL :] = residual_ref[k, pixels - OVL :] - lower
        residual = residual_ref[k].astype(jnp.bfloat16)
        smoothed = jnp.dot(ctf, residual, preferred_element_type=jnp.float32).astype(jnp.bfloat16)
        filtered = lax.dot_general(
            smoothed, ctf, (((1,), (1,)), ((), ())), preferred_element_type=jnp.float32
        )
        score_ref[0, k] = jnp.full(score_ref.shape[2:], jnp.sum(filtered * filtered), jnp.float32)
        reverse = lax.dot_general(
            ctf, filtered.astype(jnp.bfloat16), (((0,), (0,)), ((), ())),
            preferred_element_type=jnp.float32,
        ).astype(jnp.bfloat16)
        weighted = jnp.dot(reverse, ctf, preferred_element_type=jnp.float32).astype(jnp.bfloat16)
        weighted_ref[k, 0] = weighted
        edge_rows.append(
            (weighted[pixels - OVL :].astype(jnp.float32), weighted[:OVL].astype(jnp.float32))
        )

    return_ref[...] = jnp.zeros_like(return_ref)
    for k in range(own_count):
        bottom_rows, top_rows = edge_rows[k]

        def give_back(j, carry, k=k, bottom_rows=bottom_rows, top_rows=top_rows):
            q = place_ref[k, j]
            s = side_ref[k, j]
            rows = jnp.where(s == 0, bottom_rows, top_rows)
            part = (weight_ref[k, j] * rows).astype(jnp.bfloat16).astype(jnp.float32)
            return_ref[q, s] = return_ref[q, s] + part
            return carry

        lax.fori_loop(0, neighbours, give_back, 0, unroll=True)
    kept_ref[:, :, 0] = return_ref[:half]
    sent_ref[:, :, 0] = return_ref[half:].astype(jnp.bfloat16)


def middle(place, side, weight, images, projected, edges_all, ctf_filter):
    own_count, tilt_count, pixels, _ = images.shape
    total = edges_all.shape[0]
    half = total // 2
    tiles = pl.BlockSpec((own_count, 1, pixels, pixels), lambda t: (0, t, 0, 0))
    bands = pl.BlockSpec((total, 2, 1, OVL, pixels), lambda t: (0, 0, t, 0, 0))
    halves = pl.BlockSpec((half, 2, 1, OVL, pixels), lambda t: (0, 0, t, 0, 0))
    smem = pl.BlockSpec(memory_space=pltpu.SMEM)
    flops = own_count * tilt_count * 8 * pixels**3
    moved = 2 * images.size * 3 + 2 * edges_all.size + 3 * edges_all.size + 2 * ctf_filter.size
    return pl.pallas_call(
        middle_kernel,
        grid=(tilt_count,),
        in_specs=[
            smem,
            smem,
            smem,
            tiles,
            tiles,
            bands,
            pl.BlockSpec((1, pixels, pixels), lambda t: (t, 0, 0)),
        ],
        out_specs=[
            tiles,
            pl.BlockSpec((1, own_count, 8, 128), lambda t: (t, 0, 0, 0)),
            halves,
            halves,
        ],
        out_shape=[
            jax.ShapeDtypeStruct(images.shape, jnp.bfloat16),
            jax.ShapeDtypeStruct((tilt_count, own_count, 8, 128), jnp.float32),
            jax.ShapeDtypeStruct((half,) + edges_all.shape[1:], jnp.float32),
            jax.ShapeDtypeStruct((half,) + edges_all.shape[1:], jnp.bfloat16),
        ],
        scratch_shapes=[
            pltpu.VMEM((own_count, pixels, pixels), jnp.float32),
            pltpu.VMEM((total, 2, OVL, pixels), jnp.float32),
        ],
        compiler_params=pltpu.CompilerParams(dimension_semantics=("arbitrary",)),
        cost_estimate=pl.CostEstimate(flops=flops, transcendentals=0, bytes_accessed=moved),
    )(place, side, weight, images, projected, edges_all, ctf_filter)


def gather_stages(peer_count):
    steps = peer_count.bit_length() - 1
    strides = [peer_count >> (b + 1) for b in range(steps)]
    if steps <= 2:
        return [(stride,) for stride in strides]
    middle_strides = strides[1:-1]
    pairs = [tuple(middle_strides[i : i + 2]) for i in range(0, len(middle_strides), 2)]
    return [(strides[0],)] + pairs + [(strides[-1],)]


def on_device(
    sections, images, slice_rows, slice_cols, ctf_filter, nbr_owner, nbr_local, nbr_side, nbr_weight
):
    own_count = sections.shape[0]
    pixels = sections.shape[1]
    tilt_count = images.shape[1]
    neighbours = nbr_local.shape[1]
    peer_count = lax.axis_size("dom")
    total = own_count * peer_count
    me = lax.axis_index("dom")
    band_size = tilt_count * OVL * pixels

    steps = peer_count.bit_length() - 1
    relative = nbr_owner.reshape(own_count, neighbours) ^ me
    flipped = sum(((relative >> (steps - 1 - b)) & 1) << b for b in range(steps))
    place = flipped * own_count + nbr_local

    halfway = jnp.einsum(
        "kij,tlj->ktil", sections, slice_cols, preferred_element_type=jnp.float32
    ).astype(jnp.bfloat16)
    projected = jnp.einsum(
        "tai,ktil->ktal", slice_rows, halfway, preferred_element_type=jnp.float32
    ).astype(jnp.bfloat16)
    edges = jnp.stack((projected[:, :, :OVL], projected[:, :, pixels - OVL :]), axis=1)
    stages = gather_stages(peer_count)
    edges_all = edges
    for stage in stages:
        pieces = [edges_all]
        for g in range(1, 2 ** len(stage)):
            offset = sum(stride for i, stride in enumerate(stage) if (g >> i) & 1)
            pairs = [(i, i ^ offset) for i in range(peer_count)]
            pieces.append(lax.ppermute(edges_all, "dom", pairs))
        edges_all = jnp.concatenate(pieces, axis=0)

    weighted, score_tiles, kept_half, sent_half = middle(
        place, nbr_side, nbr_weight, images, projected, edges_all, ctf_filter
    )
    score_part = jnp.sum(score_tiles[:, :, 0, 0], axis=0)
    tilt_groups = lax.axis_size("tilt")

    pairs = [(i, i ^ 1) for i in range(peer_count)]
    returned = kept_half + lax.ppermute(sent_half, "dom", pairs).astype(jnp.float32)
    for stage in [tuple(reversed(stage)) for stage in reversed(stages[:-1])]:
        count = 2 ** len(stage)
        share = returned.shape[0] // count
        kept = returned[:share]
        for g in range(1, count):
            offset = sum(
                stride for i, stride in enumerate(stage) if (g >> (len(stage) - 1 - i)) & 1
            )
            pairs = [(i, i ^ offset) for i in range(peer_count)]
            given = returned[g * share : (g + 1) * share].astype(jnp.bfloat16)
            kept = kept + lax.ppermute(given, "dom", pairs).astype(jnp.float32)
        returned = kept
    add_top = returned[:, 0]
    add_bottom = returned[:, 1]

    proj_grad = weighted.astype(jnp.float32)
    proj_grad = proj_grad.at[:, :, :OVL].add(add_top)
    proj_grad = proj_grad.at[:, :, pixels - OVL :].add(add_bottom)
    proj_half = proj_grad.astype(jnp.bfloat16)
    upward = jnp.einsum(
        "tai,ktal->ktil", slice_rows, proj_half, preferred_element_type=jnp.float32
    ).astype(jnp.bfloat16)
    partial_grad = -jnp.einsum(
        "ktil,tlj->kij", upward, slice_cols, preferred_element_type=jnp.float32
    )
    scale = 0.5 / (tilt_count * tilt_groups * pixels * pixels)
    if tilt_groups != 2:
        scores = scale * lax.psum(score_part, "tilt")
        section_grad = lax.psum_scatter(partial_grad, "tilt", scatter_dimension=1, tiled=True)
        return (section_grad, scores)
    half = pixels // 2
    side = lax.axis_index("tilt")
    kept = lax.dynamic_slice_in_dim(partial_grad, side * half, half, axis=1)
    given = lax.dynamic_slice_in_dim(partial_grad, (1 - side) * half, half, axis=1)
    score_hi = score_part.astype(jnp.bfloat16)
    score_rest = score_part - score_hi.astype(jnp.float32)
    score_mid = score_rest.astype(jnp.bfloat16)
    score_low = (score_rest - score_mid.astype(jnp.float32)).astype(jnp.bfloat16)
    parcel = jnp.concatenate(
        (given.reshape(-1).astype(jnp.bfloat16), score_hi, score_mid, score_low)
    )
    parcel = lax.ppermute(parcel, "tilt", [(0, 1), (1, 0)]).astype(jnp.float32)
    section_grad = kept + parcel[: given.size].reshape(given.shape)
    parts = parcel[given.size :].reshape(3, own_count)
    scores = scale * (score_part + (parts[0] + (parts[1] + parts[2])))
    return (section_grad, scores)


def solution(mesh):
    in_specs = (
        P("dom", None, None),
        P("dom", "tilt", None, None),
        P("tilt", None, None),
        P("tilt", None, None),
        P("tilt", None, None),
        P("dom", None, None),
        P("dom", None),
        P("dom", None),
        P("dom", None),
    )
    out_specs = (P("dom", "tilt", None), P("dom"))
    return jax.shard_map(
        on_device, mesh=mesh, in_specs=in_specs, out_specs=out_specs, check_vma=False
    )
```

```python
import jax
import jax.numpy as jnp
from jax import lax
from jax.experimental import pallas as pl
from jax.experimental.pallas import tpu as pltpu
from jax.sharding import PartitionSpec as P

OVL = 16


def middle_kernel(
    owner_ref, local_ref, side_ref, weight_ref, image_ref, proj_ref, low_ref, high_ref,
    ctf_ref, weighted_ref, score_ref, kept_ref, sent_ref, residual_ref, return_ref,
):
    own_count, neighbours = local_ref.shape
    group = owner_ref.shape[2]
    half = kept_ref.shape[0]
    pixels = image_ref.shape[-1]
    peer_count = lax.axis_size("dom")
    steps = peer_count.bit_length() - 1
    me = lax.axis_index("dom")
    ctf = ctf_ref[0]
    zero = jnp.zeros((OVL, pixels), jnp.float32)

    def place_of(k, j):
        relative = owner_ref[k, j // group, j % group] ^ me
        flipped = sum(((relative >> (steps - 1 - b)) & 1) << b for b in range(steps))
        return flipped * own_count + local_ref[k, j]

    places = [[place_of(k, j) for j in range(neighbours)] for k in range(own_count)]
    edge_rows = []
    for k in range(own_count):
        lower, upper = zero, zero
        for j in range(neighbours):
            q = places[k][j]
            s = side_ref[k, j]
            w = weight_ref[k, j]
            low_band = low_ref[jnp.minimum(q, half - 1), s, 0]
            high_band = high_ref[jnp.maximum(q - half, 0), s, 0]
            band = jnp.where(q < half, low_band, high_band).astype(jnp.float32)
            lower = lower + jnp.where(s == 0, w, 0.0) * band
            upper = upper + jnp.where(s == 1, w, 0.0) * band
        residual_ref[k] = image_ref[k, 0].astype(jnp.float32) - proj_ref[k, 0].astype(jnp.float32)
        residual_ref[k, :OVL] = residual_ref[k, :OVL] - upper
        residual_ref[k, pixels - OVL :] = residual_ref[k, pixels - OVL :] - lower
        residual = residual_ref[k].astype(jnp.bfloat16)
        smoothed = jnp.dot(ctf, residual, preferred_element_type=jnp.float32).astype(jnp.bfloat16)
        filtered = lax.dot_general(
            smoothed, ctf, (((1,), (1,)), ((), ())), preferred_element_type=jnp.float32
        )
        score_ref[0, k] = jnp.full(score_ref.shape[2:], jnp.sum(filtered * filtered), jnp.float32)
        reverse = lax.dot_general(
            ctf, filtered.astype(jnp.bfloat16), (((0,), (0,)), ((), ())),
            preferred_element_type=jnp.float32,
        ).astype(jnp.bfloat16)
        weighted = jnp.dot(reverse, ctf, preferred_element_type=jnp.float32).astype(jnp.bfloat16)
        weighted_ref[k, 0] = weighted
        edge_rows.append(
            (weighted[pixels - OVL :].astype(jnp.float32), weighted[:OVL].astype(jnp.float32))
        )

    return_ref[...] = jnp.zeros_like(return_ref)
    for k in range(own_count):
        bottom_rows, top_rows = edge_rows[k]

        for j in range(neighbours):
            q = places[k][j]
            s = side_ref[k, j]
            rows = jnp.where(s == 0, bottom_rows, top_rows)
            part = (weight_ref[k, j] * rows).astype(jnp.bfloat16).astype(jnp.float32)
            return_ref[q, s] = return_ref[q, s] + part
    kept_ref[:, :, 0] = return_ref[:half]
    sent_ref[:, :, 0] = return_ref[half:].astype(jnp.bfloat16)


def middle(owner, local, side, weight, images, projected, edges_low, edges_high, ctf_filter):
    own_count, tilt_count, pixels, _ = images.shape
    half = edges_low.shape[0]
    total = 2 * half
    tiles = pl.BlockSpec((own_count, 1, pixels, pixels), lambda t: (0, t, 0, 0))
    halves = pl.BlockSpec((half, 2, 1, OVL, pixels), lambda t: (0, 0, t, 0, 0))
    smem = pl.BlockSpec(memory_space=pltpu.SMEM)
    flops = own_count * tilt_count * 8 * pixels**3
    moved = 2 * images.size * 3 + 10 * edges_low.size + 2 * ctf_filter.size
    return pl.pallas_call(
        middle_kernel,
        grid=(tilt_count,),
        in_specs=[
            smem,
            smem,
            smem,
            smem,
            tiles,
            tiles,
            halves,
            halves,
            pl.BlockSpec((1, pixels, pixels), lambda t: (t, 0, 0)),
        ],
        out_specs=[
            tiles,
            pl.BlockSpec((1, own_count, 8, 128), lambda t: (t, 0, 0, 0)),
            halves,
            halves,
        ],
        out_shape=[
            jax.ShapeDtypeStruct(images.shape, jnp.bfloat16),
            jax.ShapeDtypeStruct((tilt_count, own_count, 8, 128), jnp.float32),
            jax.ShapeDtypeStruct(edges_low.shape, jnp.float32),
            jax.ShapeDtypeStruct(edges_low.shape, jnp.bfloat16),
        ],
        scratch_shapes=[
            pltpu.VMEM((own_count, pixels, pixels), jnp.float32),
            pltpu.VMEM((total, 2, OVL, pixels), jnp.float32),
        ],
        compiler_params=pltpu.CompilerParams(dimension_semantics=("arbitrary",)),
        cost_estimate=pl.CostEstimate(flops=flops, transcendentals=0, bytes_accessed=moved),
    )(owner, local, side, weight, images, projected, edges_low, edges_high, ctf_filter)


def gather_stages(peer_count):
    steps = peer_count.bit_length() - 1
    strides = [peer_count >> (b + 1) for b in range(steps)]
    if steps <= 2:
        return [(stride,) for stride in strides]
    middle_strides = strides[1:-1]
    pairs = [tuple(middle_strides[i : i + 2]) for i in range(0, len(middle_strides), 2)]
    return [(strides[0],)] + pairs + [(strides[-1],)]


def on_device(
    sections, images, slice_rows, slice_cols, ctf_filter, nbr_owner, nbr_local, nbr_side, nbr_weight
):
    own_count = sections.shape[0]
    pixels = sections.shape[1]
    tilt_count = images.shape[1]
    neighbours = nbr_local.shape[1]
    peer_count = lax.axis_size("dom")
    total = own_count * peer_count
    me = lax.axis_index("dom")
    band_size = tilt_count * OVL * pixels

    halfway = jnp.einsum(
        "kij,tlj->ktil", sections, slice_cols, preferred_element_type=jnp.float32
    ).astype(jnp.bfloat16)
    projected = jnp.einsum(
        "tai,ktil->ktal", slice_rows, halfway, preferred_element_type=jnp.float32
    ).astype(jnp.bfloat16)
    edges = jnp.stack((projected[:, :, :OVL], projected[:, :, pixels - OVL :]), axis=1)
    stages = gather_stages(peer_count)
    edges_all = edges
    for stage in stages[:-1]:
        pieces = [edges_all]
        for g in range(1, 2 ** len(stage)):
            offset = sum(stride for i, stride in enumerate(stage) if (g >> i) & 1)
            pairs = [(i, i ^ offset) for i in range(peer_count)]
            pieces.append(lax.ppermute(edges_all, "dom", pairs))
        edges_all = jnp.concatenate(pieces, axis=0)
    edges_high = lax.ppermute(edges_all, "dom", [(i, i ^ 1) for i in range(peer_count)])

    weighted, score_tiles, kept_half, sent_half = middle(
        nbr_owner, nbr_local, nbr_side, nbr_weight, images, projected, edges_all, edges_high,
        ctf_filter,
    )
    score_part = jnp.sum(score_tiles[:, :, 0, 0], axis=0)
    tilt_groups = lax.axis_size("tilt")

    pairs = [(i, i ^ 1) for i in range(peer_count)]
    returned = kept_half + lax.ppermute(sent_half, "dom", pairs).astype(jnp.float32)
    for stage in [tuple(reversed(stage)) for stage in reversed(stages[:-1])]:
        count = 2 ** len(stage)
        share = returned.shape[0] // count
        kept = returned[:share]
        for g in range(1, count):
            offset = sum(
                stride for i, stride in enumerate(stage) if (g >> (len(stage) - 1 - i)) & 1
            )
            pairs = [(i, i ^ offset) for i in range(peer_count)]
            given = returned[g * share : (g + 1) * share].astype(jnp.bfloat16)
            kept = kept + lax.ppermute(given, "dom", pairs).astype(jnp.float32)
        returned = kept
    add_top = returned[:, 0]
    add_bottom = returned[:, 1]

    proj_grad = weighted.astype(jnp.float32)
    proj_grad = proj_grad.at[:, :, :OVL].add(add_top)
    proj_grad = proj_grad.at[:, :, pixels - OVL :].add(add_bottom)
    proj_half = proj_grad.astype(jnp.bfloat16)
    upward = jnp.einsum(
        "tai,ktal->ktil", slice_rows, proj_half, preferred_element_type=jnp.float32
    ).astype(jnp.bfloat16)
    partial_grad = -jnp.einsum(
        "ktil,tlj->kij", upward, slice_cols, preferred_element_type=jnp.float32
    )
    scale = 0.5 / (tilt_count * tilt_groups * pixels * pixels)
    if tilt_groups != 2:
        scores = scale * lax.psum(score_part, "tilt")
        section_grad = lax.psum_scatter(partial_grad, "tilt", scatter_dimension=1, tiled=True)
        return (section_grad, scores)
    half = pixels // 2
    side = lax.axis_index("tilt")
    kept = lax.dynamic_slice_in_dim(partial_grad, side * half, half, axis=1)
    given = lax.dynamic_slice_in_dim(partial_grad, (1 - side) * half, half, axis=1)
    score_hi = score_part.astype(jnp.bfloat16)
    score_rest = score_part - score_hi.astype(jnp.float32)
    score_mid = score_rest.astype(jnp.bfloat16)
    score_low = (score_rest - score_mid.astype(jnp.float32)).astype(jnp.bfloat16)
    parcel = jnp.concatenate(
        (given.reshape(-1).astype(jnp.bfloat16), score_hi, score_mid, score_low)
    )
    parcel = lax.ppermute(parcel, "tilt", [(0, 1), (1, 0)]).astype(jnp.float32)
    section_grad = kept + parcel[: given.size].reshape(given.shape)
    parts = parcel[given.size :].reshape(3, own_count)
    scores = scale * (score_part + (parts[0] + (parts[1] + parts[2])))
    return (section_grad, scores)


def solution(mesh):
    in_specs = (
        P("dom", None, None),
        P("dom", "tilt", None, None),
        P("tilt", None, None),
        P("tilt", None, None),
        P("tilt", None, None),
        P("dom", None, None),
        P("dom", None),
        P("dom", None),
        P("dom", None),
    )
    out_specs = (P("dom", "tilt", None), P("dom"))
    return jax.shard_map(
        on_device, mesh=mesh, in_specs=in_specs, out_specs=out_specs, check_vma=False
    )
```

```python
import jax
import jax.numpy as jnp
from jax import lax
from jax.experimental import pallas as pl
from jax.experimental.pallas import tpu as pltpu
from jax.sharding import PartitionSpec as P

OVL = 16


def middle_kernel(
    owner_ref, local_ref, side_ref, weight_ref, image_ref, proj_ref, low_ref, high_ref,
    ctf_ref, weighted_ref, score_ref, kept_ref, sent_ref, residual_ref, return_ref,
):
    own_count, neighbours = local_ref.shape
    group = owner_ref.shape[2]
    half = kept_ref.shape[0]
    pixels = image_ref.shape[-1]
    peer_count = lax.axis_size("dom")
    steps = peer_count.bit_length() - 1
    me = lax.axis_index("dom")
    ctf = ctf_ref[0]
    zero = jnp.zeros((OVL, pixels), jnp.float32)

    def place_of(k, j):
        relative = owner_ref[k, j // group, j % group] ^ me
        flipped = sum(((relative >> (steps - 1 - b)) & 1) << b for b in range(steps))
        return flipped * own_count + local_ref[k, j]

    places = [[place_of(k, j) for j in range(neighbours)] for k in range(own_count)]
    edge_rows = []
    for k in range(own_count):
        lower, upper = zero, zero
        for j in range(neighbours):
            q = places[k][j]
            s = side_ref[k, j]
            w = weight_ref[k, j]
            low_band = low_ref[jnp.minimum(q, half - 1), s, 0]
            high_band = high_ref[jnp.maximum(q - half, 0), s, 0]
            band = jnp.where(q < half, low_band, high_band).astype(jnp.float32)
            lower = lower + jnp.where(s == 0, w, 0.0) * band
            upper = upper + jnp.where(s == 1, w, 0.0) * band
        residual_ref[k] = image_ref[k, 0].astype(jnp.float32) - proj_ref[k, 0].astype(jnp.float32)
        residual_ref[k, :OVL] = residual_ref[k, :OVL] - upper
        residual_ref[k, pixels - OVL :] = residual_ref[k, pixels - OVL :] - lower
        residual = residual_ref[k].astype(jnp.bfloat16)
        smoothed = jnp.dot(ctf, residual, preferred_element_type=jnp.float32).astype(jnp.bfloat16)
        filtered = lax.dot_general(
            smoothed, ctf, (((1,), (1,)), ((), ())), preferred_element_type=jnp.float32
        )
        score_ref[0, k] = jnp.full(score_ref.shape[2:], jnp.sum(filtered * filtered), jnp.float32)
        reverse = lax.dot_general(
            ctf, filtered.astype(jnp.bfloat16), (((0,), (0,)), ((), ())),
            preferred_element_type=jnp.float32,
        ).astype(jnp.bfloat16)
        weighted = jnp.dot(reverse, ctf, preferred_element_type=jnp.float32).astype(jnp.bfloat16)
        weighted_ref[k, 0] = weighted
        edge_rows.append(
            (weighted[pixels - OVL :].astype(jnp.float32), weighted[:OVL].astype(jnp.float32))
        )

    return_ref[...] = jnp.zeros_like(return_ref)
    for k in range(own_count):
        bottom_rows, top_rows = edge_rows[k]

        for j in range(neighbours):
            q = places[k][j]
            s = side_ref[k, j]
            rows = jnp.where(s == 0, bottom_rows, top_rows)
            part = (weight_ref[k, j] * rows).astype(jnp.bfloat16).astype(jnp.float32)
            return_ref[q, s] = return_ref[q, s] + part
    kept_ref[:, :, 0] = return_ref[:half]
    sent_ref[:, :, 0] = return_ref[half:].astype(jnp.bfloat16)


def middle(owner, local, side, weight, images, projected, edges_low, edges_high, ctf_filter):
    own_count, tilt_count, pixels, _ = images.shape
    half = edges_low.shape[0]
    total = 2 * half
    tiles = pl.BlockSpec((own_count, 1, pixels, pixels), lambda t: (0, t, 0, 0))
    halves = pl.BlockSpec((half, 2, 1, OVL, pixels), lambda t: (0, 0, t, 0, 0))
    smem = pl.BlockSpec(memory_space=pltpu.SMEM)
    flops = own_count * tilt_count * 8 * pixels**3
    moved = 2 * images.size * 3 + 10 * edges_low.size + 2 * ctf_filter.size
    return pl.pallas_call(
        middle_kernel,
        grid=(tilt_count,),
        in_specs=[
            smem,
            smem,
            smem,
            smem,
            tiles,
            tiles,
            halves,
            halves,
            pl.BlockSpec((1, pixels, pixels), lambda t: (t, 0, 0)),
        ],
        out_specs=[
            tiles,
            pl.BlockSpec((1, own_count, 8, 128), lambda t: (t, 0, 0, 0)),
            halves,
            halves,
        ],
        out_shape=[
            jax.ShapeDtypeStruct(images.shape, jnp.bfloat16),
            jax.ShapeDtypeStruct((tilt_count, own_count, 8, 128), jnp.float32),
            jax.ShapeDtypeStruct(edges_low.shape, jnp.float32),
            jax.ShapeDtypeStruct(edges_low.shape, jnp.bfloat16),
        ],
        scratch_shapes=[
            pltpu.VMEM((own_count, pixels, pixels), jnp.float32),
            pltpu.VMEM((total, 2, OVL, pixels), jnp.float32),
        ],
        compiler_params=pltpu.CompilerParams(dimension_semantics=("arbitrary",)),
        cost_estimate=pl.CostEstimate(flops=flops, transcendentals=0, bytes_accessed=moved),
    )(owner, local, side, weight, images, projected, edges_low, edges_high, ctf_filter)


def gather_stages(peer_count):
    steps = peer_count.bit_length() - 1
    strides = [peer_count >> (b + 1) for b in range(steps)]
    if steps <= 2:
        return [(stride,) for stride in strides]
    middle_strides = strides[1:-1]
    pairs = [tuple(middle_strides[i : i + 2]) for i in range(0, len(middle_strides), 2)]
    return [(strides[0],)] + pairs + [(strides[-1],)]


def on_device(
    sections, images, slice_rows, slice_cols, ctf_filter, nbr_owner, nbr_local, nbr_side, nbr_weight
):
    own_count = sections.shape[0]
    pixels = sections.shape[1]
    tilt_count = images.shape[1]
    neighbours = nbr_local.shape[1]
    peer_count = lax.axis_size("dom")
    band_size = tilt_count * OVL * pixels

    halfway = jnp.einsum(
        "kij,tlj->ktil", sections, slice_cols, preferred_element_type=jnp.float32
    ).astype(jnp.bfloat16)
    projected = jnp.einsum(
        "tai,ktil->ktal", slice_rows, halfway, preferred_element_type=jnp.float32
    ).astype(jnp.bfloat16)
    stages = gather_stages(peer_count)
    core_pairs = [(i, i ^ 1) for i in range(peer_count)]
    chains = []
    for t in range(tilt_count):
        tilt = slice(t, t + 1)
        edges = jnp.stack(
            (projected[:, tilt, :OVL], projected[:, tilt, pixels - OVL :]), axis=1
        )
        edges_all = edges
        for stage in stages[:-1]:
            pieces = [edges_all]
            for g in range(1, 2 ** len(stage)):
                offset = sum(stride for i, stride in enumerate(stage) if (g >> i) & 1)
                pairs = [(i, i ^ offset) for i in range(peer_count)]
                pieces.append(lax.ppermute(edges_all, "dom", pairs))
            edges_all = jnp.concatenate(pieces, axis=0)
        edges_high = lax.ppermute(edges_all, "dom", core_pairs)
        weighted_t, score_t, kept_half, sent_half = middle(
            nbr_owner, nbr_local, nbr_side, nbr_weight, images[:, tilt], projected[:, tilt],
            edges_all, edges_high, ctf_filter[tilt],
        )
        returned = kept_half + lax.ppermute(sent_half, "dom", core_pairs).astype(jnp.float32)
        for stage in [tuple(reversed(stage)) for stage in reversed(stages[:-1])]:
            count = 2 ** len(stage)
            share = returned.shape[0] // count
            kept = returned[:share]
            for g in range(1, count):
                offset = sum(
                    stride for i, stride in enumerate(stage) if (g >> (len(stage) - 1 - i)) & 1
                )
                pairs = [(i, i ^ offset) for i in range(peer_count)]
                given = returned[g * share : (g + 1) * share].astype(jnp.bfloat16)
                kept = kept + lax.ppermute(given, "dom", pairs).astype(jnp.float32)
            returned = kept
        chains.append((weighted_t, score_t, returned))
    weighted = jnp.concatenate([c[0] for c in chains], axis=1)
    score_part = sum(jnp.sum(c[1][:, :, 0, 0], axis=0) for c in chains)
    returned = jnp.concatenate([c[2] for c in chains], axis=2)
    tilt_groups = lax.axis_size("tilt")

    add_top = returned[:, 0]
    add_bottom = returned[:, 1]

    proj_grad = weighted.astype(jnp.float32)
    proj_grad = proj_grad.at[:, :, :OVL].add(add_top)
    proj_grad = proj_grad.at[:, :, pixels - OVL :].add(add_bottom)
    proj_half = proj_grad.astype(jnp.bfloat16)
    upward = jnp.einsum(
        "tai,ktal->ktil", slice_rows, proj_half, preferred_element_type=jnp.float32
    ).astype(jnp.bfloat16)
    partial_grad = -jnp.einsum(
        "ktil,tlj->kij", upward, slice_cols, preferred_element_type=jnp.float32
    )
    scale = 0.5 / (tilt_count * tilt_groups * pixels * pixels)
    if tilt_groups != 2:
        scores = scale * lax.psum(score_part, "tilt")
        section_grad = lax.psum_scatter(partial_grad, "tilt", scatter_dimension=1, tiled=True)
        return (section_grad, scores)
    half = pixels // 2
    side = lax.axis_index("tilt")
    kept = lax.dynamic_slice_in_dim(partial_grad, side * half, half, axis=1)
    given = lax.dynamic_slice_in_dim(partial_grad, (1 - side) * half, half, axis=1)
    score_hi = score_part.astype(jnp.bfloat16)
    score_rest = score_part - score_hi.astype(jnp.float32)
    score_mid = score_rest.astype(jnp.bfloat16)
    score_low = (score_rest - score_mid.astype(jnp.float32)).astype(jnp.bfloat16)
    parcel = jnp.concatenate(
        (given.reshape(-1).astype(jnp.bfloat16), score_hi, score_mid, score_low)
    )
    parcel = lax.ppermute(parcel, "tilt", [(0, 1), (1, 0)]).astype(jnp.float32)
    section_grad = kept + parcel[: given.size].reshape(given.shape)
    parts = parcel[given.size :].reshape(3, own_count)
    scores = scale * (score_part + (parts[0] + (parts[1] + parts[2])))
    return (section_grad, scores)


def solution(mesh):
    in_specs = (
        P("dom", None, None),
        P("dom", "tilt", None, None),
        P("tilt", None, None),
        P("tilt", None, None),
        P("tilt", None, None),
        P("dom", None, None),
        P("dom", None),
        P("dom", None),
        P("dom", None),
    )
    out_specs = (P("dom", "tilt", None), P("dom"))
    return jax.shard_map(
        on_device, mesh=mesh, in_specs=in_specs, out_specs=out_specs, check_vma=False
    )
```

```python
import jax
import jax.numpy as jnp
from jax import lax
from jax.experimental import pallas as pl
from jax.experimental.pallas import tpu as pltpu
from jax.sharding import PartitionSpec as P

OVL = 16


def middle_kernel(
    owner_ref, local_ref, side_ref, weight_ref, image_ref, proj_ref, low_ref, high_ref,
    ctf_ref, weighted_ref, score_ref, kept_ref, sent_ref, residual_ref, return_ref,
):
    own_count, neighbours = local_ref.shape
    group = owner_ref.shape[2]
    half = kept_ref.shape[0]
    pixels = image_ref.shape[-1]
    peer_count = lax.axis_size("dom")
    steps = peer_count.bit_length() - 1
    me = lax.axis_index("dom")
    ctf = ctf_ref[0]
    zero = jnp.zeros((OVL, pixels), jnp.float32)

    def place_of(k, j):
        relative = owner_ref[k, j // group, j % group] ^ me
        flipped = sum(((relative >> (steps - 1 - b)) & 1) << b for b in range(steps))
        return flipped * own_count + local_ref[k, j]

    places = [[place_of(k, j) for j in range(neighbours)] for k in range(own_count)]
    edge_rows = []
    for k in range(own_count):
        lower, upper = zero, zero
        for j in range(neighbours):
            q = places[k][j]
            s = side_ref[k, j]
            w = weight_ref[k, j]
            low_band = low_ref[jnp.minimum(q, half - 1), s, 0]
            high_band = high_ref[jnp.maximum(q - half, 0), s, 0]
            band = jnp.where(q < half, low_band, high_band).astype(jnp.float32)
            lower = lower + jnp.where(s == 0, w, 0.0) * band
            upper = upper + jnp.where(s == 1, w, 0.0) * band
        residual_ref[k] = image_ref[k, 0].astype(jnp.float32) - proj_ref[k, 0].astype(jnp.float32)
        residual_ref[k, :OVL] = residual_ref[k, :OVL] - upper
        residual_ref[k, pixels - OVL :] = residual_ref[k, pixels - OVL :] - lower
        residual = residual_ref[k].astype(jnp.bfloat16)
        smoothed = jnp.dot(ctf, residual, preferred_element_type=jnp.float32).astype(jnp.bfloat16)
        filtered = lax.dot_general(
            smoothed, ctf, (((1,), (1,)), ((), ())), preferred_element_type=jnp.float32
        )
        score_ref[0, k] = jnp.full(score_ref.shape[2:], jnp.sum(filtered * filtered), jnp.float32)
        reverse = lax.dot_general(
            ctf, filtered.astype(jnp.bfloat16), (((0,), (0,)), ((), ())),
            preferred_element_type=jnp.float32,
        ).astype(jnp.bfloat16)
        weighted = jnp.dot(reverse, ctf, preferred_element_type=jnp.float32).astype(jnp.bfloat16)
        weighted_ref[k, 0] = weighted
        edge_rows.append(
            (weighted[pixels - OVL :].astype(jnp.float32), weighted[:OVL].astype(jnp.float32))
        )

    return_ref[...] = jnp.zeros_like(return_ref)
    for k in range(own_count):
        bottom_rows, top_rows = edge_rows[k]

        for j in range(neighbours):
            q = places[k][j]
            s = side_ref[k, j]
            rows = jnp.where(s == 0, bottom_rows, top_rows)
            part = (weight_ref[k, j] * rows).astype(jnp.bfloat16).astype(jnp.float32)
            return_ref[q, s] = return_ref[q, s] + part
    kept_ref[:, :, 0] = return_ref[:half]
    sent_ref[:, :, 0] = return_ref[half:].astype(jnp.bfloat16)


def middle(owner, local, side, weight, images, projected, edges_low, edges_high, ctf_filter):
    own_count, tilt_count, pixels, _ = images.shape
    half = edges_low.shape[0]
    total = 2 * half
    tiles = pl.BlockSpec((own_count, 1, pixels, pixels), lambda t: (0, t, 0, 0))
    halves = pl.BlockSpec((half, 2, 1, OVL, pixels), lambda t: (0, 0, t, 0, 0))
    smem = pl.BlockSpec(memory_space=pltpu.SMEM)
    flops = own_count * tilt_count * 8 * pixels**3
    moved = 2 * images.size * 3 + 10 * edges_low.size + 2 * ctf_filter.size
    return pl.pallas_call(
        middle_kernel,
        grid=(tilt_count,),
        in_specs=[
            smem,
            smem,
            smem,
            smem,
            tiles,
            tiles,
            halves,
            halves,
            pl.BlockSpec((1, pixels, pixels), lambda t: (t, 0, 0)),
        ],
        out_specs=[
            tiles,
            pl.BlockSpec((1, own_count, 8, 128), lambda t: (t, 0, 0, 0)),
            halves,
            halves,
        ],
        out_shape=[
            jax.ShapeDtypeStruct(images.shape, jnp.bfloat16),
            jax.ShapeDtypeStruct((tilt_count, own_count, 8, 128), jnp.float32),
            jax.ShapeDtypeStruct(edges_low.shape, jnp.float32),
            jax.ShapeDtypeStruct(edges_low.shape, jnp.bfloat16),
        ],
        scratch_shapes=[
            pltpu.VMEM((own_count, pixels, pixels), jnp.float32),
            pltpu.VMEM((total, 2, OVL, pixels), jnp.float32),
        ],
        compiler_params=pltpu.CompilerParams(dimension_semantics=("arbitrary",)),
        cost_estimate=pl.CostEstimate(flops=flops, transcendentals=0, bytes_accessed=moved),
    )(owner, local, side, weight, images, projected, edges_low, edges_high, ctf_filter)


def project_kernel(section_ref, rows_ref, cols_ref, projected_ref, edge_ref):
    own_count = section_ref.shape[0]
    pixels = section_ref.shape[-1]
    for k in range(own_count):
        halfway = lax.dot_general(
            section_ref[k], cols_ref[0], (((1,), (1,)), ((), ())),
            preferred_element_type=jnp.float32,
        ).astype(jnp.bfloat16)
        projected = jnp.dot(rows_ref[0], halfway, preferred_element_type=jnp.float32).astype(
            jnp.bfloat16
        )
        projected_ref[k, 0] = projected
        edge_ref[k, 0, 0] = projected[:OVL]
        edge_ref[k, 1, 0] = projected[pixels - OVL :]


def project(sections, slice_rows, slice_cols):
    own_count, pixels, _ = sections.shape
    tilt_count = slice_rows.shape[0]
    per_tilt = pl.BlockSpec((1, pixels, pixels), lambda t: (t, 0, 0))
    return pl.pallas_call(
        project_kernel,
        grid=(tilt_count,),
        in_specs=[pl.BlockSpec(sections.shape, lambda t: (0, 0, 0)), per_tilt, per_tilt],
        out_specs=[
            pl.BlockSpec((own_count, 1, pixels, pixels), lambda t: (0, t, 0, 0)),
            pl.BlockSpec((own_count, 2, 1, OVL, pixels), lambda t: (0, 0, t, 0, 0)),
        ],
        out_shape=[
            jax.ShapeDtypeStruct((own_count, tilt_count, pixels, pixels), jnp.bfloat16),
            jax.ShapeDtypeStruct((own_count, 2, tilt_count, OVL, pixels), jnp.bfloat16),
        ],
        compiler_params=pltpu.CompilerParams(dimension_semantics=("arbitrary",)),
        cost_estimate=pl.CostEstimate(
            flops=4 * own_count * tilt_count * pixels**3,
            transcendentals=0,
            bytes_accessed=2 * (sections.size + 2 * slice_rows.size + 2 * own_count * slice_rows.size),
        ),
    )(sections, slice_rows, slice_cols)


def gather_stages(peer_count):
    steps = peer_count.bit_length() - 1
    strides = [peer_count >> (b + 1) for b in range(steps)]
    if steps <= 2:
        return [(stride,) for stride in strides]
    middle_strides = strides[1:-1]
    pairs = [tuple(middle_strides[i : i + 2]) for i in range(0, len(middle_strides), 2)]
    return [(strides[0],)] + pairs + [(strides[-1],)]


def on_device(
    sections, images, slice_rows, slice_cols, ctf_filter, nbr_owner, nbr_local, nbr_side, nbr_weight
):
    own_count = sections.shape[0]
    pixels = sections.shape[1]
    tilt_count = images.shape[1]
    neighbours = nbr_local.shape[1]
    peer_count = lax.axis_size("dom")
    total = own_count * peer_count
    me = lax.axis_index("dom")
    band_size = tilt_count * OVL * pixels

    projected, edges = project(sections, slice_rows, slice_cols)
    stages = gather_stages(peer_count)
    edges_all = edges
    for stage in stages[:-1]:
        pieces = [edges_all]
        for g in range(1, 2 ** len(stage)):
            offset = sum(stride for i, stride in enumerate(stage) if (g >> i) & 1)
            pairs = [(i, i ^ offset) for i in range(peer_count)]
            pieces.append(lax.ppermute(edges_all, "dom", pairs))
        edges_all = jnp.concatenate(pieces, axis=0)
    edges_high = lax.ppermute(edges_all, "dom", [(i, i ^ 1) for i in range(peer_count)])

    weighted, score_tiles, kept_half, sent_half = middle(
        nbr_owner, nbr_local, nbr_side, nbr_weight, images, projected, edges_all, edges_high,
        ctf_filter,
    )
    score_part = jnp.sum(score_tiles[:, :, 0, 0], axis=0)
    tilt_groups = lax.axis_size("tilt")

    pairs = [(i, i ^ 1) for i in range(peer_count)]
    returned = kept_half + lax.ppermute(sent_half, "dom", pairs).astype(jnp.float32)
    for stage in [tuple(reversed(stage)) for stage in reversed(stages[:-1])]:
        count = 2 ** len(stage)
        share = returned.shape[0] // count
        kept = returned[:share]
        for g in range(1, count):
            offset = sum(
                stride for i, stride in enumerate(stage) if (g >> (len(stage) - 1 - i)) & 1
            )
            pairs = [(i, i ^ offset) for i in range(peer_count)]
            given = returned[g * share : (g + 1) * share].astype(jnp.bfloat16)
            kept = kept + lax.ppermute(given, "dom", pairs).astype(jnp.float32)
        returned = kept
    add_top = returned[:, 0]
    add_bottom = returned[:, 1]

    proj_grad = weighted.astype(jnp.float32)
    proj_grad = proj_grad.at[:, :, :OVL].add(add_top)
    proj_grad = proj_grad.at[:, :, pixels - OVL :].add(add_bottom)
    proj_half = proj_grad.astype(jnp.bfloat16)
    upward = jnp.einsum(
        "tai,ktal->ktil", slice_rows, proj_half, preferred_element_type=jnp.float32
    ).astype(jnp.bfloat16)
    partial_grad = -jnp.einsum(
        "ktil,tlj->kij", upward, slice_cols, preferred_element_type=jnp.float32
    )
    scale = 0.5 / (tilt_count * tilt_groups * pixels * pixels)
    if tilt_groups != 2:
        scores = scale * lax.psum(score_part, "tilt")
        section_grad = lax.psum_scatter(partial_grad, "tilt", scatter_dimension=1, tiled=True)
        return (section_grad, scores)
    half = pixels // 2
    side = lax.axis_index("tilt")
    kept = lax.dynamic_slice_in_dim(partial_grad, side * half, half, axis=1)
    given = lax.dynamic_slice_in_dim(partial_grad, (1 - side) * half, half, axis=1)
    score_hi = score_part.astype(jnp.bfloat16)
    score_rest = score_part - score_hi.astype(jnp.float32)
    score_mid = score_rest.astype(jnp.bfloat16)
    score_low = (score_rest - score_mid.astype(jnp.float32)).astype(jnp.bfloat16)
    parcel = jnp.concatenate(
        (given.reshape(-1).astype(jnp.bfloat16), score_hi, score_mid, score_low)
    )
    parcel = lax.ppermute(parcel, "tilt", [(0, 1), (1, 0)]).astype(jnp.float32)
    section_grad = kept + parcel[: given.size].reshape(given.shape)
    parts = parcel[given.size :].reshape(3, own_count)
    scores = scale * (score_part + (parts[0] + (parts[1] + parts[2])))
    return (section_grad, scores)


def solution(mesh):
    in_specs = (
        P("dom", None, None),
        P("dom", "tilt", None, None),
        P("tilt", None, None),
        P("tilt", None, None),
        P("tilt", None, None),
        P("dom", None, None),
        P("dom", None),
        P("dom", None),
        P("dom", None),
    )
    out_specs = (P("dom", "tilt", None), P("dom"))
    return jax.shard_map(
        on_device, mesh=mesh, in_specs=in_specs, out_specs=out_specs, check_vma=False
    )
```

```python
import jax
import jax.numpy as jnp
from jax import lax
from jax.experimental import pallas as pl
from jax.experimental.pallas import tpu as pltpu
from jax.sharding import PartitionSpec as P

OVL = 16


def middle_kernel(
    owner_ref, local_ref, side_ref, weight_ref, image_ref, proj_ref, low_ref, high_ref,
    ctf_ref, weighted_ref, score_ref, kept_ref, sent_ref, residual_ref, return_ref,
):
    own_count, neighbours = local_ref.shape
    group = owner_ref.shape[2]
    half = kept_ref.shape[0]
    pixels = image_ref.shape[-1]
    peer_count = lax.axis_size("dom")
    steps = peer_count.bit_length() - 1
    me = lax.axis_index("dom")
    ctf = ctf_ref[0]
    zero = jnp.zeros((OVL, pixels), jnp.float32)

    def place_of(k, j):
        relative = owner_ref[k, j // group, j % group] ^ me
        flipped = sum(((relative >> (steps - 1 - b)) & 1) << b for b in range(steps))
        return flipped * own_count + local_ref[k, j]

    places = [[place_of(k, j) for j in range(neighbours)] for k in range(own_count)]
    edge_rows = []
    for k in range(own_count):
        lower, upper = zero, zero
        for j in range(neighbours):
            q = places[k][j]
            s = side_ref[k, j]
            w = weight_ref[k, j]
            low_band = low_ref[jnp.minimum(q, half - 1), s, 0]
            high_band = high_ref[jnp.maximum(q - half, 0), s, 0]
            band = jnp.where(q < half, low_band, high_band).astype(jnp.float32)
            lower = lower + jnp.where(s == 0, w, 0.0) * band
            upper = upper + jnp.where(s == 1, w, 0.0) * band
        residual_ref[k] = image_ref[k, 0].astype(jnp.float32) - proj_ref[k, 0].astype(jnp.float32)
        residual_ref[k, :OVL] = residual_ref[k, :OVL] - upper
        residual_ref[k, pixels - OVL :] = residual_ref[k, pixels - OVL :] - lower
        residual = residual_ref[k].astype(jnp.bfloat16)
        smoothed = jnp.dot(ctf, residual, preferred_element_type=jnp.float32).astype(jnp.bfloat16)
        filtered = lax.dot_general(
            smoothed, ctf, (((1,), (1,)), ((), ())), preferred_element_type=jnp.float32
        )
        score_ref[0, k] = jnp.full(score_ref.shape[2:], jnp.sum(filtered * filtered), jnp.float32)
        reverse = lax.dot_general(
            ctf, filtered.astype(jnp.bfloat16), (((0,), (0,)), ((), ())),
            preferred_element_type=jnp.float32,
        ).astype(jnp.bfloat16)
        weighted = jnp.dot(reverse, ctf, preferred_element_type=jnp.float32).astype(jnp.bfloat16)
        weighted_ref[k, 0] = weighted
        edge_rows.append(
            (weighted[pixels - OVL :].astype(jnp.float32), weighted[:OVL].astype(jnp.float32))
        )

    kept_ref[...] = jnp.zeros_like(kept_ref)
    return_ref[...] = jnp.zeros_like(return_ref)
    for k in range(own_count):
        bottom_rows, top_rows = edge_rows[k]
        for j in range(neighbours):
            q = places[k][j]
            s = side_ref[k, j]
            rows = jnp.where(s == 0, bottom_rows, top_rows)
            part = (weight_ref[k, j] * rows).astype(jnp.bfloat16).astype(jnp.float32)
            kept_at = jnp.minimum(q, half - 1)
            sent_at = jnp.maximum(q - half, 0)
            kept_ref[kept_at, s, 0] = kept_ref[kept_at, s, 0] + jnp.where(q < half, part, 0.0)
            return_ref[sent_at, s] = return_ref[sent_at, s] + jnp.where(q < half, 0.0, part)
    sent_ref[:, :, 0] = return_ref[...].astype(jnp.bfloat16)


def middle(owner, local, side, weight, images, projected, edges_low, edges_high, ctf_filter):
    own_count, tilt_count, pixels, _ = images.shape
    half = edges_low.shape[0]
    total = 2 * half
    tiles = pl.BlockSpec((own_count, 1, pixels, pixels), lambda t: (0, t, 0, 0))
    halves = pl.BlockSpec((half, 2, 1, OVL, pixels), lambda t: (0, 0, t, 0, 0))
    smem = pl.BlockSpec(memory_space=pltpu.SMEM)
    flops = own_count * tilt_count * 8 * pixels**3
    moved = 2 * images.size * 3 + 10 * edges_low.size + 2 * ctf_filter.size
    return pl.pallas_call(
        middle_kernel,
        grid=(tilt_count,),
        in_specs=[
            smem,
            smem,
            smem,
            smem,
            tiles,
            tiles,
            halves,
            halves,
            pl.BlockSpec((1, pixels, pixels), lambda t: (t, 0, 0)),
        ],
        out_specs=[
            tiles,
            pl.BlockSpec((1, own_count, 8, 128), lambda t: (t, 0, 0, 0)),
            halves,
            halves,
        ],
        out_shape=[
            jax.ShapeDtypeStruct(images.shape, jnp.bfloat16),
            jax.ShapeDtypeStruct((tilt_count, own_count, 8, 128), jnp.float32),
            jax.ShapeDtypeStruct(edges_low.shape, jnp.float32),
            jax.ShapeDtypeStruct(edges_low.shape, jnp.bfloat16),
        ],
        scratch_shapes=[
            pltpu.VMEM((own_count, pixels, pixels), jnp.float32),
            pltpu.VMEM((half, 2, OVL, pixels), jnp.float32),
        ],
        compiler_params=pltpu.CompilerParams(dimension_semantics=("arbitrary",)),
        cost_estimate=pl.CostEstimate(flops=flops, transcendentals=0, bytes_accessed=moved),
    )(owner, local, side, weight, images, projected, edges_low, edges_high, ctf_filter)


def gather_stages(peer_count):
    steps = peer_count.bit_length() - 1
    strides = [peer_count >> (b + 1) for b in range(steps)]
    if steps <= 2:
        return [(stride,) for stride in strides]
    middle_strides = strides[1:-1]
    pairs = [tuple(middle_strides[i : i + 2]) for i in range(0, len(middle_strides), 2)]
    return [(strides[0],)] + pairs + [(strides[-1],)]


def on_device(
    sections, images, slice_rows, slice_cols, ctf_filter, nbr_owner, nbr_local, nbr_side, nbr_weight
):
    own_count = sections.shape[0]
    pixels = sections.shape[1]
    tilt_count = images.shape[1]
    neighbours = nbr_local.shape[1]
    peer_count = lax.axis_size("dom")
    total = own_count * peer_count
    me = lax.axis_index("dom")
    band_size = tilt_count * OVL * pixels

    halfway = jnp.einsum(
        "kij,tlj->ktil", sections, slice_cols, preferred_element_type=jnp.float32
    ).astype(jnp.bfloat16)
    projected = jnp.einsum(
        "tai,ktil->ktal", slice_rows, halfway, preferred_element_type=jnp.float32
    ).astype(jnp.bfloat16)
    edges = jnp.stack((projected[:, :, :OVL], projected[:, :, pixels - OVL :]), axis=1)
    stages = gather_stages(peer_count)
    edges_all = edges
    for stage in stages[:-1]:
        pieces = [edges_all]
        for g in range(1, 2 ** len(stage)):
            offset = sum(stride for i, stride in enumerate(stage) if (g >> i) & 1)
            pairs = [(i, i ^ offset) for i in range(peer_count)]
            pieces.append(lax.ppermute(edges_all, "dom", pairs))
        edges_all = jnp.concatenate(pieces, axis=0)
    edges_high = lax.ppermute(edges_all, "dom", [(i, i ^ 1) for i in range(peer_count)])

    weighted, score_tiles, kept_half, sent_half = middle(
        nbr_owner, nbr_local, nbr_side, nbr_weight, images, projected, edges_all, edges_high,
        ctf_filter,
    )
    score_part = jnp.sum(score_tiles[:, :, 0, 0], axis=0)
    tilt_groups = lax.axis_size("tilt")

    pairs = [(i, i ^ 1) for i in range(peer_count)]
    returned = kept_half + lax.ppermute(sent_half, "dom", pairs).astype(jnp.float32)
    for stage in [tuple(reversed(stage)) for stage in reversed(stages[:-1])]:
        count = 2 ** len(stage)
        share = returned.shape[0] // count
        kept = returned[:share]
        for g in range(1, count):
            offset = sum(
                stride for i, stride in enumerate(stage) if (g >> (len(stage) - 1 - i)) & 1
            )
            pairs = [(i, i ^ offset) for i in range(peer_count)]
            given = returned[g * share : (g + 1) * share].astype(jnp.bfloat16)
            kept = kept + lax.ppermute(given, "dom", pairs).astype(jnp.float32)
        returned = kept
    add_top = returned[:, 0]
    add_bottom = returned[:, 1]

    proj_grad = weighted.astype(jnp.float32)
    proj_grad = proj_grad.at[:, :, :OVL].add(add_top)
    proj_grad = proj_grad.at[:, :, pixels - OVL :].add(add_bottom)
    proj_half = proj_grad.astype(jnp.bfloat16)
    upward = jnp.einsum(
        "tai,ktal->ktil", slice_rows, proj_half, preferred_element_type=jnp.float32
    ).astype(jnp.bfloat16)
    partial_grad = -jnp.einsum(
        "ktil,tlj->kij", upward, slice_cols, preferred_element_type=jnp.float32
    )
    scale = 0.5 / (tilt_count * tilt_groups * pixels * pixels)
    if tilt_groups != 2:
        scores = scale * lax.psum(score_part, "tilt")
        section_grad = lax.psum_scatter(partial_grad, "tilt", scatter_dimension=1, tiled=True)
        return (section_grad, scores)
    half = pixels // 2
    side = lax.axis_index("tilt")
    kept = lax.dynamic_slice_in_dim(partial_grad, side * half, half, axis=1)
    given = lax.dynamic_slice_in_dim(partial_grad, (1 - side) * half, half, axis=1)
    score_hi = score_part.astype(jnp.bfloat16)
    score_rest = score_part - score_hi.astype(jnp.float32)
    score_mid = score_rest.astype(jnp.bfloat16)
    score_low = (score_rest - score_mid.astype(jnp.float32)).astype(jnp.bfloat16)
    parcel = jnp.concatenate(
        (given.reshape(-1).astype(jnp.bfloat16), score_hi, score_mid, score_low)
    )
    parcel = lax.ppermute(parcel, "tilt", [(0, 1), (1, 0)]).astype(jnp.float32)
    section_grad = kept + parcel[: given.size].reshape(given.shape)
    parts = parcel[given.size :].reshape(3, own_count)
    scores = scale * (score_part + (parts[0] + (parts[1] + parts[2])))
    return (section_grad, scores)


def solution(mesh):
    in_specs = (
        P("dom", None, None),
        P("dom", "tilt", None, None),
        P("tilt", None, None),
        P("tilt", None, None),
        P("tilt", None, None),
        P("dom", None, None),
        P("dom", None),
        P("dom", None),
        P("dom", None),
    )
    out_specs = (P("dom", "tilt", None), P("dom"))
    return jax.shard_map(
        on_device, mesh=mesh, in_specs=in_specs, out_specs=out_specs, check_vma=False
    )
```

```python
import jax
import jax.numpy as jnp
from jax import lax
from jax.experimental import pallas as pl
from jax.experimental.pallas import tpu as pltpu
from jax.sharding import PartitionSpec as P

OVL = 16


def middle_kernel(
    owner_ref, local_ref, side_ref, weight_ref, image_ref, proj_ref, low_ref, high_ref,
    ctf_ref, weighted_ref, score_ref, kept_ref, sent_ref, residual_ref, return_ref,
):
    own_count, neighbours = local_ref.shape
    group = owner_ref.shape[2]
    half = kept_ref.shape[0]
    pixels = image_ref.shape[-1]
    peer_count = lax.axis_size("dom")
    steps = peer_count.bit_length() - 1
    me = lax.axis_index("dom")
    ctf = ctf_ref[0]
    zero = jnp.zeros((OVL, pixels), jnp.float32)

    def place_of(k, j):
        relative = owner_ref[k, j // group, j % group] ^ me
        flipped = sum(((relative >> (steps - 1 - b)) & 1) << b for b in range(steps))
        return flipped * own_count + local_ref[k, j]

    places = [[place_of(k, j) for j in range(neighbours)] for k in range(own_count)]
    edge_rows = []
    for k in range(own_count):
        lower, upper = zero, zero
        for j in range(neighbours):
            q = places[k][j]
            s = side_ref[k, j]
            w = weight_ref[k, j]
            low_band = low_ref[jnp.minimum(q, half - 1), s, 0]
            high_band = high_ref[jnp.maximum(q - half, 0), s, 0]
            band = jnp.where(q < half, low_band, high_band).astype(jnp.float32)
            lower = lower + jnp.where(s == 0, w, 0.0) * band
            upper = upper + jnp.where(s == 1, w, 0.0) * band
        residual_ref[k] = image_ref[k, 0].astype(jnp.float32) - proj_ref[k, 0].astype(jnp.float32)
        residual_ref[k, :OVL] = residual_ref[k, :OVL] - upper
        residual_ref[k, pixels - OVL :] = residual_ref[k, pixels - OVL :] - lower
        residual = residual_ref[k].astype(jnp.bfloat16)
        smoothed = jnp.dot(ctf, residual, preferred_element_type=jnp.float32).astype(jnp.bfloat16)
        filtered = lax.dot_general(
            smoothed, ctf, (((1,), (1,)), ((), ())), preferred_element_type=jnp.float32
        )
        score_ref[0, k] = jnp.full(score_ref.shape[2:], jnp.sum(filtered * filtered), jnp.float32)
        reverse = lax.dot_general(
            ctf, filtered.astype(jnp.bfloat16), (((0,), (0,)), ((), ())),
            preferred_element_type=jnp.float32,
        ).astype(jnp.bfloat16)
        weighted = jnp.dot(reverse, ctf, preferred_element_type=jnp.float32).astype(jnp.bfloat16)
        weighted_ref[k, 0] = weighted
        edge_rows.append(
            (weighted[pixels - OVL :].astype(jnp.float32), weighted[:OVL].astype(jnp.float32))
        )

    return_ref[...] = jnp.zeros_like(return_ref)
    for k in range(own_count):
        bottom_rows, top_rows = edge_rows[k]

        for j in range(neighbours):
            q = places[k][j]
            s = side_ref[k, j]
            rows = jnp.where(s == 0, bottom_rows, top_rows)
            part = (weight_ref[k, j] * rows).astype(jnp.bfloat16).astype(jnp.float32)
            return_ref[q, s] = return_ref[q, s] + part
    kept_ref[:, :, 0] = return_ref[:half]
    sent_ref[:, :, 0] = return_ref[half:].astype(jnp.bfloat16)


def middle(owner, local, side, weight, images, projected, edges_low, edges_high, ctf_filter):
    own_count, tilt_count, pixels, _ = images.shape
    half = edges_low.shape[0]
    total = 2 * half
    tiles = pl.BlockSpec((own_count, 1, pixels, pixels), lambda t: (0, t, 0, 0))
    halves = pl.BlockSpec((half, 2, 1, OVL, pixels), lambda t: (0, 0, t, 0, 0))
    smem = pl.BlockSpec(memory_space=pltpu.SMEM)
    flops = own_count * tilt_count * 8 * pixels**3
    moved = 2 * images.size * 3 + 10 * edges_low.size + 2 * ctf_filter.size
    return pl.pallas_call(
        middle_kernel,
        grid=(tilt_count,),
        in_specs=[
            smem,
            smem,
            smem,
            smem,
            tiles,
            tiles,
            halves,
            halves,
            pl.BlockSpec((1, pixels, pixels), lambda t: (t, 0, 0)),
        ],
        out_specs=[
            tiles,
            pl.BlockSpec((1, own_count, 8, 128), lambda t: (t, 0, 0, 0)),
            halves,
            halves,
        ],
        out_shape=[
            jax.ShapeDtypeStruct(images.shape, jnp.bfloat16),
            jax.ShapeDtypeStruct((tilt_count, own_count, 8, 128), jnp.float32),
            jax.ShapeDtypeStruct(edges_low.shape, jnp.float32),
            jax.ShapeDtypeStruct(edges_low.shape, jnp.bfloat16),
        ],
        scratch_shapes=[
            pltpu.VMEM((own_count, pixels, pixels), jnp.float32),
            pltpu.VMEM((total, 2, OVL, pixels), jnp.float32),
        ],
        compiler_params=pltpu.CompilerParams(dimension_semantics=("arbitrary",)),
        cost_estimate=pl.CostEstimate(flops=flops, transcendentals=0, bytes_accessed=moved),
    )(owner, local, side, weight, images, projected, edges_low, edges_high, ctf_filter)


def gather_stages(peer_count):
    steps = peer_count.bit_length() - 1
    strides = [peer_count >> (b + 1) for b in range(steps)]
    if steps <= 2:
        return [(stride,) for stride in strides]
    middle_strides = strides[1:-1]
    pairs = [tuple(middle_strides[i : i + 2]) for i in range(0, len(middle_strides), 2)]
    return [(strides[0],)] + pairs + [(strides[-1],)]


def on_device(
    sections, images, slice_rows, slice_cols, ctf_filter, nbr_owner, nbr_local, nbr_side, nbr_weight
):
    own_count = sections.shape[0]
    pixels = sections.shape[1]
    tilt_count = images.shape[1]
    neighbours = nbr_local.shape[1]
    peer_count = lax.axis_size("dom")
    total = own_count * peer_count
    me = lax.axis_index("dom")
    band_size = tilt_count * OVL * pixels

    halfway = jnp.einsum(
        "kij,tlj->ktil", sections, slice_cols, preferred_element_type=jnp.float32
    ).astype(jnp.bfloat16)
    projected = jnp.einsum(
        "tai,ktil->ktal", slice_rows, halfway, preferred_element_type=jnp.float32
    ).astype(jnp.bfloat16)
    edges = jnp.stack((projected[:, :, :OVL], projected[:, :, pixels - OVL :]), axis=1)
    stages = gather_stages(peer_count)
    edges_all = edges
    for stage in stages[:-1]:
        pieces = [edges_all]
        for g in range(1, 2 ** len(stage)):
            offset = sum(stride for i, stride in enumerate(stage) if (g >> i) & 1)
            pairs = [(i, i ^ offset) for i in range(peer_count)]
            pieces.append(lax.ppermute(edges_all, "dom", pairs))
        edges_all = jnp.concatenate(pieces, axis=0)
    edges_high = lax.ppermute(edges_all, "dom", [(i, i ^ 1) for i in range(peer_count)])

    weighted, score_tiles, kept_half, sent_half = middle(
        nbr_owner, nbr_local, nbr_side, nbr_weight, images, projected, edges_all, edges_high,
        ctf_filter,
    )
    score_part = jnp.sum(score_tiles[:, :, 0, 0], axis=0)
    tilt_groups = lax.axis_size("tilt")
    scale = 0.5 / (tilt_count * tilt_groups * pixels * pixels)
    if tilt_groups == 2:
        score_hi = score_part.astype(jnp.bfloat16)
        score_rest = score_part - score_hi.astype(jnp.float32)
        score_mid = score_rest.astype(jnp.bfloat16)
        score_low = (score_rest - score_mid.astype(jnp.float32)).astype(jnp.bfloat16)
        parts = jnp.stack((score_hi, score_mid, score_low))
        parts = lax.ppermute(parts, "tilt", [(0, 1), (1, 0)]).astype(jnp.float32)
        scores = scale * (score_part + (parts[0] + (parts[1] + parts[2])))

    pairs = [(i, i ^ 1) for i in range(peer_count)]
    returned = kept_half + lax.ppermute(sent_half, "dom", pairs).astype(jnp.float32)
    for stage in [tuple(reversed(stage)) for stage in reversed(stages[:-1])]:
        count = 2 ** len(stage)
        share = returned.shape[0] // count
        kept = returned[:share]
        for g in range(1, count):
            offset = sum(
                stride for i, stride in enumerate(stage) if (g >> (len(stage) - 1 - i)) & 1
            )
            pairs = [(i, i ^ offset) for i in range(peer_count)]
            given = returned[g * share : (g + 1) * share].astype(jnp.bfloat16)
            kept = kept + lax.ppermute(given, "dom", pairs).astype(jnp.float32)
        returned = kept
    add_top = returned[:, 0]
    add_bottom = returned[:, 1]

    proj_grad = weighted.astype(jnp.float32)
    proj_grad = proj_grad.at[:, :, :OVL].add(add_top)
    proj_grad = proj_grad.at[:, :, pixels - OVL :].add(add_bottom)
    proj_half = proj_grad.astype(jnp.bfloat16)
    upward = jnp.einsum(
        "tai,ktal->ktil", slice_rows, proj_half, preferred_element_type=jnp.float32
    ).astype(jnp.bfloat16)
    partial_grad = -jnp.einsum(
        "ktil,tlj->kij", upward, slice_cols, preferred_element_type=jnp.float32
    )
    if tilt_groups != 2:
        scores = scale * lax.psum(score_part, "tilt")
        section_grad = lax.psum_scatter(partial_grad, "tilt", scatter_dimension=1, tiled=True)
        return (section_grad, scores)
    half = pixels // 2
    side = lax.axis_index("tilt")
    kept = lax.dynamic_slice_in_dim(partial_grad, side * half, half, axis=1)
    given = lax.dynamic_slice_in_dim(partial_grad, (1 - side) * half, half, axis=1)
    given = lax.ppermute(given.astype(jnp.bfloat16), "tilt", [(0, 1), (1, 0)])
    section_grad = kept + given.astype(jnp.float32)
    return (section_grad, scores)


def solution(mesh):
    in_specs = (
        P("dom", None, None),
        P("dom", "tilt", None, None),
        P("tilt", None, None),
        P("tilt", None, None),
        P("tilt", None, None),
        P("dom", None, None),
        P("dom", None),
        P("dom", None),
        P("dom", None),
    )
    out_specs = (P("dom", "tilt", None), P("dom"))
    return jax.shard_map(
        on_device, mesh=mesh, in_specs=in_specs, out_specs=out_specs, check_vma=False
    )
```

```python
import jax
import jax.numpy as jnp
from jax import lax
from jax.experimental import pallas as pl
from jax.experimental.pallas import tpu as pltpu
from jax.sharding import PartitionSpec as P

OVL = 16


def middle_kernel(
    owner_ref, local_ref, side_ref, weight_ref, image_ref, proj_ref, low_ref, high_ref,
    ctf_ref, weighted_ref, score_ref, kept_ref, sent_ref, residual_ref, return_ref,
):
    own_count, neighbours = local_ref.shape
    group = owner_ref.shape[2]
    half = kept_ref.shape[0]
    pixels = image_ref.shape[-1]
    peer_count = lax.axis_size("dom")
    steps = peer_count.bit_length() - 1
    me = lax.axis_index("dom")
    ctf = ctf_ref[0]
    ctf_t = ctf.T
    zero = jnp.zeros((OVL, pixels), jnp.float32)

    def place_of(k, j):
        relative = owner_ref[k, j // group, j % group] ^ me
        flipped = sum(((relative >> (steps - 1 - b)) & 1) << b for b in range(steps))
        return flipped * own_count + local_ref[k, j]

    places = [[place_of(k, j) for j in range(neighbours)] for k in range(own_count)]
    edge_rows = []
    for k in range(own_count):
        lower, upper = zero, zero
        for j in range(neighbours):
            q = places[k][j]
            s = side_ref[k, j]
            w = weight_ref[k, j]
            low_band = low_ref[jnp.minimum(q, half - 1), s, 0]
            high_band = high_ref[jnp.maximum(q - half, 0), s, 0]
            band = jnp.where(q < half, low_band, high_band).astype(jnp.float32)
            lower = lower + jnp.where(s == 0, w, 0.0) * band
            upper = upper + jnp.where(s == 1, w, 0.0) * band
        residual_ref[k] = image_ref[k, 0].astype(jnp.float32) - proj_ref[k, 0].astype(jnp.float32)
        residual_ref[k, :OVL] = residual_ref[k, :OVL] - upper
        residual_ref[k, pixels - OVL :] = residual_ref[k, pixels - OVL :] - lower
        residual = residual_ref[k].astype(jnp.bfloat16)
        smoothed = jnp.dot(ctf, residual, preferred_element_type=jnp.float32).astype(jnp.bfloat16)
        filtered = jnp.dot(smoothed, ctf_t, preferred_element_type=jnp.float32)
        score_ref[0, k] = jnp.full(score_ref.shape[2:], jnp.sum(filtered * filtered), jnp.float32)
        reverse = jnp.dot(
            ctf_t, filtered.astype(jnp.bfloat16), preferred_element_type=jnp.float32
        ).astype(jnp.bfloat16)
        weighted = jnp.dot(reverse, ctf, preferred_element_type=jnp.float32).astype(jnp.bfloat16)
        weighted_ref[k, 0] = weighted
        edge_rows.append(
            (weighted[pixels - OVL :].astype(jnp.float32), weighted[:OVL].astype(jnp.float32))
        )

    return_ref[...] = jnp.zeros_like(return_ref)
    for k in range(own_count):
        bottom_rows, top_rows = edge_rows[k]

        for j in range(neighbours):
            q = places[k][j]
            s = side_ref[k, j]
            rows = jnp.where(s == 0, bottom_rows, top_rows)
            part = (weight_ref[k, j] * rows).astype(jnp.bfloat16).astype(jnp.float32)
            return_ref[q, s] = return_ref[q, s] + part
    kept_ref[:, :, 0] = return_ref[:half]
    sent_ref[:, :, 0] = return_ref[half:].astype(jnp.bfloat16)


def middle(owner, local, side, weight, images, projected, edges_low, edges_high, ctf_filter):
    own_count, tilt_count, pixels, _ = images.shape
    half = edges_low.shape[0]
    total = 2 * half
    tiles = pl.BlockSpec((own_count, 1, pixels, pixels), lambda t: (0, t, 0, 0))
    halves = pl.BlockSpec((half, 2, 1, OVL, pixels), lambda t: (0, 0, t, 0, 0))
    smem = pl.BlockSpec(memory_space=pltpu.SMEM)
    flops = own_count * tilt_count * 8 * pixels**3
    moved = 2 * images.size * 3 + 10 * edges_low.size + 2 * ctf_filter.size
    return pl.pallas_call(
        middle_kernel,
        grid=(tilt_count,),
        in_specs=[
            smem,
            smem,
            smem,
            smem,
            tiles,
            tiles,
            halves,
            halves,
            pl.BlockSpec((1, pixels, pixels), lambda t: (t, 0, 0)),
        ],
        out_specs=[
            tiles,
            pl.BlockSpec((1, own_count, 8, 128), lambda t: (t, 0, 0, 0)),
            halves,
            halves,
        ],
        out_shape=[
            jax.ShapeDtypeStruct(images.shape, jnp.bfloat16),
            jax.ShapeDtypeStruct((tilt_count, own_count, 8, 128), jnp.float32),
            jax.ShapeDtypeStruct(edges_low.shape, jnp.float32),
            jax.ShapeDtypeStruct(edges_low.shape, jnp.bfloat16),
        ],
        scratch_shapes=[
            pltpu.VMEM((own_count, pixels, pixels), jnp.float32),
            pltpu.VMEM((total, 2, OVL, pixels), jnp.float32),
        ],
        compiler_params=pltpu.CompilerParams(dimension_semantics=("arbitrary",)),
        cost_estimate=pl.CostEstimate(flops=flops, transcendentals=0, bytes_accessed=moved),
    )(owner, local, side, weight, images, projected, edges_low, edges_high, ctf_filter)


def gather_stages(peer_count):
    steps = peer_count.bit_length() - 1
    strides = [peer_count >> (b + 1) for b in range(steps)]
    if steps <= 2:
        return [(stride,) for stride in strides]
    middle_strides = strides[1:-1]
    pairs = [tuple(middle_strides[i : i + 2]) for i in range(0, len(middle_strides), 2)]
    return [(strides[0],)] + pairs + [(strides[-1],)]


def on_device(
    sections, images, slice_rows, slice_cols, ctf_filter, nbr_owner, nbr_local, nbr_side, nbr_weight
):
    own_count = sections.shape[0]
    pixels = sections.shape[1]
    tilt_count = images.shape[1]
    neighbours = nbr_local.shape[1]
    peer_count = lax.axis_size("dom")
    total = own_count * peer_count
    me = lax.axis_index("dom")
    band_size = tilt_count * OVL * pixels

    halfway = jnp.einsum(
        "kij,tlj->ktil", sections, slice_cols, preferred_element_type=jnp.float32
    ).astype(jnp.bfloat16)
    projected = jnp.einsum(
        "tai,ktil->ktal", slice_rows, halfway, preferred_element_type=jnp.float32
    ).astype(jnp.bfloat16)
    edges = jnp.stack((projected[:, :, :OVL], projected[:, :, pixels - OVL :]), axis=1)
    stages = gather_stages(peer_count)
    edges_all = edges
    for stage in stages[:-1]:
        pieces = [edges_all]
        for g in range(1, 2 ** len(stage)):
            offset = sum(stride for i, stride in enumerate(stage) if (g >> i) & 1)
            pairs = [(i, i ^ offset) for i in range(peer_count)]
            pieces.append(lax.ppermute(edges_all, "dom", pairs))
        edges_all = jnp.concatenate(pieces, axis=0)
    edges_high = lax.ppermute(edges_all, "dom", [(i, i ^ 1) for i in range(peer_count)])

    weighted, score_tiles, kept_half, sent_half = middle(
        nbr_owner, nbr_local, nbr_side, nbr_weight, images, projected, edges_all, edges_high,
        ctf_filter,
    )
    score_part = jnp.sum(score_tiles[:, :, 0, 0], axis=0)
    tilt_groups = lax.axis_size("tilt")
    scale = 0.5 / (tilt_count * tilt_groups * pixels * pixels)
    if tilt_groups == 2:
        score_hi = score_part.astype(jnp.bfloat16)
        score_rest = score_part - score_hi.astype(jnp.float32)
        score_mid = score_rest.astype(jnp.bfloat16)
        score_low = (score_rest - score_mid.astype(jnp.float32)).astype(jnp.bfloat16)
        parts = jnp.stack((score_hi, score_mid, score_low))
        parts = lax.ppermute(parts, "tilt", [(0, 1), (1, 0)]).astype(jnp.float32)
        scores = scale * (score_part + (parts[0] + (parts[1] + parts[2])))

    pairs = [(i, i ^ 1) for i in range(peer_count)]
    returned = kept_half + lax.ppermute(sent_half, "dom", pairs).astype(jnp.float32)
    for stage in [tuple(reversed(stage)) for stage in reversed(stages[:-1])]:
        count = 2 ** len(stage)
        share = returned.shape[0] // count
        kept = returned[:share]
        for g in range(1, count):
            offset = sum(
                stride for i, stride in enumerate(stage) if (g >> (len(stage) - 1 - i)) & 1
            )
            pairs = [(i, i ^ offset) for i in range(peer_count)]
            given = returned[g * share : (g + 1) * share].astype(jnp.bfloat16)
            kept = kept + lax.ppermute(given, "dom", pairs).astype(jnp.float32)
        returned = kept
    add_top = returned[:, 0]
    add_bottom = returned[:, 1]

    proj_grad = weighted.astype(jnp.float32)
    proj_grad = proj_grad.at[:, :, :OVL].add(add_top)
    proj_grad = proj_grad.at[:, :, pixels - OVL :].add(add_bottom)
    proj_half = proj_grad.astype(jnp.bfloat16)
    upward = jnp.einsum(
        "tai,ktal->ktil", slice_rows, proj_half, preferred_element_type=jnp.float32
    ).astype(jnp.bfloat16)
    partial_grad = -jnp.einsum(
        "ktil,tlj->kij", upward, slice_cols, preferred_element_type=jnp.float32
    )
    if tilt_groups != 2:
        scores = scale * lax.psum(score_part, "tilt")
        section_grad = lax.psum_scatter(partial_grad, "tilt", scatter_dimension=1, tiled=True)
        return (section_grad, scores)
    half = pixels // 2
    side = lax.axis_index("tilt")
    kept = lax.dynamic_slice_in_dim(partial_grad, side * half, half, axis=1)
    given = lax.dynamic_slice_in_dim(partial_grad, (1 - side) * half, half, axis=1)
    given = lax.ppermute(given.astype(jnp.bfloat16), "tilt", [(0, 1), (1, 0)])
    section_grad = kept + given.astype(jnp.float32)
    return (section_grad, scores)


def solution(mesh):
    in_specs = (
        P("dom", None, None),
        P("dom", "tilt", None, None),
        P("tilt", None, None),
        P("tilt", None, None),
        P("tilt", None, None),
        P("dom", None, None),
        P("dom", None),
        P("dom", None),
        P("dom", None),
    )
    out_specs = (P("dom", "tilt", None), P("dom"))
    return jax.shard_map(
        on_device, mesh=mesh, in_specs=in_specs, out_specs=out_specs, check_vma=False
    )
```

```python
import jax
import jax.numpy as jnp
from jax import lax
from jax.experimental import pallas as pl
from jax.experimental.pallas import tpu as pltpu
from jax.sharding import PartitionSpec as P

OVL = 16


def middle_kernel(
    owner_ref, local_ref, side_ref, weight_ref, image_ref, proj_ref, low_ref, high_ref,
    ctf_ref, weighted_ref, score_ref, kept_ref, sent_ref, residual_ref, return_ref,
):
    own_count, neighbours = local_ref.shape
    group = owner_ref.shape[2]
    half = kept_ref.shape[0]
    pixels = image_ref.shape[-1]
    peer_count = lax.axis_size("dom")
    steps = peer_count.bit_length() - 1
    me = lax.axis_index("dom")
    ctf = ctf_ref[0]
    ctf_t = ctf.T
    zero = jnp.zeros((OVL, pixels), jnp.float32)

    def place_of(k, j):
        relative = owner_ref[k, j // group, j % group] ^ me
        flipped = sum(((relative >> (steps - 1 - b)) & 1) << b for b in range(steps))
        return flipped * own_count + local_ref[k, j]

    places = [[place_of(k, j) for j in range(neighbours)] for k in range(own_count)]
    edge_rows = []
    for k in range(own_count):
        lower, upper = zero, zero
        for j in range(neighbours):
            q = places[k][j]
            s = side_ref[k, j]
            w = weight_ref[k, j]
            low_band = low_ref[jnp.minimum(q, half - 1), s, 0]
            high_band = high_ref[jnp.maximum(q - half, 0), s, 0]
            band = jnp.where(q < half, low_band, high_band).astype(jnp.float32)
            lower = lower + jnp.where(s == 0, w, 0.0) * band
            upper = upper + jnp.where(s == 1, w, 0.0) * band
        residual_ref[k] = image_ref[k, 0].astype(jnp.float32) - proj_ref[k, 0].astype(jnp.float32)
        residual_ref[k, :OVL] = residual_ref[k, :OVL] - upper
        residual_ref[k, pixels - OVL :] = residual_ref[k, pixels - OVL :] - lower
        residual = residual_ref[k].astype(jnp.bfloat16)
        smoothed = jnp.dot(ctf, residual, preferred_element_type=jnp.float32).astype(jnp.bfloat16)
        filtered = jnp.dot(smoothed, ctf_t, preferred_element_type=jnp.float32)
        score_ref[0, k] = jnp.full(score_ref.shape[2:], jnp.sum(filtered * filtered), jnp.float32)
        reverse = jnp.dot(
            ctf_t, filtered.astype(jnp.bfloat16), preferred_element_type=jnp.float32
        ).astype(jnp.bfloat16)
        weighted = jnp.dot(reverse, ctf, preferred_element_type=jnp.float32).astype(jnp.bfloat16)
        weighted_ref[k, 0] = weighted
        edge_rows.append(
            (weighted[pixels - OVL :].astype(jnp.float32), weighted[:OVL].astype(jnp.float32))
        )

    return_ref[...] = jnp.zeros_like(return_ref)
    for k in range(own_count):
        bottom_rows, top_rows = edge_rows[k]

        for j in range(neighbours):
            q = places[k][j]
            s = side_ref[k, j]
            rows = jnp.where(s == 0, bottom_rows, top_rows)
            part = (weight_ref[k, j] * rows).astype(jnp.bfloat16).astype(jnp.float32)
            return_ref[q, s] = return_ref[q, s] + part
    kept_ref[:, :, 0] = return_ref[:half]
    sent_ref[:, :, 0] = return_ref[half:].astype(jnp.bfloat16)


def middle(owner, local, side, weight, images, projected, edges_low, edges_high, ctf_filter):
    own_count, tilt_count, pixels, _ = images.shape
    half = edges_low.shape[0]
    total = 2 * half
    tiles = pl.BlockSpec((own_count, 1, pixels, pixels), lambda t: (0, t, 0, 0))
    halves = pl.BlockSpec((half, 2, 1, OVL, pixels), lambda t: (0, 0, t, 0, 0))
    smem = pl.BlockSpec(memory_space=pltpu.SMEM)
    flops = own_count * tilt_count * 8 * pixels**3
    moved = 2 * images.size * 3 + 10 * edges_low.size + 2 * ctf_filter.size
    return pl.pallas_call(
        middle_kernel,
        grid=(tilt_count,),
        in_specs=[
            smem,
            smem,
            smem,
            smem,
            tiles,
            tiles,
            halves,
            halves,
            pl.BlockSpec((1, pixels, pixels), lambda t: (t, 0, 0)),
        ],
        out_specs=[
            tiles,
            pl.BlockSpec((1, own_count, 8, 128), lambda t: (t, 0, 0, 0)),
            halves,
            halves,
        ],
        out_shape=[
            jax.ShapeDtypeStruct(images.shape, jnp.bfloat16),
            jax.ShapeDtypeStruct((tilt_count, own_count, 8, 128), jnp.float32),
            jax.ShapeDtypeStruct(edges_low.shape, jnp.float32),
            jax.ShapeDtypeStruct(edges_low.shape, jnp.bfloat16),
        ],
        scratch_shapes=[
            pltpu.VMEM((own_count, pixels, pixels), jnp.float32),
            pltpu.VMEM((total, 2, OVL, pixels), jnp.float32),
        ],
        compiler_params=pltpu.CompilerParams(dimension_semantics=("arbitrary",)),
        cost_estimate=pl.CostEstimate(flops=flops, transcendentals=0, bytes_accessed=moved),
    )(owner, local, side, weight, images, projected, edges_low, edges_high, ctf_filter)


def gather_stages(peer_count):
    steps = peer_count.bit_length() - 1
    strides = [peer_count >> (b + 1) for b in range(steps)]
    if steps <= 2:
        return [(stride,) for stride in strides]
    middle_strides = strides[1:-1]
    pairs = [tuple(middle_strides[i : i + 2]) for i in range(0, len(middle_strides), 2)]
    return [(strides[0],)] + pairs + [(strides[-1],)]


def on_device(
    sections, images, slice_rows, slice_cols, ctf_filter, nbr_owner, nbr_local, nbr_side, nbr_weight
):
    own_count = sections.shape[0]
    pixels = sections.shape[1]
    tilt_count = images.shape[1]
    neighbours = nbr_local.shape[1]
    peer_count = lax.axis_size("dom")
    total = own_count * peer_count
    me = lax.axis_index("dom")
    band_size = tilt_count * OVL * pixels

    halfway = jnp.einsum(
        "kij,tlj->ktil", sections, slice_cols, preferred_element_type=jnp.float32
    ).astype(jnp.bfloat16)
    projected = jnp.einsum(
        "tai,ktil->ktal", slice_rows, halfway, preferred_element_type=jnp.float32
    ).astype(jnp.bfloat16)
    edges = jnp.stack((projected[:, :, :OVL], projected[:, :, pixels - OVL :]), axis=1)
    stages = gather_stages(peer_count)
    edges_all = edges
    for stage in stages[:-1]:
        pieces = [edges_all]
        for g in range(1, 2 ** len(stage)):
            offset = sum(stride for i, stride in enumerate(stage) if (g >> i) & 1)
            pairs = [(i, i ^ offset) for i in range(peer_count)]
            pieces.append(lax.ppermute(edges_all, "dom", pairs))
        edges_all = jnp.concatenate(pieces, axis=0)
    edges_high = lax.ppermute(edges_all, "dom", [(i, i ^ 1) for i in range(peer_count)])

    weighted, score_tiles, kept_half, sent_half = middle(
        nbr_owner, nbr_local, nbr_side, nbr_weight, images, projected, edges_all, edges_high,
        ctf_filter,
    )
    score_part = jnp.sum(score_tiles[:, :, 0, 0], axis=0)
    tilt_groups = lax.axis_size("tilt")
    scale = 0.5 / (tilt_count * tilt_groups * pixels * pixels)
    if tilt_groups == 2:
        score_hi = score_part.astype(jnp.bfloat16)
        score_rest = score_part - score_hi.astype(jnp.float32)
        score_mid = score_rest.astype(jnp.bfloat16)
        score_low = (score_rest - score_mid.astype(jnp.float32)).astype(jnp.bfloat16)
        parts = jnp.stack((score_hi, score_mid, score_low))
        parts = lax.ppermute(parts, "tilt", [(0, 1), (1, 0)]).astype(jnp.float32)
        scores = scale * (score_part + (parts[0] + (parts[1] + parts[2])))

    pairs = [(i, i ^ 1) for i in range(peer_count)]
    returned = kept_half + lax.ppermute(sent_half, "dom", pairs).astype(jnp.float32)
    for stage in [tuple(reversed(stage)) for stage in reversed(stages[:-1])]:
        count = 2 ** len(stage)
        share = returned.shape[0] // count
        kept = returned[:share]
        for g in range(1, count):
            offset = sum(
                stride for i, stride in enumerate(stage) if (g >> (len(stage) - 1 - i)) & 1
            )
            pairs = [(i, i ^ offset) for i in range(peer_count)]
            given = returned[g * share : (g + 1) * share].astype(jnp.bfloat16)
            kept = kept + lax.ppermute(given, "dom", pairs).astype(jnp.float32)
        returned = kept
    add_top = returned[:, 0]
    add_bottom = returned[:, 1]

    proj_grad = weighted.astype(jnp.float32)
    proj_grad = proj_grad.at[:, :, :OVL].add(add_top)
    proj_grad = proj_grad.at[:, :, pixels - OVL :].add(add_bottom)
    proj_half = proj_grad.astype(jnp.bfloat16)
    if tilt_groups != 2:
        upward = jnp.einsum(
            "tai,ktal->ktil", slice_rows, proj_half, preferred_element_type=jnp.float32
        ).astype(jnp.bfloat16)
        partial_grad = -jnp.einsum(
            "ktil,tlj->kij", upward, slice_cols, preferred_element_type=jnp.float32
        )
        scores = scale * lax.psum(score_part, "tilt")
        section_grad = lax.psum_scatter(partial_grad, "tilt", scatter_dimension=1, tiled=True)
        return (section_grad, scores)

    def grad_rows(start):
        rows_weight = lax.dynamic_slice_in_dim(slice_rows, start, pixels // 2, axis=2)
        upward = jnp.einsum(
            "tai,ktal->ktil", rows_weight, proj_half, preferred_element_type=jnp.float32
        ).astype(jnp.bfloat16)
        return -jnp.einsum("ktil,tlj->kij", upward, slice_cols, preferred_element_type=jnp.float32)

    side = lax.axis_index("tilt")
    given = grad_rows((1 - side) * (pixels // 2)).astype(jnp.bfloat16)
    given = lax.ppermute(given, "tilt", [(0, 1), (1, 0)])
    section_grad = grad_rows(side * (pixels // 2)) + given.astype(jnp.float32)
    return (section_grad, scores)

def solution(mesh):
    in_specs = (
        P("dom", None, None),
        P("dom", "tilt", None, None),
        P("tilt", None, None),
        P("tilt", None, None),
        P("tilt", None, None),
        P("dom", None, None),
        P("dom", None),
        P("dom", None),
        P("dom", None),
    )
    out_specs = (P("dom", "tilt", None), P("dom"))
    return jax.shard_map(
        on_device, mesh=mesh, in_specs=in_specs, out_specs=out_specs, check_vma=False
    )
```

```python
import jax
import jax.numpy as jnp
from jax import lax
from jax.experimental import pallas as pl
from jax.experimental.pallas import tpu as pltpu
from jax.sharding import PartitionSpec as P

OVL = 16


def middle_kernel(
    owner_ref, local_ref, side_ref, weight_ref, image_ref, proj_ref, low_ref, high_ref,
    ctf_ref, weighted_ref, score_ref, kept_ref, sent_ref, residual_ref, return_ref,
):
    own_count, neighbours = local_ref.shape
    group = owner_ref.shape[2]
    half = kept_ref.shape[0]
    pixels = image_ref.shape[-1]
    peer_count = lax.axis_size("dom")
    steps = peer_count.bit_length() - 1
    me = lax.axis_index("dom")
    tilt = pl.program_id(0)
    ctf = ctf_ref[0]
    ctf_t = ctf.T
    zero = jnp.zeros((OVL, pixels), jnp.float32)

    def place_of(k, j):
        relative = owner_ref[k, j // group, j % group] ^ me
        flipped = sum(((relative >> (steps - 1 - b)) & 1) << b for b in range(steps))
        return flipped * own_count + local_ref[k, j]

    places = [[place_of(k, j) for j in range(neighbours)] for k in range(own_count)]
    edge_rows = []
    for k in range(own_count):
        lower, upper = zero, zero
        for j in range(neighbours):
            q = places[k][j]
            s = side_ref[k, j]
            w = weight_ref[k, j]
            low_band = low_ref[jnp.minimum(q, half - 1), s, tilt]
            high_band = high_ref[jnp.maximum(q - half, 0), s, tilt]
            band = jnp.where(q < half, low_band, high_band).astype(jnp.float32)
            lower = lower + jnp.where(s == 0, w, 0.0) * band
            upper = upper + jnp.where(s == 1, w, 0.0) * band
        residual_ref[k] = image_ref[k, 0].astype(jnp.float32) - proj_ref[k, 0].astype(jnp.float32)
        residual_ref[k, :OVL] = residual_ref[k, :OVL] - upper
        residual_ref[k, pixels - OVL :] = residual_ref[k, pixels - OVL :] - lower
        residual = residual_ref[k].astype(jnp.bfloat16)
        smoothed = jnp.dot(ctf, residual, preferred_element_type=jnp.float32).astype(jnp.bfloat16)
        filtered = jnp.dot(smoothed, ctf_t, preferred_element_type=jnp.float32)
        score_ref[0, k] = jnp.full(score_ref.shape[2:], jnp.sum(filtered * filtered), jnp.float32)
        reverse = jnp.dot(
            ctf_t, filtered.astype(jnp.bfloat16), preferred_element_type=jnp.float32
        ).astype(jnp.bfloat16)
        weighted = jnp.dot(reverse, ctf, preferred_element_type=jnp.float32).astype(jnp.bfloat16)
        weighted_ref[k, 0] = weighted
        edge_rows.append(
            (weighted[pixels - OVL :].astype(jnp.float32), weighted[:OVL].astype(jnp.float32))
        )

    return_ref[...] = jnp.zeros_like(return_ref)
    for k in range(own_count):
        bottom_rows, top_rows = edge_rows[k]

        for j in range(neighbours):
            q = places[k][j]
            s = side_ref[k, j]
            rows = jnp.where(s == 0, bottom_rows, top_rows)
            part = (weight_ref[k, j] * rows).astype(jnp.bfloat16).astype(jnp.float32)
            return_ref[q, s] = return_ref[q, s] + part
    kept_ref[:, :, 0] = return_ref[:half]
    sent_ref[:, :, 0] = return_ref[half:].astype(jnp.bfloat16)


def middle(owner, local, side, weight, images, projected, edges_low, edges_high, ctf_filter):
    own_count, tilt_count, pixels, _ = images.shape
    half = edges_low.shape[0]
    total = 2 * half
    tiles = pl.BlockSpec((own_count, 1, pixels, pixels), lambda t: (0, t, 0, 0))
    halves = pl.BlockSpec((half, 2, 1, OVL, pixels), lambda t: (0, 0, t, 0, 0))
    smem = pl.BlockSpec(memory_space=pltpu.SMEM)
    whole = pl.BlockSpec(memory_space=pltpu.VMEM)
    flops = own_count * tilt_count * 8 * pixels**3
    moved = 2 * images.size * 3 + 10 * edges_low.size + 2 * ctf_filter.size
    return pl.pallas_call(
        middle_kernel,
        grid=(tilt_count,),
        in_specs=[
            smem,
            smem,
            smem,
            smem,
            tiles,
            tiles,
            whole,
            whole,
            pl.BlockSpec((1, pixels, pixels), lambda t: (t, 0, 0)),
        ],
        out_specs=[
            tiles,
            pl.BlockSpec((1, own_count, 8, 128), lambda t: (t, 0, 0, 0)),
            halves,
            halves,
        ],
        out_shape=[
            jax.ShapeDtypeStruct(images.shape, jnp.bfloat16),
            jax.ShapeDtypeStruct((tilt_count, own_count, 8, 128), jnp.float32),
            jax.ShapeDtypeStruct(edges_low.shape, jnp.float32),
            jax.ShapeDtypeStruct(edges_low.shape, jnp.bfloat16),
        ],
        scratch_shapes=[
            pltpu.VMEM((own_count, pixels, pixels), jnp.float32),
            pltpu.VMEM((total, 2, OVL, pixels), jnp.float32),
        ],
        compiler_params=pltpu.CompilerParams(dimension_semantics=("arbitrary",)),
        cost_estimate=pl.CostEstimate(flops=flops, transcendentals=0, bytes_accessed=moved),
    )(owner, local, side, weight, images, projected, edges_low, edges_high, ctf_filter)


def gather_stages(peer_count):
    steps = peer_count.bit_length() - 1
    strides = [peer_count >> (b + 1) for b in range(steps)]
    if steps <= 2:
        return [(stride,) for stride in strides]
    middle_strides = strides[1:-1]
    pairs = [tuple(middle_strides[i : i + 2]) for i in range(0, len(middle_strides), 2)]
    return [(strides[0],)] + pairs + [(strides[-1],)]


def on_device(
    sections, images, slice_rows, slice_cols, ctf_filter, nbr_owner, nbr_local, nbr_side, nbr_weight
):
    own_count = sections.shape[0]
    pixels = sections.shape[1]
    tilt_count = images.shape[1]
    neighbours = nbr_local.shape[1]
    peer_count = lax.axis_size("dom")
    total = own_count * peer_count
    me = lax.axis_index("dom")
    band_size = tilt_count * OVL * pixels

    halfway = jnp.einsum(
        "kij,tlj->ktil", sections, slice_cols, preferred_element_type=jnp.float32
    ).astype(jnp.bfloat16)
    projected = jnp.einsum(
        "tai,ktil->ktal", slice_rows, halfway, preferred_element_type=jnp.float32
    ).astype(jnp.bfloat16)
    edges = jnp.stack((projected[:, :, :OVL], projected[:, :, pixels - OVL :]), axis=1)
    stages = gather_stages(peer_count)
    edges_all = edges
    for stage in stages[:-1]:
        pieces = [edges_all]
        for g in range(1, 2 ** len(stage)):
            offset = sum(stride for i, stride in enumerate(stage) if (g >> i) & 1)
            pairs = [(i, i ^ offset) for i in range(peer_count)]
            pieces.append(lax.ppermute(edges_all, "dom", pairs))
        edges_all = jnp.concatenate(pieces, axis=0)
    edges_high = lax.ppermute(edges_all, "dom", [(i, i ^ 1) for i in range(peer_count)])

    weighted, score_tiles, kept_half, sent_half = middle(
        nbr_owner, nbr_local, nbr_side, nbr_weight, images, projected, edges_all, edges_high,
        ctf_filter,
    )
    score_part = jnp.sum(score_tiles[:, :, 0, 0], axis=0)
    tilt_groups = lax.axis_size("tilt")
    scale = 0.5 / (tilt_count * tilt_groups * pixels * pixels)
    if tilt_groups == 2:
        score_hi = score_part.astype(jnp.bfloat16)
        score_rest = score_part - score_hi.astype(jnp.float32)
        score_mid = score_rest.astype(jnp.bfloat16)
        score_low = (score_rest - score_mid.astype(jnp.float32)).astype(jnp.bfloat16)
        parts = jnp.stack((score_hi, score_mid, score_low))
        parts = lax.ppermute(parts, "tilt", [(0, 1), (1, 0)]).astype(jnp.float32)
        scores = scale * (score_part + (parts[0] + (parts[1] + parts[2])))

    pairs = [(i, i ^ 1) for i in range(peer_count)]
    returned = kept_half + lax.ppermute(sent_half, "dom", pairs).astype(jnp.float32)
    for stage in [tuple(reversed(stage)) for stage in reversed(stages[:-1])]:
        count = 2 ** len(stage)
        share = returned.shape[0] // count
        kept = returned[:share]
        for g in range(1, count):
            offset = sum(
                stride for i, stride in enumerate(stage) if (g >> (len(stage) - 1 - i)) & 1
            )
            pairs = [(i, i ^ offset) for i in range(peer_count)]
            given = returned[g * share : (g + 1) * share].astype(jnp.bfloat16)
            kept = kept + lax.ppermute(given, "dom", pairs).astype(jnp.float32)
        returned = kept
    add_top = returned[:, 0]
    add_bottom = returned[:, 1]

    proj_grad = weighted.astype(jnp.float32)
    proj_grad = proj_grad.at[:, :, :OVL].add(add_top)
    proj_grad = proj_grad.at[:, :, pixels - OVL :].add(add_bottom)
    proj_half = proj_grad.astype(jnp.bfloat16)
    upward = jnp.einsum(
        "tai,ktal->ktil", slice_rows, proj_half, preferred_element_type=jnp.float32
    ).astype(jnp.bfloat16)
    partial_grad = -jnp.einsum(
        "ktil,tlj->kij", upward, slice_cols, preferred_element_type=jnp.float32
    )
    if tilt_groups != 2:
        scores = scale * lax.psum(score_part, "tilt")
        section_grad = lax.psum_scatter(partial_grad, "tilt", scatter_dimension=1, tiled=True)
        return (section_grad, scores)
    half = pixels // 2
    side = lax.axis_index("tilt")
    kept = lax.dynamic_slice_in_dim(partial_grad, side * half, half, axis=1)
    given = lax.dynamic_slice_in_dim(partial_grad, (1 - side) * half, half, axis=1)
    given = lax.ppermute(given.astype(jnp.bfloat16), "tilt", [(0, 1), (1, 0)])
    section_grad = kept + given.astype(jnp.float32)
    return (section_grad, scores)


def solution(mesh):
    in_specs = (
        P("dom", None, None),
        P("dom", "tilt", None, None),
        P("tilt", None, None),
        P("tilt", None, None),
        P("tilt", None, None),
        P("dom", None, None),
        P("dom", None),
        P("dom", None),
        P("dom", None),
    )
    out_specs = (P("dom", "tilt", None), P("dom"))
    return jax.shard_map(
        on_device, mesh=mesh, in_specs=in_specs, out_specs=out_specs, check_vma=False
    )
```

```python
import jax
import jax.numpy as jnp
from jax import lax
from jax.experimental import pallas as pl
from jax.experimental.pallas import tpu as pltpu
from jax.sharding import PartitionSpec as P

OVL = 16


def middle_kernel(
    owner_ref, local_ref, side_ref, weight_ref, image_ref, proj_ref, low_ref, high_ref,
    ctf_ref, weighted_ref, score_ref, kept_ref, sent_ref, residual_ref, return_ref,
):
    own_count, neighbours = local_ref.shape
    group = owner_ref.shape[2]
    half = kept_ref.shape[0]
    pixels = image_ref.shape[-1]
    peer_count = lax.axis_size("dom")
    steps = peer_count.bit_length() - 1
    me = lax.axis_index("dom")
    ctf = ctf_ref[0]
    ctf_t = ctf.T
    zero = jnp.zeros((OVL, pixels), jnp.float32)

    def place_of(k, j):
        relative = owner_ref[k, j // group, j % group] ^ me
        flipped = sum(((relative >> (steps - 1 - b)) & 1) << b for b in range(steps))
        return flipped * own_count + local_ref[k, j]

    places = [[place_of(k, j) for j in range(neighbours)] for k in range(own_count)]
    edge_rows = []
    for k in range(own_count):
        lower, upper = zero, zero
        for j in range(neighbours):
            q = places[k][j]
            s = side_ref[k, j]
            w = weight_ref[k, j]
            low_band = low_ref[jnp.minimum(q, half - 1), s, 0]
            high_band = high_ref[jnp.maximum(q - half, 0), s, 0]
            band = jnp.where(q < half, low_band, high_band).astype(jnp.float32)
            lower = lower + jnp.where(s == 0, w, 0.0) * band
            upper = upper + jnp.where(s == 1, w, 0.0) * band
        residual_ref[k] = image_ref[k, 0].astype(jnp.float32) - proj_ref[k, 0].astype(jnp.float32)
        residual_ref[k, :OVL] = residual_ref[k, :OVL] - upper
        residual_ref[k, pixels - OVL :] = residual_ref[k, pixels - OVL :] - lower
        residual = residual_ref[k].astype(jnp.bfloat16)
        smoothed = jnp.dot(ctf, residual, preferred_element_type=jnp.float32).astype(jnp.bfloat16)
        filtered = jnp.dot(smoothed, ctf_t, preferred_element_type=jnp.float32)
        score_ref[0, k] = jnp.full(score_ref.shape[2:], jnp.sum(filtered * filtered), jnp.float32)
        reverse = jnp.dot(
            ctf_t, filtered.astype(jnp.bfloat16), preferred_element_type=jnp.float32
        ).astype(jnp.bfloat16)
        weighted = jnp.dot(reverse, ctf, preferred_element_type=jnp.float32).astype(jnp.bfloat16)
        weighted_ref[k, 0] = weighted
        edge_rows.append(
            (weighted[pixels - OVL :].astype(jnp.float32), weighted[:OVL].astype(jnp.float32))
        )

    return_ref[...] = jnp.zeros_like(return_ref)
    for k in range(own_count):
        bottom_rows, top_rows = edge_rows[k]

        for j in range(neighbours):
            q = places[k][j]
            s = side_ref[k, j]
            rows = jnp.where(s == 0, bottom_rows, top_rows)
            part = (weight_ref[k, j] * rows).astype(jnp.bfloat16).astype(jnp.float32)
            return_ref[q, s] = return_ref[q, s] + part
    kept_ref[:, :, 0] = return_ref[:half]
    sent_ref[:, :, 0] = return_ref[half:].astype(jnp.bfloat16)


def middle(owner, local, side, weight, images, projected, edges_low, edges_high, ctf_filter):
    own_count, tilt_count, pixels, _ = images.shape
    half = edges_low.shape[0]
    total = 2 * half
    tiles = pl.BlockSpec((own_count, 1, pixels, pixels), lambda t: (0, t, 0, 0))
    halves = pl.BlockSpec((half, 2, 1, OVL, pixels), lambda t: (0, 0, t, 0, 0))
    smem = pl.BlockSpec(memory_space=pltpu.SMEM)
    flops = own_count * tilt_count * 8 * pixels**3
    moved = 2 * images.size * 3 + 10 * edges_low.size + 2 * ctf_filter.size
    return pl.pallas_call(
        middle_kernel,
        grid=(tilt_count,),
        in_specs=[
            smem,
            smem,
            smem,
            smem,
            tiles,
            tiles,
            halves,
            halves,
            pl.BlockSpec((1, pixels, pixels), lambda t: (t, 0, 0)),
        ],
        out_specs=[
            tiles,
            pl.BlockSpec((1, own_count, 8, 128), lambda t: (t, 0, 0, 0)),
            halves,
            halves,
        ],
        out_shape=[
            jax.ShapeDtypeStruct(images.shape, jnp.bfloat16),
            jax.ShapeDtypeStruct((tilt_count, own_count, 8, 128), jnp.float32),
            jax.ShapeDtypeStruct(edges_low.shape, jnp.float32),
            jax.ShapeDtypeStruct(edges_low.shape, jnp.bfloat16),
        ],
        scratch_shapes=[
            pltpu.VMEM((own_count, pixels, pixels), jnp.float32),
            pltpu.VMEM((total, 2, OVL, pixels), jnp.float32),
        ],
        compiler_params=pltpu.CompilerParams(dimension_semantics=("arbitrary",)),
        cost_estimate=pl.CostEstimate(flops=flops, transcendentals=0, bytes_accessed=moved),
    )(owner, local, side, weight, images, projected, edges_low, edges_high, ctf_filter)


def gather_stages(peer_count):
    steps = peer_count.bit_length() - 1
    strides = [peer_count >> (b + 1) for b in range(steps)]
    if steps <= 2:
        return [(stride,) for stride in strides]
    middle_strides = strides[1:-1]
    pairs = [tuple(middle_strides[i : i + 2]) for i in range(0, len(middle_strides), 2)]
    return [(strides[0],)] + pairs + [(strides[-1],)]


def on_device(
    sections, images, slice_rows, slice_cols, ctf_filter, nbr_owner, nbr_local, nbr_side, nbr_weight
):
    own_count = sections.shape[0]
    pixels = sections.shape[1]
    tilt_count = images.shape[1]
    neighbours = nbr_local.shape[1]
    peer_count = lax.axis_size("dom")
    total = own_count * peer_count
    me = lax.axis_index("dom")
    band_size = tilt_count * OVL * pixels

    halfway = jnp.einsum(
        "kij,tlj->ktil", sections, slice_cols, preferred_element_type=jnp.float32
    ).astype(jnp.bfloat16)
    projected = jnp.einsum(
        "tai,ktil->ktal", slice_rows, halfway, preferred_element_type=jnp.float32
    ).astype(jnp.bfloat16)
    band_weight = jnp.concatenate((slice_rows[:, :OVL], slice_rows[:, pixels - OVL :]), axis=1)
    inner = jnp.einsum(
        "tai,kij->ktaj", band_weight, sections, preferred_element_type=jnp.float32
    ).astype(jnp.bfloat16)
    edge_rows = jnp.einsum(
        "ktaj,tlj->ktal", inner, slice_cols, preferred_element_type=jnp.float32
    ).astype(jnp.bfloat16)
    edges = jnp.stack((edge_rows[:, :, :OVL], edge_rows[:, :, OVL:]), axis=1)
    stages = gather_stages(peer_count)
    edges_all = edges
    for stage in stages[:-1]:
        pieces = [edges_all]
        for g in range(1, 2 ** len(stage)):
            offset = sum(stride for i, stride in enumerate(stage) if (g >> i) & 1)
            pairs = [(i, i ^ offset) for i in range(peer_count)]
            pieces.append(lax.ppermute(edges_all, "dom", pairs))
        edges_all = jnp.concatenate(pieces, axis=0)
    edges_high = lax.ppermute(edges_all, "dom", [(i, i ^ 1) for i in range(peer_count)])

    weighted, score_tiles, kept_half, sent_half = middle(
        nbr_owner, nbr_local, nbr_side, nbr_weight, images, projected, edges_all, edges_high,
        ctf_filter,
    )
    score_part = jnp.sum(score_tiles[:, :, 0, 0], axis=0)
    tilt_groups = lax.axis_size("tilt")
    scale = 0.5 / (tilt_count * tilt_groups * pixels * pixels)
    if tilt_groups == 2:
        score_hi = score_part.astype(jnp.bfloat16)
        score_rest = score_part - score_hi.astype(jnp.float32)
        score_mid = score_rest.astype(jnp.bfloat16)
        score_low = (score_rest - score_mid.astype(jnp.float32)).astype(jnp.bfloat16)
        parts = jnp.stack((score_hi, score_mid, score_low))
        parts = lax.ppermute(parts, "tilt", [(0, 1), (1, 0)]).astype(jnp.float32)
        scores = scale * (score_part + (parts[0] + (parts[1] + parts[2])))

    pairs = [(i, i ^ 1) for i in range(peer_count)]
    returned = kept_half + lax.ppermute(sent_half, "dom", pairs).astype(jnp.float32)
    for stage in [tuple(reversed(stage)) for stage in reversed(stages[:-1])]:
        count = 2 ** len(stage)
        share = returned.shape[0] // count
        kept = returned[:share]
        for g in range(1, count):
            offset = sum(
                stride for i, stride in enumerate(stage) if (g >> (len(stage) - 1 - i)) & 1
            )
            pairs = [(i, i ^ offset) for i in range(peer_count)]
            given = returned[g * share : (g + 1) * share].astype(jnp.bfloat16)
            kept = kept + lax.ppermute(given, "dom", pairs).astype(jnp.float32)
        returned = kept
    add_top = returned[:, 0]
    add_bottom = returned[:, 1]

    proj_grad = weighted.astype(jnp.float32)
    proj_grad = proj_grad.at[:, :, :OVL].add(add_top)
    proj_grad = proj_grad.at[:, :, pixels - OVL :].add(add_bottom)
    proj_half = proj_grad.astype(jnp.bfloat16)
    upward = jnp.einsum(
        "tai,ktal->ktil", slice_rows, proj_half, preferred_element_type=jnp.float32
    ).astype(jnp.bfloat16)
    partial_grad = -jnp.einsum(
        "ktil,tlj->kij", upward, slice_cols, preferred_element_type=jnp.float32
    )
    if tilt_groups != 2:
        scores = scale * lax.psum(score_part, "tilt")
        section_grad = lax.psum_scatter(partial_grad, "tilt", scatter_dimension=1, tiled=True)
        return (section_grad, scores)
    half = pixels // 2
    side = lax.axis_index("tilt")
    kept = lax.dynamic_slice_in_dim(partial_grad, side * half, half, axis=1)
    given = lax.dynamic_slice_in_dim(partial_grad, (1 - side) * half, half, axis=1)
    given = lax.ppermute(given.astype(jnp.bfloat16), "tilt", [(0, 1), (1, 0)])
    section_grad = kept + given.astype(jnp.float32)
    return (section_grad, scores)


def solution(mesh):
    in_specs = (
        P("dom", None, None),
        P("dom", "tilt", None, None),
        P("tilt", None, None),
        P("tilt", None, None),
        P("tilt", None, None),
        P("dom", None, None),
        P("dom", None),
        P("dom", None),
        P("dom", None),
    )
    out_specs = (P("dom", "tilt", None), P("dom"))
    return jax.shard_map(
        on_device, mesh=mesh, in_specs=in_specs, out_specs=out_specs, check_vma=False
    )
```

```python
import jax
import jax.numpy as jnp
from jax import lax
from jax.experimental import pallas as pl
from jax.experimental.pallas import tpu as pltpu
from jax.sharding import PartitionSpec as P

OVL = 16


def middle_kernel(
    owner_ref, local_ref, side_ref, weight_ref, image_ref, proj_ref, low_ref, high_ref,
    ctf_ref, weighted_ref, score_ref, kept_ref, sent_ref, residual_ref, return_ref,
):
    own_count, neighbours = local_ref.shape
    group = owner_ref.shape[2]
    half = kept_ref.shape[0]
    pixels = image_ref.shape[-1]
    peer_count = lax.axis_size("dom")
    steps = peer_count.bit_length() - 1
    me = lax.axis_index("dom")
    zero = jnp.zeros((OVL, pixels), jnp.float32)

    def place_of(k, j):
        relative = owner_ref[k, j // group, j % group] ^ me
        flipped = sum(((relative >> (steps - 1 - b)) & 1) << b for b in range(steps))
        return flipped * own_count + local_ref[k, j]

    places = [[place_of(k, j) for j in range(neighbours)] for k in range(own_count)]
    for t in range(ctf_ref.shape[0]):
        ctf = ctf_ref[t]
        ctf_t = ctf.T
        edge_rows = []
        for k in range(own_count):
            lower, upper = zero, zero
            for j in range(neighbours):
                q = places[k][j]
                s = side_ref[k, j]
                w = weight_ref[k, j]
                low_band = low_ref[jnp.minimum(q, half - 1), s, t]
                high_band = high_ref[jnp.maximum(q - half, 0), s, t]
                band = jnp.where(q < half, low_band, high_band).astype(jnp.float32)
                lower = lower + jnp.where(s == 0, w, 0.0) * band
                upper = upper + jnp.where(s == 1, w, 0.0) * band
            residual_ref[k] = image_ref[k, t].astype(jnp.float32) - proj_ref[k, t].astype(jnp.float32)
            residual_ref[k, :OVL] = residual_ref[k, :OVL] - upper
            residual_ref[k, pixels - OVL :] = residual_ref[k, pixels - OVL :] - lower
            residual = residual_ref[k].astype(jnp.bfloat16)
            smoothed = jnp.dot(ctf, residual, preferred_element_type=jnp.float32).astype(jnp.bfloat16)
            filtered = jnp.dot(smoothed, ctf_t, preferred_element_type=jnp.float32)
            score_ref[t, k] = jnp.full(score_ref.shape[2:], jnp.sum(filtered * filtered), jnp.float32)
            reverse = jnp.dot(
                ctf_t, filtered.astype(jnp.bfloat16), preferred_element_type=jnp.float32
            ).astype(jnp.bfloat16)
            weighted = jnp.dot(reverse, ctf, preferred_element_type=jnp.float32).astype(jnp.bfloat16)
            weighted_ref[k, t] = weighted
            edge_rows.append(
                (weighted[pixels - OVL :].astype(jnp.float32), weighted[:OVL].astype(jnp.float32))
            )

        return_ref[...] = jnp.zeros_like(return_ref)
        for k in range(own_count):
            bottom_rows, top_rows = edge_rows[k]
            for j in range(neighbours):
                q = places[k][j]
                s = side_ref[k, j]
                rows = jnp.where(s == 0, bottom_rows, top_rows)
                part = (weight_ref[k, j] * rows).astype(jnp.bfloat16).astype(jnp.float32)
                return_ref[q, s] = return_ref[q, s] + part
        kept_ref[:, :, t] = return_ref[:half]
        sent_ref[:, :, t] = return_ref[half:].astype(jnp.bfloat16)

def middle(owner, local, side, weight, images, projected, edges_low, edges_high, ctf_filter):
    own_count, tilt_count, pixels, _ = images.shape
    half = edges_low.shape[0]
    total = 2 * half
    tiles = pl.BlockSpec(images.shape, lambda t: (0, 0, 0, 0))
    halves = pl.BlockSpec(edges_low.shape, lambda t: (0, 0, 0, 0, 0))
    smem = pl.BlockSpec(memory_space=pltpu.SMEM)
    flops = own_count * tilt_count * 8 * pixels**3
    moved = 2 * images.size * 3 + 10 * edges_low.size + 2 * ctf_filter.size
    return pl.pallas_call(
        middle_kernel,
        grid=(1,),
        in_specs=[
            smem,
            smem,
            smem,
            smem,
            tiles,
            tiles,
            halves,
            halves,
            pl.BlockSpec(ctf_filter.shape, lambda t: (0, 0, 0)),
        ],
        out_specs=[
            tiles,
            pl.BlockSpec((tilt_count, own_count, 8, 128), lambda t: (0, 0, 0, 0)),
            halves,
            halves,
        ],
        out_shape=[
            jax.ShapeDtypeStruct(images.shape, jnp.bfloat16),
            jax.ShapeDtypeStruct((tilt_count, own_count, 8, 128), jnp.float32),
            jax.ShapeDtypeStruct(edges_low.shape, jnp.float32),
            jax.ShapeDtypeStruct(edges_low.shape, jnp.bfloat16),
        ],
        scratch_shapes=[
            pltpu.VMEM((own_count, pixels, pixels), jnp.float32),
            pltpu.VMEM((total, 2, OVL, pixels), jnp.float32),
        ],
        compiler_params=pltpu.CompilerParams(dimension_semantics=("arbitrary",)),
        cost_estimate=pl.CostEstimate(flops=flops, transcendentals=0, bytes_accessed=moved),
    )(owner, local, side, weight, images, projected, edges_low, edges_high, ctf_filter)


def gather_stages(peer_count):
    steps = peer_count.bit_length() - 1
    strides = [peer_count >> (b + 1) for b in range(steps)]
    if steps <= 2:
        return [(stride,) for stride in strides]
    middle_strides = strides[1:-1]
    pairs = [tuple(middle_strides[i : i + 2]) for i in range(0, len(middle_strides), 2)]
    return [(strides[0],)] + pairs + [(strides[-1],)]


def on_device(
    sections, images, slice_rows, slice_cols, ctf_filter, nbr_owner, nbr_local, nbr_side, nbr_weight
):
    own_count = sections.shape[0]
    pixels = sections.shape[1]
    tilt_count = images.shape[1]
    neighbours = nbr_local.shape[1]
    peer_count = lax.axis_size("dom")
    total = own_count * peer_count
    me = lax.axis_index("dom")
    band_size = tilt_count * OVL * pixels

    halfway = jnp.einsum(
        "kij,tlj->ktil", sections, slice_cols, preferred_element_type=jnp.float32
    ).astype(jnp.bfloat16)
    projected = jnp.einsum(
        "tai,ktil->ktal", slice_rows, halfway, preferred_element_type=jnp.float32
    ).astype(jnp.bfloat16)
    edges = jnp.stack((projected[:, :, :OVL], projected[:, :, pixels - OVL :]), axis=1)
    stages = gather_stages(peer_count)
    edges_all = edges
    for stage in stages[:-1]:
        pieces = [edges_all]
        for g in range(1, 2 ** len(stage)):
            offset = sum(stride for i, stride in enumerate(stage) if (g >> i) & 1)
            pairs = [(i, i ^ offset) for i in range(peer_count)]
            pieces.append(lax.ppermute(edges_all, "dom", pairs))
        edges_all = jnp.concatenate(pieces, axis=0)
    edges_high = lax.ppermute(edges_all, "dom", [(i, i ^ 1) for i in range(peer_count)])

    weighted, score_tiles, kept_half, sent_half = middle(
        nbr_owner, nbr_local, nbr_side, nbr_weight, images, projected, edges_all, edges_high,
        ctf_filter,
    )
    score_part = jnp.sum(score_tiles[:, :, 0, 0], axis=0)
    tilt_groups = lax.axis_size("tilt")
    scale = 0.5 / (tilt_count * tilt_groups * pixels * pixels)
    if tilt_groups == 2:
        score_hi = score_part.astype(jnp.bfloat16)
        score_rest = score_part - score_hi.astype(jnp.float32)
        score_mid = score_rest.astype(jnp.bfloat16)
        score_low = (score_rest - score_mid.astype(jnp.float32)).astype(jnp.bfloat16)
        parts = jnp.stack((score_hi, score_mid, score_low))
        parts = lax.ppermute(parts, "tilt", [(0, 1), (1, 0)]).astype(jnp.float32)
        scores = scale * (score_part + (parts[0] + (parts[1] + parts[2])))

    pairs = [(i, i ^ 1) for i in range(peer_count)]
    returned = kept_half + lax.ppermute(sent_half, "dom", pairs).astype(jnp.float32)
    for stage in [tuple(reversed(stage)) for stage in reversed(stages[:-1])]:
        count = 2 ** len(stage)
        share = returned.shape[0] // count
        kept = returned[:share]
        for g in range(1, count):
            offset = sum(
                stride for i, stride in enumerate(stage) if (g >> (len(stage) - 1 - i)) & 1
            )
            pairs = [(i, i ^ offset) for i in range(peer_count)]
            given = returned[g * share : (g + 1) * share].astype(jnp.bfloat16)
            kept = kept + lax.ppermute(given, "dom", pairs).astype(jnp.float32)
        returned = kept
    add_top = returned[:, 0]
    add_bottom = returned[:, 1]

    proj_grad = weighted.astype(jnp.float32)
    proj_grad = proj_grad.at[:, :, :OVL].add(add_top)
    proj_grad = proj_grad.at[:, :, pixels - OVL :].add(add_bottom)
    proj_half = proj_grad.astype(jnp.bfloat16)
    upward = jnp.einsum(
        "tai,ktal->ktil", slice_rows, proj_half, preferred_element_type=jnp.float32
    ).astype(jnp.bfloat16)
    partial_grad = -jnp.einsum(
        "ktil,tlj->kij", upward, slice_cols, preferred_element_type=jnp.float32
    )
    if tilt_groups != 2:
        scores = scale * lax.psum(score_part, "tilt")
        section_grad = lax.psum_scatter(partial_grad, "tilt", scatter_dimension=1, tiled=True)
        return (section_grad, scores)
    half = pixels // 2
    side = lax.axis_index("tilt")
    kept = lax.dynamic_slice_in_dim(partial_grad, side * half, half, axis=1)
    given = lax.dynamic_slice_in_dim(partial_grad, (1 - side) * half, half, axis=1)
    given = lax.ppermute(given.astype(jnp.bfloat16), "tilt", [(0, 1), (1, 0)])
    section_grad = kept + given.astype(jnp.float32)
    return (section_grad, scores)


def solution(mesh):
    in_specs = (
        P("dom", None, None),
        P("dom", "tilt", None, None),
        P("tilt", None, None),
        P("tilt", None, None),
        P("tilt", None, None),
        P("dom", None, None),
        P("dom", None),
        P("dom", None),
        P("dom", None),
    )
    out_specs = (P("dom", "tilt", None), P("dom"))
    return jax.shard_map(
        on_device, mesh=mesh, in_specs=in_specs, out_specs=out_specs, check_vma=False
    )
```

```python
import jax
import jax.numpy as jnp
from jax import lax
from jax.experimental import pallas as pl
from jax.experimental.pallas import tpu as pltpu
from jax.sharding import PartitionSpec as P

OVL = 16


def middle_kernel(
    owner_ref, local_ref, side_ref, weight_ref, image_ref, proj_ref, low_ref, high_ref,
    ctf_ref, weighted_ref, score_ref, kept_ref, sent_ref, residual_ref, return_ref,
):
    own_count, neighbours = local_ref.shape
    group = owner_ref.shape[2]
    half = kept_ref.shape[0]
    pixels = image_ref.shape[-1]
    peer_count = lax.axis_size("dom")
    steps = peer_count.bit_length() - 1
    me = lax.axis_index("dom")
    zero = jnp.zeros((OVL, pixels), jnp.float32)

    def place_of(k, j):
        relative = owner_ref[k, j // group, j % group] ^ me
        flipped = sum(((relative >> (steps - 1 - b)) & 1) << b for b in range(steps))
        return flipped * own_count + local_ref[k, j]

    places = [[place_of(k, j) for j in range(neighbours)] for k in range(own_count)]
    for t in range(ctf_ref.shape[0]):
        ctf = ctf_ref[t]
        ctf_t = ctf.T
        edge_rows = []
        for k in range(own_count):
            lower, upper = zero, zero
            for j in range(neighbours):
                q = places[k][j]
                s = side_ref[k, j]
                w = weight_ref[k, j]
                low_band = low_ref[jnp.minimum(q, half - 1), s, t]
                high_band = high_ref[jnp.maximum(q - half, 0), s, t]
                band = jnp.where(q < half, low_band, high_band).astype(jnp.float32)
                lower = lower + jnp.where(s == 0, w, 0.0) * band
                upper = upper + jnp.where(s == 1, w, 0.0) * band
            residual_ref[k] = image_ref[k, t].astype(jnp.float32) - proj_ref[k, t].astype(jnp.float32)
            residual_ref[k, :OVL] = residual_ref[k, :OVL] - upper
            residual_ref[k, pixels - OVL :] = residual_ref[k, pixels - OVL :] - lower
            residual = residual_ref[k].astype(jnp.bfloat16)
            smoothed = jnp.dot(ctf, residual, preferred_element_type=jnp.float32).astype(jnp.bfloat16)
            filtered = jnp.dot(smoothed, ctf_t, preferred_element_type=jnp.float32)
            score_ref[t, k] = jnp.full(score_ref.shape[2:], jnp.sum(filtered * filtered), jnp.float32)
            reverse = jnp.dot(
                ctf_t, filtered.astype(jnp.bfloat16), preferred_element_type=jnp.float32
            ).astype(jnp.bfloat16)
            weighted = jnp.dot(reverse, ctf, preferred_element_type=jnp.float32).astype(jnp.bfloat16)
            weighted_ref[k, t] = weighted
            edge_rows.append(
                (weighted[pixels - OVL :].astype(jnp.float32), weighted[:OVL].astype(jnp.float32))
            )

        return_ref[...] = jnp.zeros_like(return_ref)
        for k in range(own_count):
            bottom_rows, top_rows = edge_rows[k]
            for j in range(neighbours):
                q = places[k][j]
                s = side_ref[k, j]
                rows = jnp.where(s == 0, bottom_rows, top_rows)
                part = (weight_ref[k, j] * rows).astype(jnp.bfloat16).astype(jnp.float32)
                return_ref[q, s] = return_ref[q, s] + part
        kept_ref[:, :, t] = return_ref[:half].astype(jnp.bfloat16)
        sent_ref[:, :, t] = return_ref[half:].astype(jnp.bfloat16)

def middle(owner, local, side, weight, images, projected, edges_low, edges_high, ctf_filter):
    own_count, tilt_count, pixels, _ = images.shape
    half = edges_low.shape[0]
    total = 2 * half
    tiles = pl.BlockSpec(images.shape, lambda t: (0, 0, 0, 0))
    halves = pl.BlockSpec(edges_low.shape, lambda t: (0, 0, 0, 0, 0))
    smem = pl.BlockSpec(memory_space=pltpu.SMEM)
    flops = own_count * tilt_count * 8 * pixels**3
    moved = 2 * images.size * 3 + 10 * edges_low.size + 2 * ctf_filter.size
    return pl.pallas_call(
        middle_kernel,
        grid=(1,),
        in_specs=[
            smem,
            smem,
            smem,
            smem,
            tiles,
            tiles,
            halves,
            halves,
            pl.BlockSpec(ctf_filter.shape, lambda t: (0, 0, 0)),
        ],
        out_specs=[
            tiles,
            pl.BlockSpec((tilt_count, own_count, 8, 128), lambda t: (0, 0, 0, 0)),
            halves,
            halves,
        ],
        out_shape=[
            jax.ShapeDtypeStruct(images.shape, jnp.bfloat16),
            jax.ShapeDtypeStruct((tilt_count, own_count, 8, 128), jnp.float32),
            jax.ShapeDtypeStruct(edges_low.shape, jnp.bfloat16),
            jax.ShapeDtypeStruct(edges_low.shape, jnp.bfloat16),
        ],
        scratch_shapes=[
            pltpu.VMEM((own_count, pixels, pixels), jnp.float32),
            pltpu.VMEM((total, 2, OVL, pixels), jnp.float32),
        ],
        compiler_params=pltpu.CompilerParams(dimension_semantics=("arbitrary",)),
        cost_estimate=pl.CostEstimate(flops=flops, transcendentals=0, bytes_accessed=moved),
    )(owner, local, side, weight, images, projected, edges_low, edges_high, ctf_filter)


def gather_stages(peer_count):
    steps = peer_count.bit_length() - 1
    strides = [peer_count >> (b + 1) for b in range(steps)]
    if steps <= 2:
        return [(stride,) for stride in strides]
    middle_strides = strides[1:-1]
    pairs = [tuple(middle_strides[i : i + 2]) for i in range(0, len(middle_strides), 2)]
    return [(strides[0],)] + pairs + [(strides[-1],)]


def on_device(
    sections, images, slice_rows, slice_cols, ctf_filter, nbr_owner, nbr_local, nbr_side, nbr_weight
):
    own_count = sections.shape[0]
    pixels = sections.shape[1]
    tilt_count = images.shape[1]
    neighbours = nbr_local.shape[1]
    peer_count = lax.axis_size("dom")
    total = own_count * peer_count
    me = lax.axis_index("dom")
    band_size = tilt_count * OVL * pixels

    halfway = jnp.einsum(
        "kij,tlj->ktil", sections, slice_cols, preferred_element_type=jnp.float32
    ).astype(jnp.bfloat16)
    projected = jnp.einsum(
        "tai,ktil->ktal", slice_rows, halfway, preferred_element_type=jnp.float32
    ).astype(jnp.bfloat16)
    edges = jnp.stack((projected[:, :, :OVL], projected[:, :, pixels - OVL :]), axis=1)
    stages = gather_stages(peer_count)
    edges_all = edges
    for stage in stages[:-1]:
        pieces = [edges_all]
        for g in range(1, 2 ** len(stage)):
            offset = sum(stride for i, stride in enumerate(stage) if (g >> i) & 1)
            pairs = [(i, i ^ offset) for i in range(peer_count)]
            pieces.append(lax.ppermute(edges_all, "dom", pairs))
        edges_all = jnp.concatenate(pieces, axis=0)
    edges_high = lax.ppermute(edges_all, "dom", [(i, i ^ 1) for i in range(peer_count)])

    weighted, score_tiles, kept_half, sent_half = middle(
        nbr_owner, nbr_local, nbr_side, nbr_weight, images, projected, edges_all, edges_high,
        ctf_filter,
    )
    score_part = jnp.sum(score_tiles[:, :, 0, 0], axis=0)
    tilt_groups = lax.axis_size("tilt")
    scale = 0.5 / (tilt_count * tilt_groups * pixels * pixels)
    if tilt_groups == 2:
        score_hi = score_part.astype(jnp.bfloat16)
        score_rest = score_part - score_hi.astype(jnp.float32)
        score_mid = score_rest.astype(jnp.bfloat16)
        score_low = (score_rest - score_mid.astype(jnp.float32)).astype(jnp.bfloat16)
        parts = jnp.stack((score_hi, score_mid, score_low))
        parts = lax.ppermute(parts, "tilt", [(0, 1), (1, 0)]).astype(jnp.float32)
        scores = scale * (score_part + (parts[0] + (parts[1] + parts[2])))

    pairs = [(i, i ^ 1) for i in range(peer_count)]
    returned = kept_half.astype(jnp.float32) + lax.ppermute(sent_half, "dom", pairs).astype(
        jnp.float32
    )
    for stage in [tuple(reversed(stage)) for stage in reversed(stages[:-1])]:
        count = 2 ** len(stage)
        share = returned.shape[0] // count
        kept = returned[:share]
        for g in range(1, count):
            offset = sum(
                stride for i, stride in enumerate(stage) if (g >> (len(stage) - 1 - i)) & 1
            )
            pairs = [(i, i ^ offset) for i in range(peer_count)]
            given = returned[g * share : (g + 1) * share].astype(jnp.bfloat16)
            kept = kept + lax.ppermute(given, "dom", pairs).astype(jnp.float32)
        returned = kept
    add_top = returned[:, 0]
    add_bottom = returned[:, 1]

    proj_grad = weighted.astype(jnp.float32)
    proj_grad = proj_grad.at[:, :, :OVL].add(add_top)
    proj_grad = proj_grad.at[:, :, pixels - OVL :].add(add_bottom)
    proj_half = proj_grad.astype(jnp.bfloat16)
    upward = jnp.einsum(
        "tai,ktal->ktil", slice_rows, proj_half, preferred_element_type=jnp.float32
    ).astype(jnp.bfloat16)
    partial_grad = -jnp.einsum(
        "ktil,tlj->kij", upward, slice_cols, preferred_element_type=jnp.float32
    )
    if tilt_groups != 2:
        scores = scale * lax.psum(score_part, "tilt")
        section_grad = lax.psum_scatter(partial_grad, "tilt", scatter_dimension=1, tiled=True)
        return (section_grad, scores)
    half = pixels // 2
    side = lax.axis_index("tilt")
    kept = lax.dynamic_slice_in_dim(partial_grad, side * half, half, axis=1)
    given = lax.dynamic_slice_in_dim(partial_grad, (1 - side) * half, half, axis=1)
    given = lax.ppermute(given.astype(jnp.bfloat16), "tilt", [(0, 1), (1, 0)])
    section_grad = kept + given.astype(jnp.float32)
    return (section_grad, scores)


def solution(mesh):
    in_specs = (
        P("dom", None, None),
        P("dom", "tilt", None, None),
        P("tilt", None, None),
        P("tilt", None, None),
        P("tilt", None, None),
        P("dom", None, None),
        P("dom", None),
        P("dom", None),
        P("dom", None),
    )
    out_specs = (P("dom", "tilt", None), P("dom"))
    return jax.shard_map(
        on_device, mesh=mesh, in_specs=in_specs, out_specs=out_specs, check_vma=False
    )
```
